768 devices in a mesh: ew: 16 (over z_hi, y), ns: 48 (over z_lo, x, core).
Axes of the slice: x: 4, y: 8, z: 12 (z_hi: 2, z_lo: 6; z = z_hi * 6 + z_lo), core: 2. Of those that a mesh axis runs over, the one named last changes fastest.
Arguments:
- tokens: bfloat16 [48, 16, 2, 64, 768], P('ns', 'ew'), may hold values from -6 to 6
- vis_index: int32 [48, 16, 2, 64], P('ns', 'ew'), may hold values from 0 to 255, as said below
- counts: int32 [48, 16, 2], P('ns', 'ew'), may hold values from 32 to 64
- owners: int32 [48, 16, 2, 64, 1], P('ns', 'ew'), may hold values from 0 to 47; in each aligned block of 128 rows (0 to 127, 128 to 255, ..., all dimensions but the last counted through in order) at most 4 rows name the same one
- mask_token: bfloat16 [768], replicated, may hold values from -6 to 6
- proj_weight: bfloat16 [768, 64], replicated, may hold values from -0.21875 to 0.21875
- up_first: bfloat16 [4, 4, 64, 64], replicated, may hold values from -0.375 to 0.375
- up_second: bfloat16 [4, 4, 12, 64], replicated, may hold values from -0.375 to 0.375
- saved_pre: bfloat16 [2, 64, 384, 2048], P(None, None, 'ns', 'ew'), may hold values from -6 to 6
- cotangent: bfloat16 [2, 12, 768, 4096], P(None, None, 'ns', 'ew'), may hold values from -6 to 6
Outputs:
- token_grad: bfloat16 [48, 16, 192, 768], P('ns', 'ew')
- grad_proj: float32 [768, 64], replicated
- grad_first: float32 [4, 4, 64, 64], replicated
- grad_second: float32 [4, 4, 12, 64], replicated
- grad_mask: float32 [768], replicated
The draws below stay inside these ranges and needn't reach their ends.
Inputs may be any that keep to these rules, and one draw needn't show every extreme that they name: `vis_index`: each entry is a patch number of its tile, patches numbered row by row with 64 to a row; the 64 entries of one tile and date are distinct; the live ones are the first counts entries. `owners`: among the 128 slots of one tile, live or not, at most 4 name the same owner.
All inputs are finite; a program needn't handle non-finite values.
Results may differ from the reference program's by a relative error of at most 0.0057.
Values may be sent and summed in bfloat16 or wider, within the bound.
A program may use at most 32 MiB of HBM per device.

```python
import math
import jax
import jax.numpy as jnp
import numpy as np
from jax import lax

D = 768
C = 64
BANDS = 12
PH = 4
PW = 64
FRAMES = 2
VIS = 64
CAP = 4
ROWS_IN = 192
TILES_NS = 48
TILES_EW = 16
ROWS_MID = 384
COLS_MID = 2048
ROWS_FINE = 768
COLS_FINE = 4096
N_EW = 16
N_NS = 48


def draw_vis_index(key, part):
    patches = PH * PW
    scores = jax.random.randint(key, (TILES_NS, TILES_EW, FRAMES, patches), 0, 1 << 20)
    scores = scores * patches + jnp.arange(patches, dtype=jnp.int32)
    ordering = jnp.argsort(scores, axis=-1).astype(jnp.int32)
    return ordering[..., :VIS]


def draw_counts(key, part):
    key_values, key_spot = jax.random.split(key)
    values = jax.random.randint(key_values, (TILES_NS, TILES_EW, FRAMES), VIS // 2, VIS + 1)
    chosen_spot = jax.random.randint(key_spot, (), 0, TILES_NS * TILES_EW * FRAMES)
    flattened = values.reshape(-1)
    positions = jnp.arange(flattened.shape[0], dtype=jnp.int32)
    flattened = jnp.where(positions == chosen_spot, VIS, flattened)
    return flattened.reshape(values.shape).astype(jnp.int32)


def block_levels(stream_key, dims, shards, smallest, largest):
    factor_of = 1.0
    for position, parts in shards:
        heights = jax.random.uniform(jax.random.fold_in(jax.random.fold_in(stream_key, 6), position), (parts,), jnp.float32, smallest / len(shards), largest / len(shards))
        factor_of = factor_of * jnp.repeat(jnp.exp(heights), dims[position] // parts).reshape((-1,) + (1,) * (len(dims) - 1 - position))
    return factor_of


def assign_block(stream_key, own, number, rows, amount, top, most, slope):
    ranking = jax.random.permutation(stream_key, amount)
    crowded, common = portions_of(amount, rows * top, most, slope, True), portions_of(amount, rows * top, most, slope, False)
    places = jnp.arange(amount)

    def named(tallies, rotation):
        used = int((tallies > 0).sum())
        fixed = max(1, used // 4)
        moved = fixed + (places - fixed + rotation * (used - fixed)) % max(1, amount - fixed)
        return jnp.zeros((amount,), jnp.int32).at[ranking[jnp.where(places < fixed, places, moved)]].set(jnp.asarray(tallies, jnp.int32))

    tallies = jnp.where(number % 4 == 0, named(crowded, number // 4), named(common, number - number // 4 - 1))
    mixed = jax.random.permutation(jax.random.fold_in(own, 3), amount)
    giver, taker = mixed[0:amount // 2 * 2:2], mixed[1:amount // 2 * 2:2]
    margin = jnp.minimum(tallies[giver] - 1, most - tallies[taker]) // 2
    margin = jnp.where((giver == ranking[0]) | (taker == ranking[0]) | (tallies[taker] == 0), 0, jnp.maximum(margin, 0))
    moved = jax.random.randint(jax.random.fold_in(own, 4), (amount // 2,), 0, 1 << 20) % (margin + 1)
    tallies = tallies.at[giver].add(-moved).at[taker].add(moved)
    items = jnp.searchsorted(jnp.cumsum(tallies), jnp.arange(rows * top), side="right").astype(jnp.int32)
    listing = items.reshape(top, rows).T
    listing = listing[jax.random.permutation(jax.random.fold_in(own, 1), rows)]
    rotation = jax.random.randint(jax.random.fold_in(own, 2), (rows, 1), 0, top)
    return jnp.take_along_axis(listing, (jnp.arange(top)[None, :] + rotation) % top, axis=1)


def portions_of(count, total, limit, slope, full):
    portions = [(1 << 20) // math.isqrt(standing ** slope) + 1 for standing in range(1, count + 1)]
    largest = limit if full else min(limit, max(-(-total // count), total * portions[0] // sum(portions)))
    least = 1 if total - largest >= count - 1 else 0
    holding, spare = [largest] + [least] * (count - 1), total - largest - least * (count - 1)
    while spare > 0:
        candidates = [i for i in range(1, count) if holding[i] < largest] or [i for i in range(1, count) if holding[i] < limit]
        mass, left = sum([portions[i] for i in candidates]), spare
        for i in candidates:
            addition = min(limit - holding[i], max(1, left * portions[i] // mass), spare)
            holding[i] = holding[i] + addition
            spare = spare - addition
    return np.array(holding)


def scatter_about(stream_key, extent, spread, reach, cuts=(), kind=jnp.bfloat16):
    gain = block_levels(stream_key, extent, cuts, -0.22, 0.18) if cuts else 1.0
    entries = jax.random.normal(stream_key, extent, jnp.float32) * spread * gain
    return jnp.minimum(jnp.maximum(entries, -reach), reach).astype(kind)


def setup_inputs(seed: int = 0) -> dict:
    seeds = jax.random.split(jax.random.key(seed), 11)
    tokens = scatter_about(seeds[0], (TILES_NS, TILES_EW, FRAMES, VIS, D), 1.0, 6.0, ((0, 48), (1, 16)))
    vis_index = draw_vis_index(jax.random.fold_in(seeds[10], 71), 0)
    counts = draw_counts(jax.random.fold_in(seeds[10], 71), 0)
    owners_keys = jax.random.split(jax.random.fold_in(seeds[3], 1), TILES_NS * TILES_EW * FRAMES * VIS // (FRAMES * VIS))
    owners_turns = jax.random.permutation(jax.random.fold_in(seeds[3], 3), TILES_NS * TILES_EW * FRAMES * VIS // (FRAMES * VIS))
    owners = jax.vmap(lambda own, number: assign_block(jax.random.fold_in(seeds[3], 2), own, number, FRAMES * VIS, N_NS, 1, CAP, 2))(owners_keys, owners_turns).reshape((TILES_NS, TILES_EW, FRAMES, VIS, 1))
    mask_token = scatter_about(seeds[4], (D,), 1.0, 6.0)
    proj_weight = scatter_about(seeds[5], (D, C), D ** -0.5, 0.21875)
    up_first = scatter_about(seeds[6], (4, 4, C, C), (4 * C) ** -0.5, 0.375)
    up_second = scatter_about(seeds[7], (4, 4, BANDS, C), (4 * C) ** -0.5, 0.375)
    saved_pre = scatter_about(seeds[8], (FRAMES, C, ROWS_MID, COLS_MID), 1.0, 6.0, ((2, 48), (3, 16)))
    cotangent = scatter_about(seeds[9], (FRAMES, BANDS, ROWS_FINE, COLS_FINE), 1.0, 6.0, ((2, 48), (3, 16)))
    return {"tokens": tokens, "vis_index": vis_index, "counts": counts, "owners": owners, "mask_token": mask_token, "proj_weight": proj_weight, "up_first": up_first, "up_second": up_second, "saved_pre": saved_pre, "cotangent": cotangent}


def gelu_value(preact):
    return preact * jax.nn.sigmoid(1.702 * preact)


def gelu_slope(preact):
    sigmoid_value = jax.nn.sigmoid(1.702 * preact)
    return sigmoid_value + 1.702 * preact * sigmoid_value * (1.0 - sigmoid_value)


def transpose_back(inputs, padded, kernel):
    height = inputs.shape[2]
    breadth = inputs.shape[3]
    inputs_wide = inputs.astype(jnp.float32)
    padded_wide = padded.astype(jnp.float32)
    kernel_wide = kernel.astype(jnp.float32)
    grad_inputs = jnp.zeros(inputs.shape, jnp.float32)
    grad_taps = []
    for tap_y in range(4):
        for tap_x in range(4):
            window = padded_wide[:, :, tap_y:tap_y + 2 * height:2, tap_x:tap_x + 2 * breadth:2]
            grad_inputs = grad_inputs + jnp.einsum("oi,fohw->fihw", kernel_wide[tap_y, tap_x], window)
            grad_taps.append(jnp.einsum("fihw,fohw->oi", inputs_wide, window))
    grad_kernel = jnp.stack(grad_taps).reshape((4, 4) + kernel.shape[2:])
    return grad_inputs, grad_kernel


def reference(tokens, vis_index, counts, owners, mask_token, proj_weight, up_first, up_second, saved_pre, cotangent):
    patches = PH * PW
    slot_ids = jnp.arange(VIS, dtype=jnp.int32)
    live = slot_ids[None, None, None, :] < counts[:, :, :, None]
    ns_ids = jnp.broadcast_to(jnp.arange(N_NS, dtype=jnp.int32)[:, None, None], (N_NS, N_EW, VIS))
    ew_ids = jnp.broadcast_to(jnp.arange(N_EW, dtype=jnp.int32)[None, :, None], (N_NS, N_EW, VIS))
    mask_proj = jnp.dot(mask_token[None, :], proj_weight, preferred_element_type=jnp.float32).astype(jnp.bfloat16)[0]

    def frame_step(carry, frame_data):
        grad_proj, grad_first, grad_second, mask_sum = carry
        frame_tokens, frame_index, frame_live, frame_pre, frame_cot = frame_data
        target = jnp.where(frame_live, frame_index, patches).astype(jnp.int32)
        token_proj = jnp.dot(frame_tokens.reshape(-1, D), proj_weight, preferred_element_type=jnp.float32).astype(jnp.bfloat16)
        token_proj = token_proj.reshape(N_NS, N_EW, VIS, C)
        first_tiles = jnp.broadcast_to(mask_proj, (N_NS, N_EW, patches, C))
        first_tiles = first_tiles.at[ns_ids, ew_ids, target].set(token_proj, mode="drop")
        shown = jnp.zeros((N_NS, N_EW, patches), jnp.float32).at[ns_ids, ew_ids, target].set(1.0, mode="drop")
        first_grid = first_tiles.reshape(N_NS, N_EW, PH, PW, C).transpose(4, 0, 2, 1, 3).reshape(1, C, N_NS * PH, N_EW * PW)
        cot_pad = jnp.pad(frame_cot[None], ((0, 0), (0, 0), (1, 1), (1, 1)))
        pre_wide = frame_pre.astype(jnp.float32)[None]
        hidden = gelu_value(pre_wide).astype(jnp.bfloat16)
        grad_hidden, second_term = transpose_back(hidden, cot_pad, up_second)
        deltas = (grad_hidden * gelu_slope(pre_wide)).astype(jnp.bfloat16)
        deltas_pad = jnp.pad(deltas, ((0, 0), (0, 0), (1, 1), (1, 1)))
        grad_grid, first_term = transpose_back(first_grid, deltas_pad, up_first)
        grad_grid = grad_grid.astype(jnp.bfloat16)[0]
        grad_tiles = grad_grid.reshape(C, N_NS, PH, N_EW, PW).transpose(1, 3, 2, 4, 0).reshape(N_NS, N_EW, patches, C)
        safe_index = jnp.clip(frame_index, 0, patches - 1).astype(jnp.int32)
        chosen = grad_tiles[ns_ids, ew_ids, safe_index]
        chosen = jnp.where(frame_live[..., None], chosen, jnp.zeros_like(chosen))
        proj_term = jnp.einsum("tevd,tevc->dc", frame_tokens.astype(jnp.float32), chosen.astype(jnp.float32))
        mask_term = jnp.einsum("tep,tepc->c", 1.0 - shown, grad_tiles.astype(jnp.float32))
        carry = (grad_proj + proj_term, grad_first + first_term, grad_second + second_term, mask_sum + mask_term)
        return carry, chosen

    start = (jnp.zeros((D, C), jnp.float32), jnp.zeros((4, 4, C, C), jnp.float32),
             jnp.zeros((4, 4, BANDS, C), jnp.float32), jnp.zeros((C,), jnp.float32))
    frame_data = (tokens.transpose(2, 0, 1, 3, 4), vis_index.transpose(2, 0, 1, 3), live.transpose(2, 0, 1, 3),
                  saved_pre, cotangent)
    totals, chosen_all = lax.scan(frame_step, start, frame_data)
    grad_proj, grad_first, grad_second, mask_sum = totals
    grad_proj = grad_proj + mask_token.astype(jnp.float32)[:, None] * mask_sum[None, :]
    grad_mask = jnp.dot(proj_weight.astype(jnp.float32), mask_sum, precision=lax.Precision.HIGHEST)

    rows_all = FRAMES * VIS
    chosen_rows = chosen_all.transpose(1, 2, 0, 3, 4).reshape(N_NS, N_EW, rows_all, C)
    owner_rows = owners.reshape(N_NS, N_EW, rows_all).astype(jnp.int32)
    live_rows = live.reshape(N_NS, N_EW, rows_all)
    owner_hits = ((owner_rows[..., None] == jnp.arange(N_NS, dtype=jnp.int32)) & live_rows[..., None]).astype(jnp.int32)
    earlier = jnp.cumsum(owner_hits, axis=2, dtype=jnp.int32) - owner_hits
    place = jnp.sum(earlier * owner_hits, axis=-1, dtype=jnp.int32)
    source_ns = jnp.broadcast_to(jnp.arange(N_NS, dtype=jnp.int32)[:, None, None], (N_NS, N_EW, rows_all))
    source_ew = jnp.broadcast_to(jnp.arange(N_EW, dtype=jnp.int32)[None, :, None], (N_NS, N_EW, rows_all))
    flat_index = (owner_rows * N_EW + source_ew) * ROWS_IN + source_ns * CAP + place
    flat_index = jnp.where(live_rows, flat_index, N_NS * N_EW * ROWS_IN).astype(jnp.int32)
    narrow = jnp.zeros((N_NS * N_EW * ROWS_IN, C), jnp.bfloat16)
    narrow = narrow.at[flat_index.reshape(-1)].set(chosen_rows.reshape(-1, C), mode="drop")

    def widen(block_rows):
        return jnp.dot(block_rows, proj_weight.T, preferred_element_type=jnp.float32).astype(jnp.bfloat16)

    token_grad = lax.map(widen, narrow.reshape(N_NS, N_EW * ROWS_IN, C)).reshape(N_NS, N_EW, ROWS_IN, D)
    return token_grad, grad_proj, grad_first, grad_second, grad_mask
```

```python
import functools

import jax
import jax.numpy as jnp
from jax import lax
from jax.experimental import pallas as pl
from jax.experimental.pallas import tpu as pltpu
from jax.sharding import PartitionSpec as P

MESH = pl.DeviceIdType.MESH
GROUP_A = 8
GROUP_Y = 8
Z_LOW = 6
Z_HIGH = 2


def padded_2(block, sides, width):
    for axis, dim in sides:
        count = lax.axis_size(axis)
        forward = [(i, i + 1) for i in range(count - 1)]
        backward = [(target, source) for source, target in forward]
        low = lax.ppermute(
            lax.slice_in_dim(block, block.shape[dim] - width, None, axis=dim), axis, forward
        )
        high = lax.ppermute(lax.slice_in_dim(block, 0, width, axis=dim), axis, backward)
        block = jnp.concatenate([low, block, high], axis=dim)
    return block


def gelu_value(preact):
    return preact * jax.nn.sigmoid(1.702 * preact)


def gelu_slope(preact):
    sigmoid_value = jax.nn.sigmoid(1.702 * preact)
    return sigmoid_value + 1.702 * preact * sigmoid_value * (1.0 - sigmoid_value)


def transpose_back(inputs, padded, kernel):
    height = inputs.shape[2]
    breadth = inputs.shape[3]
    grad_inputs = None
    grad_taps = []
    for tap_y in range(4):
        for tap_x in range(4):
            window = padded[:, :, tap_y : tap_y + 2 * height : 2, tap_x : tap_x + 2 * breadth : 2]
            partial_term = jnp.einsum(
                "oi,fohw->fihw", kernel[tap_y, tap_x], window, preferred_element_type=jnp.float32
            )
            grad_inputs = partial_term if grad_inputs is None else grad_inputs + partial_term
            grad_taps.append(
                jnp.einsum("fihw,fohw->oi", inputs, window, preferred_element_type=jnp.float32)
            )
    grad_kernel = jnp.stack(grad_taps).reshape((4, 4) + kernel.shape[2:])
    return (grad_inputs, grad_kernel)


def exchange_kernel(
    payload,
    rows_out,
    total_out,
    rows_in,
    buf_a,
    red_a,
    buf_b,
    buf_c,
    buf_d,
    buf_s,
    tok_z,
    tok_s,
    send_a,
    recv_a,
    send_b,
    recv_b,
    send_c,
    recv_c,
    send_d,
    recv_d,
    send_e,
    recv_e,
    send_z,
    recv_z,
    send_t,
    recv_t,
    local_sem,
):
    n = lax.axis_index("ns")
    e = lax.axis_index("ew")
    g = lax.rem(n, GROUP_A)
    zl = lax.div(n, GROUP_A)
    zh = lax.div(e, GROUP_Y)
    y = lax.rem(e, GROUP_Y)
    zi = zh * Z_LOW + zl
    z_count = Z_LOW * Z_HIGH

    def peer_a(k):
        other = lax.rem(g + k, GROUP_A)
        return other, {"ew": e, "ns": zl * GROUP_A + other}

    def peer_b(k):
        other = lax.rem(y + k, GROUP_Y)
        return other, {"ew": zh * GROUP_Y + other, "ns": n}

    def peer_c(k):
        other = lax.rem(zi + k, z_count)
        return other, {
            "ew": lax.div(other, Z_LOW) * GROUP_Y + y,
            "ns": lax.rem(other, Z_LOW) * GROUP_A + g,
        }

    def peer_z(k):
        other = lax.rem(zl + k, Z_LOW)
        return other, {"ew": e, "ns": other * GROUP_A + g}

    barrier = pltpu.get_barrier_semaphore()
    for count, peer in ((GROUP_A, peer_a), (GROUP_Y, peer_b), (z_count, peer_c)):
        for k in range(1, count):
            pl.semaphore_signal(barrier, inc=1, device_id=peer(k)[1], device_id_type=MESH)
    pl.semaphore_wait(barrier, GROUP_A + GROUP_Y + z_count - 3)

    def remote(src, dst, send, recv, target):
        return pltpu.make_async_remote_copy(
            src_ref=src,
            dst_ref=dst,
            send_sem=send,
            recv_sem=recv,
            device_id=target,
            device_id_type=MESH,
        )

    copies_a = []
    for k in range(1, GROUP_A):
        other, target = peer_a(k)
        copies_a.append(
            remote(payload.at[other], buf_a.at[k - 1], send_a.at[k - 1], recv_a.at[k - 1], target)
        )
    for copy in copies_a:
        copy.start()
    copies_z = []
    for k in range(1, Z_LOW):
        other, target = peer_z(k)
        copies_z.append(
            remote(rows_out.at[other], tok_z.at[zl], send_z.at[k - 1], recv_z.at[k - 1], target)
        )
    for copy in copies_z:
        copy.start()
    tok_z[zl] = rows_out[zl]

    for copy in copies_a:
        copy.wait()
    summed = payload[g]
    for k in range(1, GROUP_A):
        summed = summed + buf_a[k - 1]
    red_a[...] = summed

    copies_b = []
    for k in range(1, GROUP_Y):
        other, target = peer_b(k)
        copies_b.append(
            remote(red_a.at[other], buf_b.at[k - 1], send_b.at[k - 1], recv_b.at[k - 1], target)
        )
    for copy in copies_b:
        copy.start()

    for copy in copies_z:
        copy.wait()
    stacked = tok_z[...].reshape(Z_LOW * 16, 128)
    picked = lax.broadcasted_iota(jnp.int32, (GROUP_A * 16, Z_LOW * 16), 0)
    column = lax.broadcasted_iota(jnp.int32, (GROUP_A * 16, Z_LOW * 16), 1)
    wanted = ((picked % 16) // 2) * 16 + (picked // 16) * 2 + picked % 2
    choose = jnp.where(column == wanted, 1.0, 0.0).astype(jnp.bfloat16)
    sorted_rows = jnp.dot(choose, stacked, preferred_element_type=jnp.float32)
    tok_s[...] = sorted_rows.astype(jnp.bfloat16).reshape(GROUP_A, 16, 128)
    copies_t = []
    for k in range(1, GROUP_A):
        other, target = peer_a(k)
        copies_t.append(
            remote(tok_s.at[other], buf_s.at[g], send_t.at[k - 1], recv_t.at[k - 1], target)
        )
    for copy in copies_t:
        copy.start()
    buf_s[g] = tok_s[g]

    for copy in copies_b:
        copy.wait()
    summed = red_a[y]
    for k in range(1, GROUP_Y):
        summed = summed + buf_b[k - 1]
    buf_c[zi] = summed

    copies_c = []
    for k in range(1, z_count):
        _, target = peer_c(k)
        copies_c.append(
            remote(buf_c.at[zi], buf_c.at[zi], send_c.at[k - 1], recv_c.at[k - 1], target)
        )
    for copy in copies_c:
        copy.start()
    for copy in copies_c:
        copy.wait()
    summed = buf_c[0]
    for k in range(1, z_count):
        summed = summed + buf_c[k]
    buf_d[y] = summed

    copies_d = []
    for k in range(1, GROUP_Y):
        _, target = peer_b(k)
        copies_d.append(
            remote(buf_d.at[y], buf_d.at[y], send_d.at[k - 1], recv_d.at[k - 1], target)
        )
    for copy in copies_d:
        copy.start()
    for copy in copies_d:
        copy.wait()

    copies_e = []
    for k in range(1, GROUP_A):
        _, target = peer_a(k)
        copies_e.append(
            remote(buf_d, total_out.at[g], send_e.at[k - 1], recv_e.at[k - 1], target)
        )
    for copy in copies_e:
        copy.start()
    own = pltpu.make_async_copy(buf_d, total_out.at[g], local_sem)
    own.start()
    for copy in copies_t:
        copy.wait()
    rows_in[...] = buf_s[...]
    own.wait()
    for copy in copies_e:
        copy.wait()


def exchange(payload, rows_out):
    dma = pltpu.SemaphoreType.DMA
    z_count = Z_LOW * Z_HIGH
    vmem = pl.BlockSpec(memory_space=pltpu.VMEM)
    return pl.pallas_call(
        exchange_kernel,
        out_shape=(
            jax.ShapeDtypeStruct((GROUP_A, GROUP_Y, 16, 128), jnp.float32),
            jax.ShapeDtypeStruct((GROUP_A, 16, 128), jnp.bfloat16),
        ),
        in_specs=[vmem, vmem],
        out_specs=(pl.BlockSpec(memory_space=pl.ANY), vmem),
        scratch_shapes=[
            pltpu.VMEM((GROUP_A - 1, GROUP_Y, 16, 128), jnp.float32),
            pltpu.VMEM((GROUP_Y, 16, 128), jnp.float32),
            pltpu.VMEM((GROUP_Y - 1, 16, 128), jnp.float32),
            pltpu.VMEM((z_count, 16, 128), jnp.float32),
            pltpu.VMEM((GROUP_Y, 16, 128), jnp.float32),
            pltpu.VMEM((GROUP_A, 16, 128), jnp.bfloat16),
            pltpu.VMEM((Z_LOW, 16, 128), jnp.bfloat16),
            pltpu.VMEM((GROUP_A, 16, 128), jnp.bfloat16),
            dma((GROUP_A - 1,)),
            dma((GROUP_A - 1,)),
            dma((GROUP_Y - 1,)),
            dma((GROUP_Y - 1,)),
            dma((z_count - 1,)),
            dma((z_count - 1,)),
            dma((GROUP_Y - 1,)),
            dma((GROUP_Y - 1,)),
            dma((GROUP_A - 1,)),
            dma((GROUP_A - 1,)),
            dma((Z_LOW - 1,)),
            dma((Z_LOW - 1,)),
            dma((GROUP_A - 1,)),
            dma((GROUP_A - 1,)),
            dma(()),
        ],
        compiler_params=pltpu.CompilerParams(collective_id=0, has_side_effects=True),
        name="exchange",
    )(payload, rows_out)


def per_device(
    tokens,
    vis_index,
    counts,
    owners,
    mask_token,
    proj_weight,
    up_first,
    up_second,
    saved_pre,
    cotangent,
):
    tile_tokens = tokens[0, 0]
    tile_index = vis_index[0, 0]
    tile_counts = counts[0, 0]
    tile_owners = owners[0, 0, :, :, 0]
    frames, slots, features = tile_tokens.shape
    channels = proj_weight.shape[1]
    tok_rows = saved_pre.shape[2] // 2
    tok_cols = saved_pre.shape[3] // 2
    patches = tok_rows * tok_cols
    is_live = jnp.arange(slots, dtype=jnp.int32)[None, :] < tile_counts[:, None]
    picks = (
        tile_index[:, :, None] == jnp.arange(patches, dtype=jnp.int32)[None, None, :]
    ) & is_live[:, :, None]
    picks_half = picks.astype(jnp.bfloat16)
    hidden_mask = 1.0 - jnp.sum(picks.astype(jnp.float32), axis=1)
    token_proj = jnp.einsum(
        "fvd,dc->fvc", tile_tokens, proj_weight, preferred_element_type=jnp.float32
    ).astype(jnp.bfloat16)
    mask_proj = jnp.dot(
        mask_token[None, :], proj_weight, preferred_element_type=jnp.float32
    ).astype(jnp.bfloat16)[0]
    placed = jnp.einsum("fvp,fvc->fcp", picks_half, token_proj, preferred_element_type=jnp.float32)
    placed = placed + hidden_mask[:, None, :] * mask_proj.astype(jnp.float32)[None, :, None]
    first_in = placed.astype(jnp.bfloat16).reshape(frames, channels, tok_rows, tok_cols)
    padded_cot = padded_2(cotangent, (("ew", 3), ("ns", 2)), 1)
    pre_wide = saved_pre.astype(jnp.float32)
    hidden = gelu_value(pre_wide).astype(jnp.bfloat16)
    grad_hidden, grad_second = transpose_back(hidden, padded_cot, up_second)
    deltas = (grad_hidden * gelu_slope(pre_wide)).astype(jnp.bfloat16)
    padded_deltas = padded_2(deltas, (("ew", 3), ("ns", 2)), 1)
    grad_grid, grad_first = transpose_back(first_in, padded_deltas, up_first)
    grad_grid = grad_grid.astype(jnp.bfloat16).reshape(frames, channels, patches)
    chosen = jnp.einsum(
        "fvp,fcp->fvc", picks_half, grad_grid, preferred_element_type=jnp.float32
    ).astype(jnp.bfloat16)
    mask_sum = jnp.einsum(
        "fp,fcp->c", hidden_mask, grad_grid.astype(jnp.float32), precision=lax.Precision.HIGHEST
    )
    grad_proj = jnp.einsum("fvd,fvc->dc", tile_tokens, chosen, preferred_element_type=jnp.float32)
    grad_proj = grad_proj + mask_token.astype(jnp.float32)[:, None] * mask_sum[None, :]
    owner_count = lax.axis_size("ns")
    row_count = frames * slots
    capacity = 3 * row_count // (2 * owner_count)
    owner_rows = tile_owners.reshape(row_count)
    live_rows = is_live.reshape(row_count)
    owner_hits = (
        (owner_rows[:, None] == jnp.arange(owner_count, dtype=jnp.int32)[None, :])
        & live_rows[:, None]
    ).astype(jnp.int32)
    earlier = jnp.cumsum(owner_hits, axis=0, dtype=jnp.int32) - owner_hits
    place = jnp.sum(earlier * owner_hits, axis=1, dtype=jnp.int32)
    target = jnp.where(live_rows, owner_rows * capacity + place, owner_count * capacity)
    slot_hot = (
        target[:, None] == jnp.arange(owner_count * capacity, dtype=jnp.int32)[None, :]
    ).astype(jnp.bfloat16)
    narrow = jnp.einsum(
        "rs,rc->sc", slot_hot, chosen.reshape(row_count, channels),
        preferred_element_type=jnp.float32,
    ).astype(jnp.bfloat16)
    rows_out = narrow.reshape(Z_LOW, 16, 128)

    left = grad_first.reshape(1024, channels)
    right = jnp.concatenate(
        [
            grad_proj,
            grad_second.reshape(192, channels),
            mask_sum[None, :],
            jnp.zeros((63, channels), jnp.float32),
        ],
        axis=0,
    )
    payload = jnp.concatenate([left, right], axis=1).reshape(GROUP_A, GROUP_Y, 16, 128)
    total, rows_in = exchange(payload, rows_out)
    total = total.reshape(1024, 128)
    grad_first = total[:, :channels].reshape(4, 4, channels, channels)
    grad_proj = total[:768, channels:]
    grad_second = total[768:960, channels:].reshape(4, 4, 12, channels)
    mask_sum = total[960, channels:]
    grad_mask = jnp.dot(proj_weight.astype(jnp.float32), mask_sum, precision=lax.Precision.HIGHEST)
    arrived = rows_in[:, : 2 * Z_LOW].reshape(GROUP_A, Z_LOW, 2, 128).transpose(1, 0, 2, 3)
    arrived = arrived.reshape(owner_count * capacity, channels)
    token_grad = jnp.einsum(
        "rc,dc->rd", arrived, proj_weight, preferred_element_type=jnp.float32
    ).astype(jnp.bfloat16)
    return (token_grad[None, None], grad_proj, grad_first, grad_second, grad_mask)


def solution(mesh):
    return jax.shard_map(
        per_device,
        mesh=mesh,
        in_specs=(
            P("ns", "ew", None, None, None),
            P("ns", "ew", None, None),
            P("ns", "ew", None),
            P("ns", "ew", None, None, None),
            P(),
            P(),
            P(),
            P(),
            P(None, None, "ns", "ew"),
            P(None, None, "ns", "ew"),
        ),
        out_specs=(P("ns", "ew", None, None), P(), P(), P(), P()),
        check_vma=False,
    )
```

```python
import jax
import jax.numpy as jnp
import numpy as np
from jax import lax
from jax.experimental import pallas as pl
from jax.experimental.pallas import tpu as pltpu
from jax.sharding import PartitionSpec as P

MESH = pl.DeviceIdType.MESH
GROUP_A = 8
GROUP_Y = 8
Z_LOW = 6
Z_HIGH = 2


BANDS_PAD = 16
LANES = 128


def tap_select():
    wide = np.zeros((256, 4, 256), np.float32)
    halo = np.zeros((16, 4, 256), np.float32)
    for tap in range(4):
        for lane, cell in [(j, j) for j in range(128)] + [(128, 128), (255, -1)]:
            col = 2 * cell + tap - 1
            if col < 0:
                halo[8 + col + 3, tap, lane] = 1
            elif col < 256:
                wide[col, tap, lane] = 1
            else:
                halo[col - 256, tap, lane] = 1
    fine = np.zeros((256, 4, 2, 64), np.float32)
    for tap in range(4):
        for cell in range(64):
            col = 2 * cell + tap - 1
            fine[col if col >= 0 else 255, tap, :, cell] = 1
    edge = np.zeros((2, 8, 128, 128), np.float32)
    for frame in range(2):
        for row in range(8):
            spots = [row + 1] + ([0] if row == 7 else []) + ([9] if row == 0 else [])
            for spot in spots:
                pair = 2 * (frame * 10 + spot)
                edge[frame, row, 0, pair] = 1
                edge[frame, row, 127, (pair - 1) % 128] = 1
    cols = np.zeros((16, 256), np.float32)
    for k in range(3):
        cols[k, k] = 1
        cols[8 + k, 253 + k] = 1
    half = jnp.bfloat16
    return (
        jnp.asarray(wide.reshape(256, 1024), half),
        jnp.asarray(halo.reshape(16, 1024), half),
        jnp.asarray(fine.reshape(256, 512), half),
        jnp.asarray(edge.reshape(2048, 128), half),
        jnp.asarray(cols, half),
    )


def dot_nn(a, b):
    return jnp.dot(a, b, preferred_element_type=jnp.float32)


def dot_nt(a, b):
    return lax.dot_general(a, b, (((1,), (1,)), ((), ())), preferred_element_type=jnp.float32)


def dot_tn(a, b):
    return lax.dot_general(a, b, (((0,), (0,)), ((), ())), preferred_element_type=jnp.float32)


def prepare_kernel(cot, pre, cols, edge, cot_rows, cot_cols, pre_rows, pre_cols, wide_c, wide_p):
    half = jnp.bfloat16
    for f in range(2):
        for o in range(12):
            for part in range(2):
                wide_c[part, pl.ds((f * 16 + o) * 16, 16), :] = cot[
                    f, o, :, part * 128 : part * 128 + 128
                ].astype(jnp.float32)
        for part in range(2):
            wide_c[part, pl.ds((f * 16 + 12) * 16, 64), :] = jnp.zeros((64, 128), jnp.float32)
        for r in range(16):
            for part in range(2):
                cot_rows[f, r, :, part * 128 : part * 128 + 128] = wide_c[
                    part, pl.ds(f * 256 + r, 16, stride=16), :
                ].astype(half)
        for part in range(2):
            block = cot_rows[f, part * 8 : part * 8 + 8].reshape(128, 256)
            cot_cols[f, part] = dot_nt(cols[...], block).astype(half)
    for f in range(2):
        wide_p[pl.ds(f * 512, 512), :] = pre[f].reshape(512, 128).astype(jnp.float32)
    packed = jnp.zeros((64, 128), jnp.float32)
    for f in range(2):
        for i in range(8):
            slab = wide_p[pl.ds(f * 512 + i, 64, stride=8), :].astype(half)
            pre_rows[f, i] = slab
            packed = packed + dot_nn(slab, edge[pl.ds((f * 8 + i) * 128, 128), :])
    pre_cols[...] = packed.astype(half)


def prepare(cot, pre, cols, edge):
    vmem = pl.BlockSpec(memory_space=pltpu.VMEM)
    half = jnp.bfloat16
    return pl.pallas_call(
        prepare_kernel,
        out_shape=(
            jax.ShapeDtypeStruct((2, 16, 16, 256), half),
            jax.ShapeDtypeStruct((2, 2, 16, 128), half),
            jax.ShapeDtypeStruct((2, 8, 64, 128), half),
            jax.ShapeDtypeStruct((64, 128), half),
        ),
        in_specs=[vmem] * 4,
        out_specs=(vmem,) * 4,
        scratch_shapes=[pltpu.VMEM((2, 512, 128), jnp.float32), pltpu.VMEM((1024, 128), jnp.float32)],
        name="prepare",
    )(cot, pre, cols, edge)


SIDES = ((-1, 0), (1, 0), (0, -1), (0, 1), (-1, -1), (-1, 1), (1, -1), (1, 1))


def halo_kernel(cot_rows, cot_cols, pre_rows, pre_cols, rows_c, rows_p, cols_c, cols_p, send, recv):
    n = lax.axis_index("ns")
    e = lax.axis_index("ew")
    n_count = lax.axis_size("ns")
    e_count = lax.axis_size("ew")

    def peer(side):
        return {
            "ew": lax.rem(e + side[1] + e_count, e_count),
            "ns": lax.rem(n + side[0] + n_count, n_count),
        }

    barrier = pltpu.get_barrier_semaphore()
    for side in SIDES:
        pl.semaphore_signal(barrier, inc=1, device_id=peer(side), device_id_type=MESH)
    pl.semaphore_wait(barrier, len(SIDES))
    copies = []

    def put(src, dst, side):
        slot = len(copies)
        copy = pltpu.make_async_remote_copy(
            src_ref=src,
            dst_ref=dst,
            send_sem=send.at[slot],
            recv_sem=recv.at[slot],
            device_id=peer(side),
            device_id_type=MESH,
        )
        copy.start()
        copies.append(copy)

    put(cot_cols, cols_c.at[1], (0, -1))
    put(cot_cols, cols_c.at[0], (0, 1))
    put(pre_cols, cols_p.at[1], (0, -1))
    put(pre_cols, cols_p.at[0], (0, 1))
    put(cot_cols, cols_c.at[5], (-1, -1))
    put(cot_cols, cols_c.at[4], (-1, 1))
    put(cot_cols, cols_c.at[3], (1, -1))
    put(cot_cols, cols_c.at[2], (1, 1))
    put(pre_cols, cols_p.at[5], (-1, -1))
    put(pre_cols, cols_p.at[4], (-1, 1))
    put(pre_cols, cols_p.at[3], (1, -1))
    put(pre_cols, cols_p.at[2], (1, 1))
    put(cot_rows.at[:, 0:3], rows_c.at[1], (-1, 0))
    put(cot_rows.at[:, 13:16], rows_c.at[0], (1, 0))
    put(pre_rows.at[:, 0], rows_p.at[1], (-1, 0))
    put(pre_rows.at[:, 7], rows_p.at[0], (1, 0))
    for copy in copies:
        copy.wait()


def halo(cot_rows, cot_cols, pre_rows, pre_cols):
    vmem = pl.BlockSpec(memory_space=pltpu.VMEM)
    half = jnp.bfloat16
    return pl.pallas_call(
        halo_kernel,
        out_shape=(
            jax.ShapeDtypeStruct((2, 2, 3, 16, 256), half),
            jax.ShapeDtypeStruct((2, 2, 64, 128), half),
            jax.ShapeDtypeStruct((6, 2, 2, 16, 128), half),
            jax.ShapeDtypeStruct((6, 64, 128), half),
        ),
        in_specs=[vmem] * 4,
        out_specs=(vmem,) * 4,
        scratch_shapes=[pltpu.SemaphoreType.DMA((16,)), pltpu.SemaphoreType.DMA((16,))],
        compiler_params=pltpu.CompilerParams(collective_id=1, has_side_effects=True),
        name="halo",
    )(cot_rows, cot_cols, pre_rows, pre_cols)


def gradient_kernel(
    place,
    live_counts,
    index,
    owners,
    tokens,
    mask_token,
    proj,
    first,
    second,
    wide,
    narrow,
    fine,
    cot_rows,
    pre_rows,
    rows_c,
    rows_p,
    cols_c,
    cols_p,
    payload,
    rows_out,
    taps,
    windows,
    hidden,
    deltas,
    taps_fine,
    windows_fine,
):
    half = jnp.bfloat16
    n = place[0]
    e = place[1]
    north = n > 0
    south = n < place[2] - 1
    west = e > 0
    east = e < place[3] - 1

    def flag(condition, shape):
        return jnp.full(shape, jnp.where(condition, 1.0, 0.0), jnp.float32)

    def keep(condition, value):
        return (value.astype(jnp.float32) * flag(condition, value.shape)).astype(half)

    row_16 = lax.broadcasted_iota(jnp.int32, (16, 128), 0)

    def side_cols(west_block, east_block):
        east_part = east_block.astype(jnp.float32) * flag(east, (16, 128))
        west_part = west_block.astype(jnp.float32) * flag(west, (16, 128))
        return jnp.where(row_16 < 8, east_part, west_part).astype(half)

    wide_map = wide[...]
    narrow_map = narrow[...]
    for f in range(2):
        for part in range(2):
            value = dot_nn(cot_rows[f, part * 8 : part * 8 + 8].reshape(128, 256), wide_map)
            cols = side_cols(cols_c[0, f, part], cols_c[1, f, part])
            value = value + dot_tn(cols, narrow_map)
            taps[f, 3 + part * 8 : 11 + part * 8] = value.astype(half).reshape(8, 16, 1024)
        value = dot_nn(rows_c[0, f].reshape(48, 256), wide_map)
        cols = side_cols(cols_c[2, f, 1], cols_c[3, f, 1])
        value = (value + dot_tn(cols, narrow_map)[80:128]) * flag(north, (48, 1024))
        taps[f, 0:3] = value.astype(half).reshape(3, 16, 1024)
        value = dot_nn(rows_c[1, f].reshape(48, 256), wide_map)
        cols = side_cols(cols_c[4, f, 0], cols_c[5, f, 0])
        value = (value + dot_tn(cols, narrow_map)[0:48]) * flag(south, (48, 1024))
        taps[f, 19:22] = value.astype(half).reshape(3, 16, 1024)

    lane = lax.broadcasted_iota(jnp.int32, (64, 128), 1)
    spot = lax.rem(lax.div(lane + 1, 2), 64)
    spot = lax.rem(spot, 10)
    right = lax.rem(lane, 2) == 0
    halo_pre = jnp.where(
        spot == 0,
        jnp.where(right, cols_p[3].astype(jnp.float32), cols_p[2].astype(jnp.float32)),
        jnp.where(
            spot == 9,
            jnp.where(right, cols_p[5].astype(jnp.float32), cols_p[4].astype(jnp.float32)),
            jnp.where(right, cols_p[1].astype(jnp.float32), cols_p[0].astype(jnp.float32)),
        ),
    )
    halo_keep = jnp.where(
        lane == 0, jnp.where(east, 1.0, 0.0), jnp.where(lane == 127, jnp.where(west, 1.0, 0.0), 0.0)
    )
    second_t = second[...]

    for f in range(2):
        for i in range(10):
            column = (f * 10 + i) * 256
            window = jnp.concatenate(
                [
                    taps[f, 2 * i + a, :, b * 256 : b * 256 + 256]
                    for a in range(4)
                    for b in range(4)
                ],
                axis=0,
            )
            grad = dot_nn(second_t, window)
            if i == 0:
                center = rows_p[0, f]
            elif i == 9:
                center = rows_p[1, f]
            else:
                center = pre_rows[f, i - 1]
                windows[:, (f * 8 + i - 1) * 128 : (f * 8 + i) * 128] = window[:, :128]
            center = center.astype(jnp.float32)
            sigmoid = jax.nn.sigmoid(1.702 * center)
            slope = sigmoid + 1.702 * center * sigmoid * (1.0 - sigmoid)
            value = grad[:, :128] * slope
            if 0 < i < 9:
                hidden[:, (f * 8 + i - 1) * 128 : (f * 8 + i) * 128] = (center * sigmoid).astype(half)
            edge_pre = halo_pre
            if f + i > 0:
                edge_pre = pltpu.roll(halo_pre, 128 - 2 * (f * 10 + i), 1)
            sigmoid = jax.nn.sigmoid(1.702 * edge_pre)
            slope = sigmoid + 1.702 * edge_pre * sigmoid * (1.0 - sigmoid)
            edge_value = grad[:, 128:] * slope * halo_keep
            if i == 0:
                value = value * flag(north, value.shape)
                edge_value = edge_value * flag(north, value.shape)
            if i == 9:
                value = value * flag(south, value.shape)
                edge_value = edge_value * flag(south, value.shape)
            deltas[f, i, :, 0:128] = value.astype(half)
            deltas[f, i, :, 128:256] = edge_value.astype(half)

    zeros_64 = jnp.zeros((64, 2048), half)
    hidden_value = hidden[...]
    grad_second = dot_nt(windows[0:128, :], jnp.concatenate([hidden_value, zeros_64], axis=0))
    grad_second = grad_second + dot_nt(
        windows[128:256, :], jnp.concatenate([zeros_64, hidden_value], axis=0)
    )

    fine_map = fine[...]
    for f in range(2):
        for i in range(10):
            taps_fine[f, i] = dot_nn(deltas[f, i], fine_map).astype(half)
    low_lane = lax.broadcasted_iota(jnp.int32, (64, 128), 1) < 64
    for f in range(2):
        for pair in range(2):
            for a in range(4):
                for b in range(4):
                    low = taps_fine[f, 4 * pair + a, :, b * 128 : b * 128 + 128]
                    high = taps_fine[f, 4 * pair + 2 + a, :, b * 128 : b * 128 + 128]
                    windows_fine[
                        (a * 4 + b) * 64 : (a * 4 + b) * 64 + 64,
                        (f * 2 + pair) * 128 : (f * 2 + pair) * 128 + 128,
                    ] = jnp.where(low_lane, low, high)

    token_t = lax.dot_general(
        proj[...], tokens[...], (((0,), (1,)), ((), ())), preferred_element_type=jnp.float32
    ).astype(half)
    mask_row = mask_token[...]
    mask_t = lax.dot_general(
        proj[...],
        jnp.broadcast_to(mask_row, (8, 768)),
        (((0,), (1,)), ((), ())),
        preferred_element_type=jnp.float32,
    ).astype(half)
    mask_column = mask_t[:, 0:1].astype(jnp.float32)
    patch = lax.broadcasted_iota(jnp.int32, (256, 64), 0)
    slot = lax.broadcasted_iota(jnp.int32, (256, 64), 1)
    picks = []
    unseen = []
    first_in = []
    for f in range(2):
        hit = (patch == index[f : f + 1, :]) & (slot < live_counts[f])
        pick = jnp.where(hit, 1.0, 0.0).astype(half)
        picks.append(pick)
        shown = dot_nt(jnp.ones((8, 64), half), pick)
        unseen.append(1.0 - shown)
        placed = dot_nt(token_t[:, f * 64 : f * 64 + 64], pick)
        placed = placed + mask_column * unseen[f][0:1, :]
        first_in.append(placed.astype(half))
    first_grid = jnp.concatenate(first_in, axis=1)
    unseen = jnp.concatenate(unseen, axis=1)

    window = windows_fine[...]
    grid = dot_nn(first[...], window).astype(half)
    zeros_fine = jnp.zeros((64, 512), half)
    grad_first = dot_nt(window[0:512], jnp.concatenate([first_grid, zeros_fine], axis=0))
    grad_first = grad_first + dot_nt(
        window[512:1024], jnp.concatenate([zeros_fine, first_grid], axis=0)
    )
    grid_wide = grid.astype(jnp.float32)
    mask_sum = jnp.sum(grid_wide * unseen[0:1, :], axis=1, keepdims=True)
    mask_sum_row = dot_nt(unseen.astype(half), jnp.concatenate([grid, zeros_fine], axis=0))
    chosen = jnp.concatenate(
        [dot_nn(grid[:, f * 256 : f * 256 + 256], picks[f]) for f in range(2)], axis=1
    ).astype(half)
    grad_proj = dot_nn(chosen, tokens[...]) + mask_sum * mask_row.astype(jnp.float32)

    row_second = lax.broadcasted_iota(jnp.int32, (128, 128), 0)
    lane_second = lax.broadcasted_iota(jnp.int32, (128, 128), 1)
    grad_second = jnp.where(
        (row_second == 12) & (lane_second < 64), mask_sum_row[0:1, :], grad_second
    )
    payload[0:4] = grad_first.reshape(4, 8, 16, 128)
    payload[4:5] = grad_second.reshape(1, 8, 16, 128)
    for part in range(6):
        payload[5 + part // 2, (part % 2) * 4 : (part % 2) * 4 + 4] = grad_proj[
            :, part * 128 : part * 128 + 128
        ].reshape(4, 16, 128)

    owner_row = owners[...]
    lane_row = lax.broadcasted_iota(jnp.int32, (1, 128), 1)
    live_row = lane_row < jnp.where(lane_row < 64, live_counts[0], live_counts[1] + 64)
    marked = jnp.where(live_row, owner_row, -1).astype(jnp.float32)
    across = jnp.broadcast_to(marked, (128, 128))
    down = across.T
    earlier = (across == down) & (row_second < lane_second)
    rank = jnp.sum(jnp.where(earlier, 1.0, 0.0), axis=0, keepdims=True)
    target = jnp.where(live_row, marked * 4.0 + rank, -1.0)
    number = lax.broadcasted_iota(jnp.int32, (96, 128), 0).astype(jnp.float32) * 2.0
    zeros_slot = jnp.zeros((64, 128), half)
    even = jnp.where(number == target, 1.0, 0.0).astype(half)
    odd = jnp.where(number + 1.0 == target, 1.0, 0.0).astype(half)
    packed = dot_nt(even, jnp.concatenate([chosen, zeros_slot], axis=0))
    packed = packed + dot_nt(odd, jnp.concatenate([zeros_slot, chosen], axis=0))
    rows_out[...] = packed.astype(half).reshape(6, 16, 128)


def gradient(scalars, counts, index, owners, arrays):
    vmem = pl.BlockSpec(memory_space=pltpu.VMEM)
    smem = pl.BlockSpec(memory_space=pltpu.SMEM)
    half = jnp.bfloat16
    return pl.pallas_call(
        gradient_kernel,
        out_shape=(
            jax.ShapeDtypeStruct((8, 8, 16, 128), jnp.float32),
            jax.ShapeDtypeStruct((6, 16, 128), half),
        ),
        in_specs=[smem, smem] + [vmem] * (2 + len(arrays)),
        out_specs=(vmem, vmem),
        scratch_shapes=[
            pltpu.VMEM((2, 22, 16, 1024), half),
            pltpu.VMEM((256, 2048), half),
            pltpu.VMEM((64, 2048), half),
            pltpu.VMEM((2, 10, 64, 256), half),
            pltpu.VMEM((2, 10, 64, 512), half),
            pltpu.VMEM((1024, 512), half),
        ],
        name="gradient",
    )(scalars, counts, index, owners, *arrays)


def finish_kernel(
    total, rows_in, proj, token_grad, grad_proj, grad_first, grad_second, grad_mask
):
    half = jnp.bfloat16
    row = lax.broadcasted_iota(jnp.int32, (192, 128), 0)
    column = lax.broadcasted_iota(jnp.int32, (192, 128), 1)
    tile = lax.div(row, 4)
    source = lax.rem(tile, 8) * 16 + lax.div(tile, 8) * 2 + lax.div(lax.rem(row, 4), 2)
    choose = jnp.where(column == source, 1.0, 0.0).astype(half)
    arrived = dot_nn(choose, rows_in[...].reshape(128, 128))
    arrived = jnp.where(lax.div(column, 64) == lax.rem(row, 2), arrived, 0.0).astype(half)
    proj_t = proj[...].astype(jnp.float32).T
    double = jnp.concatenate([proj_t, proj_t], axis=0).astype(half)
    token_grad[...] = dot_nn(arrived, double).astype(half)
    packed = total[0:4].reshape(512, 128)
    grad_first[0:512] = packed[:, 0:64]
    grad_first[512:1024] = packed[:, 64:128]
    for k in range(16):
        lanes = 64 * (k // 8)
        grad_second[k // 4, k % 4] = total[4, k % 8, 0:12, lanes : lanes + 64]
    for part in range(6):
        block = total[5 + part // 2, (part % 2) * 4 : (part % 2) * 4 + 4].reshape(64, 128)
        grad_proj[part * 128 : part * 128 + 128, :] = block.T
    mask_row = total[4, 0, 12:13, 0:64]
    grad_mask[...] = lax.dot_general(
        jnp.broadcast_to(mask_row, (8, 64)),
        proj[...].astype(jnp.float32),
        (((1,), (1,)), ((), ())),
        precision=lax.Precision.HIGHEST,
        preferred_element_type=jnp.float32,
    )[0:1]


def finish(total, rows_in, proj):
    vmem = pl.BlockSpec(memory_space=pltpu.VMEM)
    return pl.pallas_call(
        finish_kernel,
        out_shape=(
            jax.ShapeDtypeStruct((192, 768), jnp.bfloat16),
            jax.ShapeDtypeStruct((768, 64), jnp.float32),
            jax.ShapeDtypeStruct((1024, 64), jnp.float32),
            jax.ShapeDtypeStruct((4, 4, 12, 64), jnp.float32),
            jax.ShapeDtypeStruct((1, 768), jnp.float32),
        ),
        in_specs=[vmem] * 3,
        out_specs=(vmem,) * 5,
        name="finish",
    )(total, rows_in, proj)


def exchange_kernel(
    payload,
    rows_out,
    total_out,
    rows_in,
    buf_a,
    red_a,
    buf_b,
    buf_c,
    buf_d,
    buf_s,
    tok_z,
    tok_s,
    send_a,
    recv_a,
    send_b,
    recv_b,
    send_c,
    recv_c,
    send_d,
    recv_d,
    send_e,
    recv_e,
    send_z,
    recv_z,
    send_t,
    recv_t,
    local_sem,
):
    n = lax.axis_index("ns")
    e = lax.axis_index("ew")
    g = lax.rem(n, GROUP_A)
    zl = lax.div(n, GROUP_A)
    zh = lax.div(e, GROUP_Y)
    y = lax.rem(e, GROUP_Y)
    zi = zh * Z_LOW + zl
    z_count = Z_LOW * Z_HIGH

    def peer_a(k):
        other = lax.rem(g + k, GROUP_A)
        return other, {"ew": e, "ns": zl * GROUP_A + other}

    def peer_b(k):
        other = lax.rem(y + k, GROUP_Y)
        return other, {"ew": zh * GROUP_Y + other, "ns": n}

    def peer_c(k):
        other = lax.rem(zi + k, z_count)
        return other, {
            "ew": lax.div(other, Z_LOW) * GROUP_Y + y,
            "ns": lax.rem(other, Z_LOW) * GROUP_A + g,
        }

    def peer_z(k):
        other = lax.rem(zl + k, Z_LOW)
        return other, {"ew": e, "ns": other * GROUP_A + g}

    barrier = pltpu.get_barrier_semaphore()
    for count, peer in ((GROUP_A, peer_a), (GROUP_Y, peer_b), (z_count, peer_c)):
        for k in range(1, count):
            pl.semaphore_signal(barrier, inc=1, device_id=peer(k)[1], device_id_type=MESH)
    pl.semaphore_wait(barrier, GROUP_A + GROUP_Y + z_count - 3)

    def remote(src, dst, send, recv, target):
        return pltpu.make_async_remote_copy(
            src_ref=src,
            dst_ref=dst,
            send_sem=send,
            recv_sem=recv,
            device_id=target,
            device_id_type=MESH,
        )

    copies_a = []
    for k in range(1, GROUP_A):
        other, target = peer_a(k)
        copies_a.append(
            remote(payload.at[other], buf_a.at[k - 1], send_a.at[k - 1], recv_a.at[k - 1], target)
        )
    for copy in copies_a:
        copy.start()
    copies_z = []
    for k in range(1, Z_LOW):
        other, target = peer_z(k)
        copies_z.append(
            remote(rows_out.at[other], tok_z.at[zl], send_z.at[k - 1], recv_z.at[k - 1], target)
        )
    for copy in copies_z:
        copy.start()
    tok_z[zl] = rows_out[zl]

    for copy in copies_a:
        copy.wait()
    summed = payload[g]
    for k in range(1, GROUP_A):
        summed = summed + buf_a[k - 1]
    red_a[...] = summed

    copies_b = []
    for k in range(1, GROUP_Y):
        other, target = peer_b(k)
        copies_b.append(
            remote(red_a.at[other], buf_b.at[k - 1], send_b.at[k - 1], recv_b.at[k - 1], target)
        )
    for copy in copies_b:
        copy.start()

    for copy in copies_z:
        copy.wait()
    stacked = tok_z[...].reshape(Z_LOW * 16, 128)
    picked = lax.broadcasted_iota(jnp.int32, (GROUP_A * 16, Z_LOW * 16), 0)
    column = lax.broadcasted_iota(jnp.int32, (GROUP_A * 16, Z_LOW * 16), 1)
    wanted = ((picked % 16) // 2) * 16 + (picked // 16) * 2 + picked % 2
    choose = jnp.where(column == wanted, 1.0, 0.0).astype(jnp.bfloat16)
    sorted_rows = jnp.dot(choose, stacked, preferred_element_type=jnp.float32)
    tok_s[...] = sorted_rows.astype(jnp.bfloat16).reshape(GROUP_A, 16, 128)
    copies_t = []
    for k in range(1, GROUP_A):
        other, target = peer_a(k)
        copies_t.append(
            remote(tok_s.at[other], buf_s.at[g], send_t.at[k - 1], recv_t.at[k - 1], target)
        )
    for copy in copies_t:
        copy.start()
    buf_s[g] = tok_s[g]

    for copy in copies_b:
        copy.wait()
    summed = red_a[y]
    for k in range(1, GROUP_Y):
        summed = summed + buf_b[k - 1]
    buf_c[zi] = summed

    copies_c = []
    for k in range(1, z_count):
        _, target = peer_c(k)
        copies_c.append(
            remote(buf_c.at[zi], buf_c.at[zi], send_c.at[k - 1], recv_c.at[k - 1], target)
        )
    for copy in copies_c:
        copy.start()
    for copy in copies_c:
        copy.wait()
    summed = buf_c[0]
    for k in range(1, z_count):
        summed = summed + buf_c[k]
    buf_d[y] = summed

    copies_d = []
    for k in range(1, GROUP_Y):
        _, target = peer_b(k)
        copies_d.append(
            remote(buf_d.at[y], buf_d.at[y], send_d.at[k - 1], recv_d.at[k - 1], target)
        )
    for copy in copies_d:
        copy.start()
    for copy in copies_d:
        copy.wait()

    copies_e = []
    for k in range(1, GROUP_A):
        _, target = peer_a(k)
        copies_e.append(
            remote(buf_d, total_out.at[g], send_e.at[k - 1], recv_e.at[k - 1], target)
        )
    for copy in copies_e:
        copy.start()
    own = pltpu.make_async_copy(buf_d, total_out.at[g], local_sem)
    own.start()
    for copy in copies_t:
        copy.wait()
    rows_in[...] = buf_s[...]
    own.wait()
    for copy in copies_e:
        copy.wait()


def exchange(payload, rows_out):
    dma = pltpu.SemaphoreType.DMA
    z_count = Z_LOW * Z_HIGH
    vmem = pl.BlockSpec(memory_space=pltpu.VMEM)
    return pl.pallas_call(
        exchange_kernel,
        out_shape=(
            jax.ShapeDtypeStruct((GROUP_A, GROUP_Y, 16, 128), jnp.float32),
            jax.ShapeDtypeStruct((GROUP_A, 16, 128), jnp.bfloat16),
        ),
        in_specs=[vmem, vmem],
        out_specs=(pl.BlockSpec(memory_space=pl.ANY), vmem),
        scratch_shapes=[
            pltpu.VMEM((GROUP_A - 1, GROUP_Y, 16, 128), jnp.float32),
            pltpu.VMEM((GROUP_Y, 16, 128), jnp.float32),
            pltpu.VMEM((GROUP_Y - 1, 16, 128), jnp.float32),
            pltpu.VMEM((z_count, 16, 128), jnp.float32),
            pltpu.VMEM((GROUP_Y, 16, 128), jnp.float32),
            pltpu.VMEM((GROUP_A, 16, 128), jnp.bfloat16),
            pltpu.VMEM((Z_LOW, 16, 128), jnp.bfloat16),
            pltpu.VMEM((GROUP_A, 16, 128), jnp.bfloat16),
            dma((GROUP_A - 1,)),
            dma((GROUP_A - 1,)),
            dma((GROUP_Y - 1,)),
            dma((GROUP_Y - 1,)),
            dma((z_count - 1,)),
            dma((z_count - 1,)),
            dma((GROUP_Y - 1,)),
            dma((GROUP_Y - 1,)),
            dma((GROUP_A - 1,)),
            dma((GROUP_A - 1,)),
            dma((Z_LOW - 1,)),
            dma((Z_LOW - 1,)),
            dma((GROUP_A - 1,)),
            dma((GROUP_A - 1,)),
            dma(()),
        ],
        compiler_params=pltpu.CompilerParams(collective_id=0, has_side_effects=True),
        name="exchange",
    )(payload, rows_out)


def local_gradients(
    tokens, vis_index, counts, owners, mask_token, proj_weight, up_first, up_second, saved_pre, cotangent
):
    half = jnp.bfloat16
    wide, narrow, fine, edge, cols = tap_select()
    cot_rows, cot_cols, pre_rows, pre_cols = prepare(cotangent, saved_pre, cols, edge)
    rows_c, rows_p, cols_c, cols_p = halo(cot_rows, cot_cols, pre_rows, pre_cols)
    scalars = jnp.stack(
        [
            lax.axis_index("ns"),
            lax.axis_index("ew"),
            jnp.int32(lax.axis_size("ns")),
            jnp.int32(lax.axis_size("ew")),
        ]
    ).astype(jnp.int32)
    first_t = up_first.reshape(1024, 64).T
    second_t = jnp.pad(up_second, ((0, 0), (0, 0), (0, 4), (0, 0))).reshape(256, 64).T
    return gradient(
        scalars,
        counts.reshape(2),
        vis_index.reshape(2, 64),
        owners.reshape(1, 128),
        [
            tokens.reshape(128, 768),
            mask_token.reshape(1, 768),
            proj_weight,
            first_t,
            second_t,
            wide,
            narrow,
            fine,
            cot_rows,
            pre_rows,
            rows_c,
            rows_p,
            cols_c,
            cols_p,
        ],
    )


def per_device(
    tokens,
    vis_index,
    counts,
    owners,
    mask_token,
    proj_weight,
    up_first,
    up_second,
    saved_pre,
    cotangent,
):
    payload, rows_out = local_gradients(
        tokens, vis_index, counts, owners, mask_token, proj_weight, up_first, up_second, saved_pre, cotangent
    )
    total, rows_in = exchange(payload, rows_out)
    token_grad, grad_proj, grad_first, grad_second, grad_mask = finish(total, rows_in, proj_weight)
    return (
        token_grad[None, None],
        grad_proj,
        grad_first.reshape(4, 4, 64, 64),
        grad_second,
        grad_mask.reshape(768),
    )


def solution(mesh):
    return jax.shard_map(
        per_device,
        mesh=mesh,
        in_specs=(
            P("ns", "ew", None, None, None),
            P("ns", "ew", None, None),
            P("ns", "ew", None),
            P("ns", "ew", None, None, None),
            P(),
            P(),
            P(),
            P(),
            P(None, None, "ns", "ew"),
            P(None, None, "ns", "ew"),
        ),
        out_specs=(P("ns", "ew", None, None), P(), P(), P(), P()),
        check_vma=False,
    )
```

```python
import jax
import jax.numpy as jnp
import numpy as np
from jax import lax
from jax.experimental import pallas as pl
from jax.experimental.pallas import tpu as pltpu
from jax.sharding import PartitionSpec as P

MESH = pl.DeviceIdType.MESH
GROUP_A = 8
GROUP_Y = 8
Z_LOW = 6
Z_HIGH = 2


BANDS_PAD = 16
LANES = 128


def tap_select():
    wide = np.zeros((256, 4, 256), np.float32)
    halo = np.zeros((16, 4, 256), np.float32)
    for tap in range(4):
        for lane, cell in [(j, j) for j in range(128)] + [(128, 128), (255, -1)]:
            col = 2 * cell + tap - 1
            if col < 0:
                halo[8 + col + 3, tap, lane] = 1
            elif col < 256:
                wide[col, tap, lane] = 1
            else:
                halo[col - 256, tap, lane] = 1
    fine = np.zeros((256, 4, 2, 64), np.float32)
    for tap in range(4):
        for cell in range(64):
            col = 2 * cell + tap - 1
            fine[col if col >= 0 else 255, tap, :, cell] = 1
    edge = np.zeros((2, 8, 128, 128), np.float32)
    for frame in range(2):
        for row in range(8):
            spots = [row + 1] + ([0] if row == 7 else []) + ([9] if row == 0 else [])
            for spot in spots:
                pair = 2 * (frame * 10 + spot)
                edge[frame, row, 0, pair] = 1
                edge[frame, row, 127, (pair - 1) % 128] = 1
    cols = np.zeros((16, 256), np.float32)
    for k in range(3):
        cols[k, k] = 1
        cols[8 + k, 253 + k] = 1
    order = np.zeros((4, 12, 4, 4, 4, 16), np.float32)
    for a in range(4):
        for o in range(12):
            for b in range(4):
                order[a, o, b, a, b, o] = 1
    half = jnp.bfloat16
    return (
        jnp.asarray(wide.reshape(256, 1024), half),
        jnp.asarray(halo.reshape(16, 1024), half),
        jnp.asarray(fine.reshape(256, 512), half),
        jnp.asarray(edge.reshape(2048, 128), half),
        jnp.asarray(cols, half),
        jnp.asarray(order.reshape(192, 256), half),
    )


def dot_nn(a, b):
    return jnp.dot(a, b, preferred_element_type=jnp.float32)


def dot_nt(a, b):
    return lax.dot_general(a, b, (((1,), (1,)), ((), ())), preferred_element_type=jnp.float32)


def dot_tn(a, b):
    return lax.dot_general(a, b, (((0,), (0,)), ((), ())), preferred_element_type=jnp.float32)


SIDES = ((-1, 0), (1, 0), (0, -1), (0, 1), (-1, -1), (-1, 1), (1, -1), (1, 1))
STREAMS = 2
Z_COUNT = Z_LOW * Z_HIGH


def main_kernel(
    live_counts,
    index,
    owners,
    tokens,
    mask_token,
    proj_t,
    first,
    second,
    cot,
    pre,
    wide,
    narrow,
    fine,
    edge,
    cols,
    order,
    total_out,
    rows_in,
    wide_c,
    wide_p,
    cot_rows,
    cot_cols,
    pre_rows,
    pre_cols,
    rows_c,
    rows_p,
    cols_c,
    cols_p,
    taps,
    windows,
    hidden,
    deltas,
    taps_fine,
    windows_fine,
    payload,
    buf_a,
    red_a,
    buf_b,
    buf_c,
    buf_d,
    rows_out,
    tok_z,
    tok_s,
    buf_s,
    send,
    recv,
    local_sem,
):
    half = jnp.bfloat16
    n = lax.axis_index("ns")
    e = lax.axis_index("ew")
    n_count = lax.axis_size("ns")
    e_count = lax.axis_size("ew")
    g = lax.rem(n, GROUP_A)
    zl = lax.div(n, GROUP_A)
    zh = lax.div(e, GROUP_Y)
    y = lax.rem(e, GROUP_Y)
    zi = zh * Z_LOW + zl

    def peer_side(side):
        return {
            "ew": lax.rem(e + side[1] + e_count, e_count),
            "ns": lax.rem(n + side[0] + n_count, n_count),
        }

    def peer_a(k):
        other = lax.rem(g + k, GROUP_A)
        return other, {"ew": e, "ns": zl * GROUP_A + other}

    def peer_b(k):
        other = lax.rem(y + k, GROUP_Y)
        return other, {"ew": zh * GROUP_Y + other, "ns": n}

    def peer_c(k):
        other = lax.rem(zi + k, Z_COUNT)
        return other, {
            "ew": lax.div(other, Z_LOW) * GROUP_Y + y,
            "ns": lax.rem(other, Z_LOW) * GROUP_A + g,
        }

    def peer_z(k):
        other = lax.rem(zl + k, Z_LOW)
        return other, {"ew": e, "ns": other * GROUP_A + g}

    barrier = pltpu.get_barrier_semaphore()
    for side in SIDES:
        pl.semaphore_signal(barrier, inc=1, device_id=peer_side(side), device_id_type=MESH)
    for count, peer in ((GROUP_A, peer_a), (GROUP_Y, peer_b), (Z_COUNT, peer_c)):
        for k in range(1, count):
            pl.semaphore_signal(barrier, inc=1, device_id=peer(k)[1], device_id_type=MESH)

    used = [0]

    def put(src, dst, target):
        slot = used[0]
        used[0] += 1
        copy = pltpu.make_async_remote_copy(
            src_ref=src,
            dst_ref=dst,
            send_sem=send.at[slot],
            recv_sem=recv.at[slot],
            device_id=target,
            device_id_type=MESH,
        )
        copy.start()
        return copy

    def wait_all(copies):
        for copy in copies:
            copy.wait()

    for f in range(2):
        for o in range(12):
            for part in range(2):
                wide_c[part, pl.ds((f * 16 + o) * 16, 16), :] = cot[
                    f, o, :, part * 128 : part * 128 + 128
                ].astype(jnp.float32)
        for part in range(2):
            wide_c[part, pl.ds((f * 16 + 12) * 16, 64), :] = jnp.zeros((64, 128), jnp.float32)
        for r in range(16):
            for part in range(2):
                cot_rows[f, r, :, part * 128 : part * 128 + 128] = wide_c[
                    part, pl.ds(f * 256 + r, 16, stride=16), :
                ].astype(half)
        for part in range(2):
            block = cot_rows[f, part * 8 : part * 8 + 8].reshape(128, 256)
            cot_cols[f, part] = dot_nt(cols[...], block).astype(half)
    for f in range(2):
        wide_p[pl.ds(f * 512, 512), :] = pre[f].reshape(512, 128).astype(jnp.float32)
    packed = jnp.zeros((64, 128), jnp.float32)
    for f in range(2):
        for i in range(8):
            slab = wide_p[pl.ds(f * 512 + i, 64, stride=8), :].astype(half)
            pre_rows[f, i] = slab
            packed = packed + dot_nn(slab, edge[pl.ds((f * 8 + i) * 128, 128), :])
    pre_cols[...] = packed.astype(half)

    pl.semaphore_wait(barrier, len(SIDES) + GROUP_A + GROUP_Y + Z_COUNT - 3)

    halo = []
    halo.append(put(cot_cols, cols_c.at[1], peer_side((0, -1))))
    halo.append(put(cot_cols, cols_c.at[0], peer_side((0, 1))))
    halo.append(put(pre_cols, cols_p.at[1], peer_side((0, -1))))
    halo.append(put(pre_cols, cols_p.at[0], peer_side((0, 1))))
    halo.append(put(cot_cols, cols_c.at[5], peer_side((-1, -1))))
    halo.append(put(cot_cols, cols_c.at[4], peer_side((-1, 1))))
    halo.append(put(cot_cols, cols_c.at[3], peer_side((1, -1))))
    halo.append(put(cot_cols, cols_c.at[2], peer_side((1, 1))))
    halo.append(put(pre_cols, cols_p.at[5], peer_side((-1, -1))))
    halo.append(put(pre_cols, cols_p.at[4], peer_side((-1, 1))))
    halo.append(put(pre_cols, cols_p.at[3], peer_side((1, -1))))
    halo.append(put(pre_cols, cols_p.at[2], peer_side((1, 1))))
    halo.append(put(cot_rows.at[:, 0:3], rows_c.at[1], peer_side((-1, 0))))
    halo.append(put(cot_rows.at[:, 13:16], rows_c.at[0], peer_side((1, 0))))
    halo.append(put(pre_rows.at[:, 0], rows_p.at[1], peer_side((-1, 0))))
    halo.append(put(pre_rows.at[:, 7], rows_p.at[0], peer_side((1, 0))))

    token_t = dot_nt(proj_t[...], tokens[...]).astype(half)
    mask_row = mask_token[...].astype(jnp.float32).reshape(1, 768)
    mask_t = dot_nt(proj_t[...], jnp.broadcast_to(mask_row, (8, 768)).astype(half)).astype(half)
    mask_column = mask_t[:, 0:1].astype(jnp.float32)
    patch = lax.broadcasted_iota(jnp.int32, (256, 64), 0)
    slot = lax.broadcasted_iota(jnp.int32, (256, 64), 1)
    picks = []
    unseen = []
    first_in = []
    for f in range(2):
        hit = (patch == index[f : f + 1, :]) & (slot < live_counts[f])
        pick = jnp.where(hit, 1.0, 0.0).astype(half)
        picks.append(pick)
        shown = dot_nt(jnp.ones((8, 64), half), pick)
        unseen.append(1.0 - shown)
        placed = dot_nt(token_t[:, f * 64 : f * 64 + 64], pick)
        placed = placed + mask_column * unseen[f][0:1, :]
        first_in.append(placed.astype(half))
    first_grid = jnp.concatenate(first_in, axis=1)
    unseen = jnp.concatenate(unseen, axis=1)
    second_t = dot_tn(
        second[...].astype(jnp.float32).reshape(192, 64).astype(half), order[...]
    ).astype(half)

    row_second = lax.broadcasted_iota(jnp.int32, (128, 128), 0)
    lane_second = lax.broadcasted_iota(jnp.int32, (128, 128), 1)
    owner_row = jnp.concatenate([owners[0], owners[1]], axis=1)
    lane_row = lax.broadcasted_iota(jnp.int32, (1, 128), 1)
    live_row = lane_row < jnp.where(lane_row < 64, live_counts[0], live_counts[1] + 64)
    marked = jnp.where(live_row, owner_row, -1).astype(jnp.float32)
    across = jnp.broadcast_to(marked, (128, 128))
    down = across.T
    earlier = (across == down) & (row_second < lane_second)
    rank = jnp.sum(jnp.where(earlier, 1.0, 0.0), axis=0, keepdims=True)
    target = jnp.where(live_row, marked * 4.0 + rank, -1.0)
    number = lax.broadcasted_iota(jnp.int32, (96, 128), 0).astype(jnp.float32) * 2.0
    even = jnp.where(number == target, 1.0, 0.0).astype(half)
    odd = jnp.where(number + 1.0 == target, 1.0, 0.0).astype(half)

    wait_all(halo)

    north = n > 0
    south = n < n_count - 1
    west = e > 0
    east = e < e_count - 1

    def flag(condition, shape):
        return jnp.full(shape, jnp.where(condition, 1.0, 0.0), jnp.float32)

    row_16 = lax.broadcasted_iota(jnp.int32, (16, 128), 0)

    def side_cols(west_block, east_block):
        east_part = east_block.astype(jnp.float32) * flag(east, (16, 128))
        west_part = west_block.astype(jnp.float32) * flag(west, (16, 128))
        return jnp.where(row_16 < 8, east_part, west_part).astype(half)

    wide_map = wide[...]
    narrow_map = narrow[...]
    for f in range(2):
        for part in range(2):
            value = dot_nn(cot_rows[f, part * 8 : part * 8 + 8].reshape(128, 256), wide_map)
            side = side_cols(cols_c[0, f, part], cols_c[1, f, part])
            value = value + dot_tn(side, narrow_map)
            taps[f, 3 + part * 8 : 11 + part * 8] = value.astype(half).reshape(8, 16, 1024)
        value = dot_nn(rows_c[0, f].reshape(48, 256), wide_map)
        side = side_cols(cols_c[2, f, 1], cols_c[3, f, 1])
        value = (value + dot_tn(side, narrow_map)[80:128]) * flag(north, (48, 1024))
        taps[f, 0:3] = value.astype(half).reshape(3, 16, 1024)
        value = dot_nn(rows_c[1, f].reshape(48, 256), wide_map)
        side = side_cols(cols_c[4, f, 0], cols_c[5, f, 0])
        value = (value + dot_tn(side, narrow_map)[0:48]) * flag(south, (48, 1024))
        taps[f, 19:22] = value.astype(half).reshape(3, 16, 1024)

    lane = lax.broadcasted_iota(jnp.int32, (64, 128), 1)
    spot = lax.rem(lax.rem(lax.div(lane + 1, 2), 64), 10)
    right = lax.rem(lane, 2) == 0
    halo_pre = jnp.where(
        spot == 0,
        jnp.where(right, cols_p[3].astype(jnp.float32), cols_p[2].astype(jnp.float32)),
        jnp.where(
            spot == 9,
            jnp.where(right, cols_p[5].astype(jnp.float32), cols_p[4].astype(jnp.float32)),
            jnp.where(right, cols_p[1].astype(jnp.float32), cols_p[0].astype(jnp.float32)),
        ),
    )
    halo_keep = jnp.where(
        lane == 0, jnp.where(east, 1.0, 0.0), jnp.where(lane == 127, jnp.where(west, 1.0, 0.0), 0.0)
    )
    sigmoid = jax.nn.sigmoid(1.702 * halo_pre)
    halo_slope = sigmoid + 1.702 * halo_pre * sigmoid * (1.0 - sigmoid)

    for f in range(2):
        for i in range(10):
            window = jnp.concatenate(
                [
                    taps[f, 2 * i + a, :, b * 256 : b * 256 + 256]
                    for a in range(4)
                    for b in range(4)
                ],
                axis=0,
            )
            grad = dot_nn(second_t, window)
            if i == 0:
                center = rows_p[0, f]
            elif i == 9:
                center = rows_p[1, f]
            else:
                center = pre_rows[f, i - 1]
                windows[:, (f * 8 + i - 1) * 128 : (f * 8 + i) * 128] = window[:, :128]
            center = center.astype(jnp.float32)
            sigmoid = jax.nn.sigmoid(1.702 * center)
            slope = sigmoid + 1.702 * center * sigmoid * (1.0 - sigmoid)
            value = grad[:, :128] * slope
            if 0 < i < 9:
                hidden[:, (f * 8 + i - 1) * 128 : (f * 8 + i) * 128] = (center * sigmoid).astype(half)
            edge_slope = halo_slope
            if f + i > 0:
                edge_slope = pltpu.roll(halo_slope, 128 - 2 * (f * 10 + i), 1)
            edge_value = grad[:, 128:] * edge_slope * halo_keep
            if i == 0:
                value = value * flag(north, value.shape)
                edge_value = edge_value * flag(north, value.shape)
            if i == 9:
                value = value * flag(south, value.shape)
                edge_value = edge_value * flag(south, value.shape)
            deltas[f, i, :, 0:128] = value.astype(half)
            deltas[f, i, :, 128:256] = edge_value.astype(half)

    fine_map = fine[...]
    for f in range(2):
        for i in range(10):
            taps_fine[f, i] = dot_nn(deltas[f, i], fine_map).astype(half)
    low_lane = lane < 64
    for f in range(2):
        for pair in range(2):
            for a in range(4):
                for b in range(4):
                    low = taps_fine[f, 4 * pair + a, :, b * 128 : b * 128 + 128]
                    high = taps_fine[f, 4 * pair + 2 + a, :, b * 128 : b * 128 + 128]
                    windows_fine[
                        (a * 4 + b) * 64 : (a * 4 + b) * 64 + 64,
                        (f * 2 + pair) * 128 : (f * 2 + pair) * 128 + 128,
                    ] = jnp.where(low_lane, low, high)

    zeros_fine = jnp.zeros((64, 512), half)
    grad_first = dot_nt(windows_fine[0:512], jnp.concatenate([first_grid, zeros_fine], axis=0))
    grad_first = grad_first + dot_nt(
        windows_fine[512:1024], jnp.concatenate([zeros_fine, first_grid], axis=0)
    )
    payload[0] = grad_first.reshape(GROUP_A, GROUP_Y, 8, 128)

    def scatter_a(s):
        copies = []
        for k in range(1, GROUP_A):
            other, target_device = peer_a(k)
            copies.append(put(payload.at[s, other], buf_a.at[s, k - 1], target_device))
        return copies

    copies_a = [scatter_a(0)]

    grid = dot_tn(first[...], windows_fine[...]).astype(half)
    chosen = jnp.concatenate(
        [dot_nn(grid[:, f * 256 : f * 256 + 256], picks[f]) for f in range(2)], axis=1
    ).astype(half)
    zeros_slot = jnp.zeros((64, 128), half)
    outgoing = dot_nt(even, jnp.concatenate([chosen, zeros_slot], axis=0))
    outgoing = outgoing + dot_nt(odd, jnp.concatenate([zeros_slot, chosen], axis=0))
    rows_out[...] = outgoing.astype(half).reshape(Z_LOW, 16, 128)
    copies_z = []
    for k in range(1, Z_LOW):
        other, target_device = peer_z(k)
        copies_z.append(put(rows_out.at[other], tok_z.at[zl], target_device))
    tok_z[zl] = rows_out[zl]

    zeros_64 = jnp.zeros((64, 2048), half)
    hidden_value = hidden[...]
    grad_second = dot_nt(windows[0:128, :], jnp.concatenate([hidden_value, zeros_64], axis=0))
    grad_second = grad_second + dot_nt(
        windows[128:256, :], jnp.concatenate([zeros_64, hidden_value], axis=0)
    )
    mask_sum = jnp.sum(grid.astype(jnp.float32) * unseen[0:1, :], axis=1, keepdims=True)
    mask_sum_row = dot_nt(unseen.astype(half), jnp.concatenate([grid, zeros_fine], axis=0))
    grad_proj = dot_nn(chosen, tokens[...]) + mask_sum * mask_row
    grad_second = jnp.where(
        (row_second == 12) & (lane_second < 64), mask_sum_row[0:1, :], grad_second
    )
    payload[1, 0:2] = grad_second.reshape(2, GROUP_Y, 8, 128)
    for part in range(6):
        payload[1, 2 + part] = grad_proj[:, part * 128 : part * 128 + 128].reshape(GROUP_Y, 8, 128)
    copies_a.append(scatter_a(1))

    copies_b = []
    for s in range(STREAMS):
        wait_all(copies_a[s])
        summed = payload[s, g]
        for k in range(1, GROUP_A):
            summed = summed + buf_a[s, k - 1]
        red_a[s] = summed
        copies = []
        for k in range(1, GROUP_Y):
            other, target_device = peer_b(k)
            copies.append(put(red_a.at[s, other], buf_b.at[s, k - 1], target_device))
        copies_b.append(copies)

    wait_all(copies_z)
    stacked = tok_z[...].reshape(Z_LOW * 16, 128)
    picked = lax.broadcasted_iota(jnp.int32, (GROUP_A * 16, Z_LOW * 16), 0)
    column = lax.broadcasted_iota(jnp.int32, (GROUP_A * 16, Z_LOW * 16), 1)
    wanted = ((picked % 16) // 2) * 16 + (picked // 16) * 2 + picked % 2
    choose = jnp.where(column == wanted, 1.0, 0.0).astype(half)
    tok_s[...] = dot_nn(choose, stacked).astype(half).reshape(GROUP_A, 16, 128)
    copies_t = []
    for k in range(1, GROUP_A):
        other, target_device = peer_a(k)
        copies_t.append(put(tok_s.at[other], buf_s.at[g], target_device))
    buf_s[g] = tok_s[g]

    copies_c = []
    for s in range(STREAMS):
        wait_all(copies_b[s])
        summed = red_a[s, y]
        for k in range(1, GROUP_Y):
            summed = summed + buf_b[s, k - 1]
        buf_c[s, zi] = summed
        copies = []
        for k in range(1, Z_COUNT):
            copies.append(put(buf_c.at[s, zi], buf_c.at[s, zi], peer_c(k)[1]))
        copies_c.append(copies)

    row_8 = lax.broadcasted_iota(jnp.int32, (8, 128), 0)
    copies_d = []
    for s in range(STREAMS):
        wait_all(copies_c[s])
        summed = buf_c[s, 0]
        for k in range(1, Z_COUNT):
            summed = summed + buf_c[s, k]
        if s == 1:
            rounded = summed.astype(half).astype(jnp.float32)
            rest = jnp.broadcast_to((summed - rounded)[4:5], (8, 128))
            here = jnp.where((g == 0) & (y == 1), 5, -1)
            summed = jnp.where(row_8 == here, rest, summed)
        buf_d[s, y] = summed.astype(half)
        copies = []
        for k in range(1, GROUP_Y):
            copies.append(put(buf_d.at[s, y], buf_d.at[s, y], peer_b(k)[1]))
        copies_d.append(copies)

    copies_e = []
    own = []
    for s in range(STREAMS):
        wait_all(copies_d[s])
        for k in range(1, GROUP_A):
            copies_e.append(put(buf_d.at[s], total_out.at[s, g], peer_a(k)[1]))
        copy = pltpu.make_async_copy(buf_d.at[s], total_out.at[s, g], local_sem.at[s])
        copy.start()
        own.append(copy)
    wait_all(copies_t)
    rows_in[...] = buf_s[...]
    wait_all(own)
    wait_all(copies_e)


COPIES = 16 + 2 * (2 * (GROUP_A - 1) + 2 * (GROUP_Y - 1) + Z_COUNT - 1) + Z_LOW - 1 + GROUP_A - 1


def main(counts, index, owners, arrays):
    vmem = pl.BlockSpec(memory_space=pltpu.VMEM)
    smem = pl.BlockSpec(memory_space=pltpu.SMEM)
    half = jnp.bfloat16
    wide = jnp.float32
    dma = pltpu.SemaphoreType.DMA
    return pl.pallas_call(
        main_kernel,
        out_shape=(
            jax.ShapeDtypeStruct((STREAMS, GROUP_A, GROUP_Y, 8, 128), half),
            jax.ShapeDtypeStruct((GROUP_A, 16, 128), half),
        ),
        in_specs=[smem] + [vmem] * (2 + len(arrays)),
        out_specs=(pl.BlockSpec(memory_space=pl.ANY), vmem),
        scratch_shapes=[
            pltpu.VMEM((2, 512, 128), wide),
            pltpu.VMEM((1024, 128), wide),
            pltpu.VMEM((2, 16, 16, 256), half),
            pltpu.VMEM((2, 2, 16, 128), half),
            pltpu.VMEM((2, 8, 64, 128), half),
            pltpu.VMEM((64, 128), half),
            pltpu.VMEM((2, 2, 3, 16, 256), half),
            pltpu.VMEM((2, 2, 64, 128), half),
            pltpu.VMEM((6, 2, 2, 16, 128), half),
            pltpu.VMEM((6, 64, 128), half),
            pltpu.VMEM((2, 22, 16, 1024), half),
            pltpu.VMEM((256, 2048), half),
            pltpu.VMEM((64, 2048), half),
            pltpu.VMEM((2, 10, 64, 256), half),
            pltpu.VMEM((2, 10, 64, 512), half),
            pltpu.VMEM((1024, 512), half),
            pltpu.VMEM((STREAMS, GROUP_A, GROUP_Y, 8, 128), wide),
            pltpu.VMEM((STREAMS, GROUP_A - 1, GROUP_Y, 8, 128), wide),
            pltpu.VMEM((STREAMS, GROUP_Y, 8, 128), wide),
            pltpu.VMEM((STREAMS, GROUP_Y - 1, 8, 128), wide),
            pltpu.VMEM((STREAMS, Z_COUNT, 8, 128), wide),
            pltpu.VMEM((STREAMS, GROUP_Y, 8, 128), half),
            pltpu.VMEM((Z_LOW, 16, 128), half),
            pltpu.VMEM((Z_LOW, 16, 128), half),
            pltpu.VMEM((GROUP_A, 16, 128), half),
            pltpu.VMEM((GROUP_A, 16, 128), half),
            dma((COPIES,)),
            dma((COPIES,)),
            dma((STREAMS,)),
        ],
        compiler_params=pltpu.CompilerParams(collective_id=0, has_side_effects=True),
        name="main",
    )(counts, index, owners, *arrays)


def finish_kernel(
    total, rows_in, proj_t, token_grad, grad_proj, grad_first, grad_second, grad_mask
):
    half = jnp.bfloat16
    row = lax.broadcasted_iota(jnp.int32, (192, 128), 0)
    column = lax.broadcasted_iota(jnp.int32, (192, 128), 1)
    tile = lax.div(row, 4)
    source = lax.rem(tile, 8) * 16 + lax.div(tile, 8) * 2 + lax.div(lax.rem(row, 4), 2)
    choose = jnp.where(column == source, 1.0, 0.0).astype(half)
    arrived = dot_nn(choose, rows_in[...].reshape(128, 128))
    arrived = jnp.where(lax.div(column, 64) == lax.rem(row, 2), arrived, 0.0).astype(half)
    double = jnp.concatenate([proj_t[...], proj_t[...]], axis=0)
    token_grad[...] = dot_nn(arrived, double).astype(half)
    packed = total[0].astype(jnp.float32).reshape(512, 128)
    grad_first[0:512] = packed[:, 0:64]
    grad_first[512:1024] = packed[:, 64:128]
    other = total[1].astype(jnp.float32).reshape(512, 128)
    for k in range(16):
        lanes = 64 * (k // 8)
        start = (k % 8) * 16
        grad_second[k // 4, :, k % 4, :] = other[start : start + 12, lanes : lanes + 64]
    for part in range(6):
        grad_proj[:, part * 128 : part * 128 + 128] = other[128 + part * 64 : 192 + part * 64]
    mask_row = other[12:13, 0:64] + other[13:14, 0:64]
    grad_mask[...] = jnp.dot(
        jnp.broadcast_to(mask_row, (8, 64)),
        proj_t[...].astype(jnp.float32),
        precision=lax.Precision.HIGHEST,
        preferred_element_type=jnp.float32,
    )[0:1].reshape(768)


def finish(total, rows_in, proj_t):
    vmem = pl.BlockSpec(memory_space=pltpu.VMEM)
    return pl.pallas_call(
        finish_kernel,
        out_shape=(
            jax.ShapeDtypeStruct((192, 768), jnp.bfloat16),
            jax.ShapeDtypeStruct((64, 768), jnp.float32),
            jax.ShapeDtypeStruct((1024, 64), jnp.float32),
            jax.ShapeDtypeStruct((4, 12, 4, 64), jnp.float32),
            jax.ShapeDtypeStruct((768,), jnp.float32),
        ),
        in_specs=[vmem] * 3,
        out_specs=(vmem,) * 5,
        name="finish",
    )(total, rows_in, proj_t)


def per_device(
    tokens,
    vis_index,
    counts,
    owners,
    mask_token,
    proj_weight,
    up_first,
    up_second,
    saved_pre,
    cotangent,
):
    wide, narrow, fine, edge, cols, order = tap_select()
    proj_t = proj_weight.T
    total, rows_in = main(
        counts.reshape(2),
        vis_index.reshape(2, 64),
        owners.reshape(2, 1, 64),
        [
            tokens.reshape(128, 768),
            mask_token,
            proj_t,
            up_first.reshape(1024, 64),
            up_second.transpose(0, 2, 1, 3),
            cotangent,
            saved_pre,
            wide,
            narrow,
            fine,
            edge,
            cols,
            order,
        ],
    )
    token_grad, grad_proj, grad_first, grad_second, grad_mask = finish(total, rows_in, proj_t)
    return (
        token_grad[None, None],
        grad_proj.T,
        grad_first.reshape(4, 4, 64, 64),
        grad_second.transpose(0, 2, 1, 3),
        grad_mask,
    )


def solution(mesh):
    return jax.shard_map(
        per_device,
        mesh=mesh,
        in_specs=(
            P("ns", "ew", None, None, None),
            P("ns", "ew", None, None),
            P("ns", "ew", None),
            P("ns", "ew", None, None, None),
            P(),
            P(),
            P(),
            P(),
            P(None, None, "ns", "ew"),
            P(None, None, "ns", "ew"),
        ),
        out_specs=(P("ns", "ew", None, None), P(), P(), P(), P()),
        check_vma=False,
    )
```

```python
import jax
import jax.numpy as jnp
import numpy as np
from jax import lax
from jax.experimental import pallas as pl
from jax.experimental.pallas import tpu as pltpu
from jax.sharding import PartitionSpec as P

MESH = pl.DeviceIdType.MESH
GROUP_A = 8
GROUP_Y = 8
Z_LOW = 6
Z_HIGH = 2


BANDS_PAD = 16
LANES = 128


def tap_select():
    wide = np.zeros((256, 4, 256), np.float32)
    halo = np.zeros((16, 4, 256), np.float32)
    for tap in range(4):
        for lane, cell in [(j, j) for j in range(128)] + [(128, 128), (255, -1)]:
            col = 2 * cell + tap - 1
            if col < 0:
                halo[8 + col + 3, tap, lane] = 1
            elif col < 256:
                wide[col, tap, lane] = 1
            else:
                halo[col - 256, tap, lane] = 1
    fine = np.zeros((256, 4, 2, 64), np.float32)
    for tap in range(4):
        for cell in range(64):
            col = 2 * cell + tap - 1
            fine[col if col >= 0 else 255, tap, :, cell] = 1
    edge = np.zeros((2, 8, 128, 128), np.float32)
    for frame in range(2):
        for row in range(8):
            spots = [row + 1] + ([0] if row == 7 else []) + ([9] if row == 0 else [])
            for spot in spots:
                pair = 2 * (frame * 10 + spot)
                edge[frame, row, 0, pair] = 1
                edge[frame, row, 127, (pair - 1) % 128] = 1
    cols = np.zeros((16, 256), np.float32)
    for k in range(3):
        cols[k, k] = 1
        cols[8 + k, 253 + k] = 1
    order = np.zeros((4, 12, 4, 4, 4, 16), np.float32)
    for a in range(4):
        for o in range(12):
            for b in range(4):
                order[a, o, b, a, b, o] = 1
    half = jnp.bfloat16
    return (
        jnp.asarray(wide.reshape(256, 1024), half),
        jnp.asarray(halo.reshape(16, 1024), half),
        jnp.asarray(fine.reshape(256, 512), half),
        jnp.asarray(edge.reshape(2048, 128), half),
        jnp.asarray(cols, half),
        jnp.asarray(order.reshape(192, 256), half),
    )


def dot_nn(a, b):
    return jnp.dot(a, b, preferred_element_type=jnp.float32)


def dot_nt(a, b):
    return lax.dot_general(a, b, (((1,), (1,)), ((), ())), preferred_element_type=jnp.float32)


def dot_tn(a, b):
    return lax.dot_general(a, b, (((0,), (0,)), ((), ())), preferred_element_type=jnp.float32)


SIDES = ((-1, 0), (1, 0), (0, -1), (0, 1), (-1, -1), (-1, 1), (1, -1), (1, 1))
STREAMS = 2
Z_COUNT = Z_LOW * Z_HIGH


def fetch_all(pairs, sem):
    copies = []
    for k, (src, dst) in enumerate(pairs):
        copy = pltpu.make_async_copy(src, dst, sem.at[k])
        copy.start()
        copies.append(copy)
    return copies


def wait_all(copies):
    for copy in copies:
        copy.wait()


def halo_kernel(
    cot_in,
    pre_in,
    cols_in,
    edge_in,
    cot_rows,
    pre_rows,
    rows_c,
    rows_p,
    cols_c,
    cols_p,
    cot,
    pre,
    cols,
    edge,
    wide_c,
    wide_p,
    cot_cols,
    pre_cols,
    send,
    recv,
    fetch,
):
    half = jnp.bfloat16
    n = lax.axis_index("ns")
    e = lax.axis_index("ew")
    n_count = lax.axis_size("ns")
    e_count = lax.axis_size("ew")

    def peer_side(side):
        return {
            "ew": lax.rem(e + side[1] + e_count, e_count),
            "ns": lax.rem(n + side[0] + n_count, n_count),
        }

    barrier = pltpu.get_barrier_semaphore()
    for side in SIDES:
        pl.semaphore_signal(barrier, inc=1, device_id=peer_side(side), device_id_type=MESH)
    fetched = fetch_all(((cot_in, cot), (cols_in, cols), (pre_in, pre), (edge_in, edge)), fetch)

    used = [0]

    def put(src, dst, target):
        slot = used[0]
        used[0] += 1
        copy = pltpu.make_async_remote_copy(
            src_ref=src,
            dst_ref=dst,
            send_sem=send.at[slot],
            recv_sem=recv.at[slot],
            device_id=target,
            device_id_type=MESH,
        )
        copy.start()
        return copy

    wait_all(fetched)
    for f in range(2):
        for o in range(12):
            for part in range(2):
                wide_c[part, pl.ds((f * 16 + o) * 16, 16), :] = cot[
                    f, o, :, part * 128 : part * 128 + 128
                ].astype(jnp.float32)
        for part in range(2):
            wide_c[part, pl.ds((f * 16 + 12) * 16, 64), :] = jnp.zeros((64, 128), jnp.float32)
        for r in range(16):
            for part in range(2):
                cot_rows[f, r, :, part * 128 : part * 128 + 128] = wide_c[
                    part, pl.ds(f * 256 + r, 16, stride=16), :
                ].astype(half)
        for part in range(2):
            block = cot_rows[f, part * 8 : part * 8 + 8].reshape(128, 256)
            cot_cols[f, part] = dot_nt(cols[...], block).astype(half)
    for f in range(2):
        wide_p[pl.ds(f * 512, 512), :] = pre[f].reshape(512, 128).astype(jnp.float32)
    packed = jnp.zeros((64, 128), jnp.float32)
    for f in range(2):
        for i in range(8):
            slab = wide_p[pl.ds(f * 512 + i, 64, stride=8), :].astype(half)
            pre_rows[f, i] = slab
            packed = packed + dot_nn(slab, edge[pl.ds((f * 8 + i) * 128, 128), :])
    pre_cols[...] = packed.astype(half)

    pl.semaphore_wait(barrier, len(SIDES))

    halo = []
    halo.append(put(cot_cols, cols_c.at[1], peer_side((0, -1))))
    halo.append(put(cot_cols, cols_c.at[0], peer_side((0, 1))))
    halo.append(put(pre_cols, cols_p.at[1], peer_side((0, -1))))
    halo.append(put(pre_cols, cols_p.at[0], peer_side((0, 1))))
    halo.append(put(cot_cols, cols_c.at[5], peer_side((-1, -1))))
    halo.append(put(cot_cols, cols_c.at[4], peer_side((-1, 1))))
    halo.append(put(cot_cols, cols_c.at[3], peer_side((1, -1))))
    halo.append(put(cot_cols, cols_c.at[2], peer_side((1, 1))))
    halo.append(put(pre_cols, cols_p.at[5], peer_side((-1, -1))))
    halo.append(put(pre_cols, cols_p.at[4], peer_side((-1, 1))))
    halo.append(put(pre_cols, cols_p.at[3], peer_side((1, -1))))
    halo.append(put(pre_cols, cols_p.at[2], peer_side((1, 1))))
    halo.append(put(cot_rows.at[:, 0:3], rows_c.at[1], peer_side((-1, 0))))
    halo.append(put(cot_rows.at[:, 13:16], rows_c.at[0], peer_side((1, 0))))
    halo.append(put(pre_rows.at[:, 0], rows_p.at[1], peer_side((-1, 0))))
    halo.append(put(pre_rows.at[:, 7], rows_p.at[0], peer_side((1, 0))))

    wait_all(halo)


def halo(cotangent, saved_pre, cols, edge):
    vmem = pl.BlockSpec(memory_space=pltpu.VMEM)
    hbm = pl.BlockSpec(memory_space=pl.ANY)
    half = jnp.bfloat16
    wide = jnp.float32
    dma = pltpu.SemaphoreType.DMA
    return pl.pallas_call(
        halo_kernel,
        out_shape=(
            jax.ShapeDtypeStruct((2, 16, 16, 256), half),
            jax.ShapeDtypeStruct((2, 8, 64, 128), half),
            jax.ShapeDtypeStruct((2, 2, 3, 16, 256), half),
            jax.ShapeDtypeStruct((2, 2, 64, 128), half),
            jax.ShapeDtypeStruct((6, 2, 2, 16, 128), half),
            jax.ShapeDtypeStruct((6, 64, 128), half),
        ),
        in_specs=[hbm] * 4,
        out_specs=(vmem,) * 6,
        scratch_shapes=[pltpu.VMEM(x.shape, x.dtype) for x in (cotangent, saved_pre, cols, edge)]
        + [
            pltpu.VMEM((2, 512, 128), wide),
            pltpu.VMEM((1024, 128), wide),
            pltpu.VMEM((2, 2, 16, 128), half),
            pltpu.VMEM((64, 128), half),
            dma((16,)),
            dma((16,)),
            dma((4,)),
        ],
        compiler_params=pltpu.CompilerParams(collective_id=1, has_side_effects=True),
        name="halo",
    )(cotangent, saved_pre, cols, edge)


OPERANDS = tuple(range(17))


def main_kernel(live_counts, *refs):
    sources = refs[: len(OPERANDS)]
    (total_out, rows_in) = refs[len(OPERANDS) : len(OPERANDS) + 2]
    held = refs[len(OPERANDS) + 2 : 2 * len(OPERANDS) + 2]
    (
        index,
        owners,
        tokens,
        mask_token,
        proj_t,
        first,
        second,
        wide,
        narrow,
        fine,
        order,
        cot_rows,
        pre_rows,
        rows_c,
        rows_p,
        cols_c,
        cols_p,
    ) = held
    (
        taps,
        windows,
        hidden,
        deltas,
        taps_fine,
        windows_fine,
        payload,
        buf_a,
        red_a,
        buf_b,
        buf_c,
        buf_d,
        rows_out,
        tok_z,
        tok_s,
        buf_s,
        send,
        recv,
        local_sem,
        fetch,
    ) = refs[2 * len(OPERANDS) + 2 :]
    half = jnp.bfloat16
    n = lax.axis_index("ns")
    e = lax.axis_index("ew")
    n_count = lax.axis_size("ns")
    e_count = lax.axis_size("ew")
    g = lax.rem(n, GROUP_A)
    zl = lax.div(n, GROUP_A)
    zh = lax.div(e, GROUP_Y)
    y = lax.rem(e, GROUP_Y)
    zi = zh * Z_LOW + zl

    def peer_a(k):
        other = lax.rem(g + k, GROUP_A)
        return other, {"ew": e, "ns": zl * GROUP_A + other}

    def peer_b(k):
        other = lax.rem(y + k, GROUP_Y)
        return other, {"ew": zh * GROUP_Y + other, "ns": n}

    def peer_c(k):
        other = lax.rem(zi + k, Z_COUNT)
        return other, {
            "ew": lax.div(other, Z_LOW) * GROUP_Y + y,
            "ns": lax.rem(other, Z_LOW) * GROUP_A + g,
        }

    def peer_z(k):
        other = lax.rem(zl + k, Z_LOW)
        return other, {"ew": e, "ns": other * GROUP_A + g}

    barrier = pltpu.get_barrier_semaphore()
    for count, peer in ((GROUP_A, peer_a), (GROUP_Y, peer_b), (Z_COUNT, peer_c)):
        for k in range(1, count):
            pl.semaphore_signal(barrier, inc=1, device_id=peer(k)[1], device_id_type=MESH)

    fetched = fetch_all(tuple(zip(sources, held)), fetch)
    used = [0]

    def put(src, dst, target):
        slot = used[0]
        used[0] += 1
        copy = pltpu.make_async_remote_copy(
            src_ref=src,
            dst_ref=dst,
            send_sem=send.at[slot],
            recv_sem=recv.at[slot],
            device_id=target,
            device_id_type=MESH,
        )
        copy.start()
        return copy

    wait_all(fetched)

    token_t = dot_nt(proj_t[...], tokens[...]).astype(half)
    mask_row = mask_token[...].astype(jnp.float32).reshape(1, 768)
    mask_t = dot_nt(proj_t[...], jnp.broadcast_to(mask_row, (8, 768)).astype(half)).astype(half)
    mask_column = mask_t[:, 0:1].astype(jnp.float32)
    patch = lax.broadcasted_iota(jnp.int32, (256, 64), 0)
    slot = lax.broadcasted_iota(jnp.int32, (256, 64), 1)
    picks = []
    unseen = []
    first_in = []
    for f in range(2):
        hit = (patch == index[f : f + 1, :]) & (slot < live_counts[f])
        pick = jnp.where(hit, 1.0, 0.0).astype(half)
        picks.append(pick)
        shown = dot_nt(jnp.ones((8, 64), half), pick)
        unseen.append(1.0 - shown)
        placed = dot_nt(token_t[:, f * 64 : f * 64 + 64], pick)
        placed = placed + mask_column * unseen[f][0:1, :]
        first_in.append(placed.astype(half))
    first_grid = jnp.concatenate(first_in, axis=1)
    unseen = jnp.concatenate(unseen, axis=1)
    second_t = dot_tn(
        second[...].astype(jnp.float32).reshape(192, 64).astype(half), order[...]
    ).astype(half)

    row_second = lax.broadcasted_iota(jnp.int32, (128, 128), 0)
    lane_second = lax.broadcasted_iota(jnp.int32, (128, 128), 1)
    owner_row = jnp.concatenate([owners[0], owners[1]], axis=1)
    lane_row = lax.broadcasted_iota(jnp.int32, (1, 128), 1)
    live_row = lane_row < jnp.where(lane_row < 64, live_counts[0], live_counts[1] + 64)
    marked = jnp.where(live_row, owner_row, -1).astype(jnp.float32)
    across = jnp.broadcast_to(marked, (128, 128))
    down = across.T
    earlier = (across == down) & (row_second < lane_second)
    rank = jnp.sum(jnp.where(earlier, 1.0, 0.0), axis=0, keepdims=True)
    target = jnp.where(live_row, marked * 4.0 + rank, -1.0)
    number = lax.broadcasted_iota(jnp.int32, (96, 128), 0).astype(jnp.float32) * 2.0
    even = jnp.where(number == target, 1.0, 0.0).astype(half)
    odd = jnp.where(number + 1.0 == target, 1.0, 0.0).astype(half)

    north = n > 0
    south = n < n_count - 1
    west = e > 0
    east = e < e_count - 1

    def flag(condition, shape):
        return jnp.full(shape, jnp.where(condition, 1.0, 0.0), jnp.float32)

    row_16 = lax.broadcasted_iota(jnp.int32, (16, 128), 0)

    def side_cols(west_block, east_block):
        east_part = east_block.astype(jnp.float32) * flag(east, (16, 128))
        west_part = west_block.astype(jnp.float32) * flag(west, (16, 128))
        return jnp.where(row_16 < 8, east_part, west_part).astype(half)

    wide_map = wide[...]
    narrow_map = narrow[...]
    for f in range(2):
        for part in range(2):
            value = dot_nn(cot_rows[f, part * 8 : part * 8 + 8].reshape(128, 256), wide_map)
            side = side_cols(cols_c[0, f, part], cols_c[1, f, part])
            value = value + dot_tn(side, narrow_map)
            taps[f, 3 + part * 8 : 11 + part * 8] = value.astype(half).reshape(8, 16, 1024)
        value = dot_nn(rows_c[0, f].reshape(48, 256), wide_map)
        side = side_cols(cols_c[2, f, 1], cols_c[3, f, 1])
        value = (value + dot_tn(side, narrow_map)[80:128]) * flag(north, (48, 1024))
        taps[f, 0:3] = value.astype(half).reshape(3, 16, 1024)
        value = dot_nn(rows_c[1, f].reshape(48, 256), wide_map)
        side = side_cols(cols_c[4, f, 0], cols_c[5, f, 0])
        value = (value + dot_tn(side, narrow_map)[0:48]) * flag(south, (48, 1024))
        taps[f, 19:22] = value.astype(half).reshape(3, 16, 1024)

    lane = lax.broadcasted_iota(jnp.int32, (64, 128), 1)
    spot = lax.rem(lax.rem(lax.div(lane + 1, 2), 64), 10)
    right = lax.rem(lane, 2) == 0
    halo_pre = jnp.where(
        spot == 0,
        jnp.where(right, cols_p[3].astype(jnp.float32), cols_p[2].astype(jnp.float32)),
        jnp.where(
            spot == 9,
            jnp.where(right, cols_p[5].astype(jnp.float32), cols_p[4].astype(jnp.float32)),
            jnp.where(right, cols_p[1].astype(jnp.float32), cols_p[0].astype(jnp.float32)),
        ),
    )
    halo_keep = jnp.where(
        lane == 0, jnp.where(east, 1.0, 0.0), jnp.where(lane == 127, jnp.where(west, 1.0, 0.0), 0.0)
    )
    sigmoid = jax.nn.sigmoid(1.702 * halo_pre)
    halo_slope = sigmoid + 1.702 * halo_pre * sigmoid * (1.0 - sigmoid)

    for f in range(2):
        for i in range(10):
            window = jnp.concatenate(
                [
                    taps[f, 2 * i + a, :, b * 256 : b * 256 + 256]
                    for a in range(4)
                    for b in range(4)
                ],
                axis=0,
            )
            grad = dot_nn(second_t, window)
            if i == 0:
                center = rows_p[0, f]
            elif i == 9:
                center = rows_p[1, f]
            else:
                center = pre_rows[f, i - 1]
                windows[:, (f * 8 + i - 1) * 128 : (f * 8 + i) * 128] = window[:, :128]
            center = center.astype(jnp.float32)
            sigmoid = jax.nn.sigmoid(1.702 * center)
            slope = sigmoid + 1.702 * center * sigmoid * (1.0 - sigmoid)
            value = grad[:, :128] * slope
            if 0 < i < 9:
                hidden[:, (f * 8 + i - 1) * 128 : (f * 8 + i) * 128] = (center * sigmoid).astype(half)
            edge_slope = halo_slope
            if f + i > 0:
                edge_slope = pltpu.roll(halo_slope, 128 - 2 * (f * 10 + i), 1)
            edge_value = grad[:, 128:] * edge_slope * halo_keep
            if i == 0:
                value = value * flag(north, value.shape)
                edge_value = edge_value * flag(north, value.shape)
            if i == 9:
                value = value * flag(south, value.shape)
                edge_value = edge_value * flag(south, value.shape)
            deltas[f, i, :, 0:128] = value.astype(half)
            deltas[f, i, :, 128:256] = edge_value.astype(half)

    fine_map = fine[...]
    for f in range(2):
        for i in range(10):
            taps_fine[f, i] = dot_nn(deltas[f, i], fine_map).astype(half)
    low_lane = lane < 64
    for f in range(2):
        for pair in range(2):
            for a in range(4):
                for b in range(4):
                    low = taps_fine[f, 4 * pair + a, :, b * 128 : b * 128 + 128]
                    high = taps_fine[f, 4 * pair + 2 + a, :, b * 128 : b * 128 + 128]
                    windows_fine[
                        (a * 4 + b) * 64 : (a * 4 + b) * 64 + 64,
                        (f * 2 + pair) * 128 : (f * 2 + pair) * 128 + 128,
                    ] = jnp.where(low_lane, low, high)

    zeros_fine = jnp.zeros((64, 512), half)
    grad_first = dot_nt(windows_fine[0:512], jnp.concatenate([first_grid, zeros_fine], axis=0))
    grad_first = grad_first + dot_nt(
        windows_fine[512:1024], jnp.concatenate([zeros_fine, first_grid], axis=0)
    )
    payload[0] = grad_first.astype(half).reshape(GROUP_A, GROUP_Y, 8, 128)
    pl.semaphore_wait(barrier, GROUP_A + GROUP_Y + Z_COUNT - 3)

    def scatter_a(s):
        copies = []
        for k in range(1, GROUP_A):
            other, target_device = peer_a(k)
            copies.append(put(payload.at[s, other], buf_a.at[s, k - 1], target_device))
        return copies

    copies_a = [scatter_a(0)]

    grid = dot_tn(first[...], windows_fine[...]).astype(half)
    chosen = jnp.concatenate(
        [dot_nn(grid[:, f * 256 : f * 256 + 256], picks[f]) for f in range(2)], axis=1
    ).astype(half)
    zeros_slot = jnp.zeros((64, 128), half)
    outgoing = dot_nt(even, jnp.concatenate([chosen, zeros_slot], axis=0))
    outgoing = outgoing + dot_nt(odd, jnp.concatenate([zeros_slot, chosen], axis=0))
    rows_out[...] = outgoing.astype(half).reshape(Z_LOW, 16, 128)
    copies_z = []
    for k in range(1, Z_LOW):
        other, target_device = peer_z(k)
        copies_z.append(put(rows_out.at[other], tok_z.at[zl], target_device))
    tok_z[zl] = rows_out[zl]

    zeros_64 = jnp.zeros((64, 2048), half)
    hidden_value = hidden[...]
    grad_second = dot_nt(windows[0:128, :], jnp.concatenate([hidden_value, zeros_64], axis=0))
    grad_second = grad_second + dot_nt(
        windows[128:256, :], jnp.concatenate([zeros_64, hidden_value], axis=0)
    )
    mask_sum = jnp.sum(grid.astype(jnp.float32) * unseen[0:1, :], axis=1, keepdims=True)
    mask_sum_row = dot_nt(unseen.astype(half), jnp.concatenate([grid, zeros_fine], axis=0))
    grad_proj = dot_nn(chosen, tokens[...]) + mask_sum * mask_row
    mask_sum_row = mask_sum_row[0:1, :]
    mask_rest = mask_sum_row - mask_sum_row.astype(half).astype(jnp.float32)
    grad_second = jnp.where(
        (row_second == 12) & (lane_second < 64),
        mask_sum_row,
        jnp.where((row_second == 13) & (lane_second < 64), mask_rest, grad_second),
    )
    payload[1, 0:2] = grad_second.astype(half).reshape(2, GROUP_Y, 8, 128)
    for part in range(6):
        block = grad_proj[:, part * 128 : part * 128 + 128].astype(half)
        payload[1, 2 + part] = block.reshape(GROUP_Y, 8, 128)
    copies_a.append(scatter_a(1))

    copies_b = []
    for s in range(STREAMS):
        wait_all(copies_a[s])
        summed = payload[s, g].astype(jnp.float32)
        for k in range(1, GROUP_A):
            summed = summed + buf_a[s, k - 1].astype(jnp.float32)
        red_a[s] = summed
        copies = []
        for k in range(1, GROUP_Y):
            other, target_device = peer_b(k)
            copies.append(put(red_a.at[s, other], buf_b.at[s, k - 1], target_device))
        copies_b.append(copies)

    wait_all(copies_z)
    stacked = tok_z[...].reshape(Z_LOW * 16, 128)
    picked = lax.broadcasted_iota(jnp.int32, (GROUP_A * 16, Z_LOW * 16), 0)
    column = lax.broadcasted_iota(jnp.int32, (GROUP_A * 16, Z_LOW * 16), 1)
    wanted = ((picked % 16) // 2) * 16 + (picked // 16) * 2 + picked % 2
    choose = jnp.where(column == wanted, 1.0, 0.0).astype(half)
    tok_s[...] = dot_nn(choose, stacked).astype(half).reshape(GROUP_A, 16, 128)
    copies_t = []
    for k in range(1, GROUP_A):
        other, target_device = peer_a(k)
        copies_t.append(put(tok_s.at[other], buf_s.at[g], target_device))
    buf_s[g] = tok_s[g]

    copies_c = []
    for s in range(STREAMS):
        wait_all(copies_b[s])
        summed = red_a[s, y]
        for k in range(1, GROUP_Y):
            summed = summed + buf_b[s, k - 1]
        buf_c[s, zi] = summed
        copies = []
        for k in range(1, Z_COUNT):
            copies.append(put(buf_c.at[s, zi], buf_c.at[s, zi], peer_c(k)[1]))
        copies_c.append(copies)

    row_8 = lax.broadcasted_iota(jnp.int32, (8, 128), 0)
    copies_d = []
    for s in range(STREAMS):
        wait_all(copies_c[s])
        summed = buf_c[s, 0]
        for k in range(1, Z_COUNT):
            summed = summed + buf_c[s, k]
        if s == 1:
            mask_total = summed[4:5] + summed[5:6]
            rest = mask_total - mask_total.astype(half).astype(jnp.float32)
            here = jnp.where((g == 0) & (y == 1), 4, -2)
            summed = jnp.where(row_8 == here, mask_total, summed)
            summed = jnp.where(row_8 == here + 1, rest, summed)
        buf_d[s, y] = summed.astype(half)
        copies = []
        for k in range(1, GROUP_Y):
            copies.append(put(buf_d.at[s, y], buf_d.at[s, y], peer_b(k)[1]))
        copies_d.append(copies)

    copies_e = []
    own = []
    for s in range(STREAMS):
        wait_all(copies_d[s])
        for k in range(1, GROUP_A):
            copies_e.append(put(buf_d.at[s], total_out.at[s, g], peer_a(k)[1]))
        copy = pltpu.make_async_copy(buf_d.at[s], total_out.at[s, g], local_sem.at[s])
        copy.start()
        own.append(copy)
    wait_all(copies_t)
    rows_in[...] = buf_s[...]
    wait_all(own)
    wait_all(copies_e)


COPIES = 2 * (2 * (GROUP_A - 1) + 2 * (GROUP_Y - 1) + Z_COUNT - 1) + Z_LOW - 1 + GROUP_A - 1


def main(counts, arrays):
    vmem = pl.BlockSpec(memory_space=pltpu.VMEM)
    smem = pl.BlockSpec(memory_space=pltpu.SMEM)
    hbm = pl.BlockSpec(memory_space=pl.ANY)
    half = jnp.bfloat16
    wide = jnp.float32
    dma = pltpu.SemaphoreType.DMA
    return pl.pallas_call(
        main_kernel,
        out_shape=(
            jax.ShapeDtypeStruct((STREAMS, GROUP_A, GROUP_Y, 8, 128), half),
            jax.ShapeDtypeStruct((GROUP_A, 16, 128), half),
        ),
        in_specs=[smem] + [hbm] * len(arrays),
        out_specs=(hbm, vmem),
        scratch_shapes=[pltpu.VMEM(x.shape, x.dtype) for x in arrays]
        + [
            pltpu.VMEM((2, 22, 16, 1024), half),
            pltpu.VMEM((256, 2048), half),
            pltpu.VMEM((64, 2048), half),
            pltpu.VMEM((2, 10, 64, 256), half),
            pltpu.VMEM((2, 10, 64, 512), half),
            pltpu.VMEM((1024, 512), half),
            pltpu.VMEM((STREAMS, GROUP_A, GROUP_Y, 8, 128), half),
            pltpu.VMEM((STREAMS, GROUP_A - 1, GROUP_Y, 8, 128), half),
            pltpu.VMEM((STREAMS, GROUP_Y, 8, 128), wide),
            pltpu.VMEM((STREAMS, GROUP_Y - 1, 8, 128), wide),
            pltpu.VMEM((STREAMS, Z_COUNT, 8, 128), wide),
            pltpu.VMEM((STREAMS, GROUP_Y, 8, 128), half),
            pltpu.VMEM((Z_LOW, 16, 128), half),
            pltpu.VMEM((Z_LOW, 16, 128), half),
            pltpu.VMEM((GROUP_A, 16, 128), half),
            pltpu.VMEM((GROUP_A, 16, 128), half),
            dma((COPIES,)),
            dma((COPIES,)),
            dma((STREAMS,)),
            dma((len(arrays),)),
        ],
        compiler_params=pltpu.CompilerParams(collective_id=0, has_side_effects=True),
        name="main",
    )(counts, *arrays)


def finish_kernel(
    total, rows_in, proj_t, token_grad, grad_proj, grad_first, grad_second, grad_mask
):
    half = jnp.bfloat16
    row = lax.broadcasted_iota(jnp.int32, (192, 128), 0)
    column = lax.broadcasted_iota(jnp.int32, (192, 128), 1)
    tile = lax.div(row, 4)
    source = lax.rem(tile, 8) * 16 + lax.div(tile, 8) * 2 + lax.div(lax.rem(row, 4), 2)
    choose = jnp.where(column == source, 1.0, 0.0).astype(half)
    arrived = dot_nn(choose, rows_in[...].reshape(128, 128))
    arrived = jnp.where(lax.div(column, 64) == lax.rem(row, 2), arrived, 0.0).astype(half)
    double = jnp.concatenate([proj_t[...], proj_t[...]], axis=0)
    token_grad[...] = dot_nn(arrived, double).astype(half)
    packed = total[0].astype(jnp.float32).reshape(512, 128)
    grad_first[0:512] = packed[:, 0:64]
    grad_first[512:1024] = packed[:, 64:128]
    other = total[1].astype(jnp.float32).reshape(512, 128)
    for k in range(16):
        lanes = 64 * (k // 8)
        start = (k % 8) * 16
        grad_second[k // 4, :, k % 4, :] = other[start : start + 12, lanes : lanes + 64]
    for part in range(6):
        grad_proj[:, part * 128 : part * 128 + 128] = other[128 + part * 64 : 192 + part * 64]
    mask_row = other[12:13, 0:64] + other[13:14, 0:64]
    grad_mask[...] = jnp.dot(
        jnp.broadcast_to(mask_row, (8, 64)),
        proj_t[...].astype(jnp.float32),
        precision=lax.Precision.HIGHEST,
        preferred_element_type=jnp.float32,
    )[0:1].reshape(768)


def finish(total, rows_in, proj_t):
    vmem = pl.BlockSpec(memory_space=pltpu.VMEM)
    return pl.pallas_call(
        finish_kernel,
        out_shape=(
            jax.ShapeDtypeStruct((192, 768), jnp.bfloat16),
            jax.ShapeDtypeStruct((64, 768), jnp.float32),
            jax.ShapeDtypeStruct((1024, 64), jnp.float32),
            jax.ShapeDtypeStruct((4, 12, 4, 64), jnp.float32),
            jax.ShapeDtypeStruct((768,), jnp.float32),
        ),
        in_specs=[vmem] * 3,
        out_specs=(vmem,) * 5,
        name="finish",
    )(total, rows_in, proj_t)


def per_device(
    tokens,
    vis_index,
    counts,
    owners,
    mask_token,
    proj_weight,
    up_first,
    up_second,
    saved_pre,
    cotangent,
):
    wide, narrow, fine, edge, cols, order = tap_select()
    proj_t = proj_weight.T
    parts = halo(cotangent, saved_pre, cols, edge)
    total, rows_in = main(
        counts.reshape(2),
        [
            vis_index.reshape(2, 64),
            owners.reshape(2, 1, 64),
            tokens.reshape(128, 768),
            mask_token,
            proj_t,
            up_first.reshape(1024, 64),
            up_second.transpose(0, 2, 1, 3),
            wide,
            narrow,
            fine,
            order,
            *parts,
        ],
    )
    token_grad, grad_proj, grad_first, grad_second, grad_mask = finish(total, rows_in, proj_t)
    return (
        token_grad[None, None],
        grad_proj.T,
        grad_first.reshape(4, 4, 64, 64),
        grad_second.transpose(0, 2, 1, 3),
        grad_mask,
    )


def solution(mesh):
    return jax.shard_map(
        per_device,
        mesh=mesh,
        in_specs=(
            P("ns", "ew", None, None, None),
            P("ns", "ew", None, None),
            P("ns", "ew", None),
            P("ns", "ew", None, None, None),
            P(),
            P(),
            P(),
            P(),
            P(None, None, "ns", "ew"),
            P(None, None, "ns", "ew"),
        ),
        out_specs=(P("ns", "ew", None, None), P(), P(), P(), P()),
        check_vma=False,
    )
```

```python
import jax
import jax.numpy as jnp
import numpy as np
from jax import lax
from jax.experimental import pallas as pl
from jax.experimental.pallas import tpu as pltpu
from jax.sharding import PartitionSpec as P

MESH = pl.DeviceIdType.MESH
GROUP_A = 8
GROUP_Y = 8
Z_LOW = 6
Z_HIGH = 2


BANDS_PAD = 16
LANES = 128


def tap_select():
    wide = np.zeros((256, 4, 256), np.float32)
    halo = np.zeros((16, 4, 256), np.float32)
    for tap in range(4):
        for lane, cell in [(j, j) for j in range(128)] + [(128, 128), (255, -1)]:
            col = 2 * cell + tap - 1
            if col < 0:
                halo[8 + col + 3, tap, lane] = 1
            elif col < 256:
                wide[col, tap, lane] = 1
            else:
                halo[col - 256, tap, lane] = 1
    fine = np.zeros((256, 4, 2, 64), np.float32)
    for tap in range(4):
        for cell in range(64):
            col = 2 * cell + tap - 1
            fine[col if col >= 0 else 255, tap, :, cell] = 1
    edge = np.zeros((2, 8, 128, 128), np.float32)
    for frame in range(2):
        for row in range(8):
            spots = [row + 1] + ([0] if row == 7 else []) + ([9] if row == 0 else [])
            for spot in spots:
                pair = 2 * (frame * 10 + spot)
                edge[frame, row, 0, pair] = 1
                edge[frame, row, 127, (pair - 1) % 128] = 1
    cols = np.zeros((16, 256), np.float32)
    for k in range(3):
        cols[k, k] = 1
        cols[8 + k, 253 + k] = 1
    order = np.zeros((4, 12, 4, 4, 4, 16), np.float32)
    for a in range(4):
        for o in range(12):
            for b in range(4):
                order[a, o, b, a, b, o] = 1
    half = jnp.bfloat16
    return (
        jnp.asarray(wide.reshape(256, 1024), half),
        jnp.asarray(halo.reshape(16, 1024), half),
        jnp.asarray(fine.reshape(256, 512), half),
        jnp.asarray(edge.reshape(2048, 128), half),
        jnp.asarray(cols, half),
        jnp.asarray(order.reshape(192, 256), half),
    )


def dot_nn(a, b):
    return jnp.dot(a, b, preferred_element_type=jnp.float32)


def dot_nt(a, b):
    return lax.dot_general(a, b, (((1,), (1,)), ((), ())), preferred_element_type=jnp.float32)


def dot_tn(a, b):
    return lax.dot_general(a, b, (((0,), (0,)), ((), ())), preferred_element_type=jnp.float32)


SIDES = ((-1, 0), (1, 0), (0, -1), (0, 1), (-1, -1), (-1, 1), (1, -1), (1, 1))
STREAMS = 2
Z_COUNT = Z_LOW * Z_HIGH


def fetch_all(pairs, sem, first):
    copies = []
    for k, (src, dst) in enumerate(pairs):
        copy = pltpu.make_async_copy(src, dst, sem.at[first + k])
        copy.start()
        copies.append(copy)
    return copies


def wait_all(copies):
    for copy in copies:
        copy.wait()


EARLY = 4
MAIN_VMEM = 24 * 1024 * 1024
FINISH_VMEM = 8 * 1024 * 1024
OPERANDS = tuple(range(16))


def main_kernel(*refs):
    sources = refs[: len(OPERANDS)]
    (total_out, rows_in) = refs[len(OPERANDS) : len(OPERANDS) + 2]
    held = refs[len(OPERANDS) + 2 : 2 * len(OPERANDS) + 2]
    (
        cot,
        cols,
        pre,
        edge,
        live_counts,
        index,
        owners,
        tokens,
        mask_token,
        proj_t,
        first,
        second,
        wide,
        narrow,
        fine,
        order,
    ) = held
    (
        wide_c,
        wide_p,
        cot_rows,
        cot_cols,
        pre_rows,
        pre_cols,
        rows_c,
        rows_p,
        cols_c,
        cols_p,
        slopes,
        taps,
        windows,
        hidden,
        deltas,
        taps_fine,
        windows_fine,
        payload,
        buf_a,
        red_a,
        buf_b,
        buf_c,
        buf_d,
        rows_out,
        tok_z,
        tok_s,
        buf_s,
        send,
        recv,
        local_sem,
        fetch,
    ) = refs[2 * len(OPERANDS) + 2 :]
    half = jnp.bfloat16
    n = lax.axis_index("ns")
    e = lax.axis_index("ew")
    n_count = lax.axis_size("ns")
    e_count = lax.axis_size("ew")
    g = lax.rem(n, GROUP_A)
    zl = lax.div(n, GROUP_A)
    zh = lax.div(e, GROUP_Y)
    y = lax.rem(e, GROUP_Y)
    zi = zh * Z_LOW + zl

    def peer_side(side):
        return {
            "ew": lax.rem(e + side[1] + e_count, e_count),
            "ns": lax.rem(n + side[0] + n_count, n_count),
        }

    def peer_a(k):
        other = lax.rem(g + k, GROUP_A)
        return other, {"ew": e, "ns": zl * GROUP_A + other}

    def peer_b(k):
        other = lax.rem(y + k, GROUP_Y)
        return other, {"ew": zh * GROUP_Y + other, "ns": n}

    def peer_c(k):
        other = lax.rem(zi + k, Z_COUNT)
        return other, {
            "ew": lax.div(other, Z_LOW) * GROUP_Y + y,
            "ns": lax.rem(other, Z_LOW) * GROUP_A + g,
        }

    def peer_z(k):
        other = lax.rem(zl + k, Z_LOW)
        return other, {"ew": e, "ns": other * GROUP_A + g}

    pairs = tuple(zip(sources, held))
    early = fetch_all(pairs[:EARLY], fetch, 0)
    barrier = pltpu.get_barrier_semaphore()
    for side in SIDES:
        pl.semaphore_signal(barrier, inc=1, device_id=peer_side(side), device_id_type=MESH)
    for count, peer in ((GROUP_A, peer_a), (GROUP_Y, peer_b), (Z_COUNT, peer_c)):
        for k in range(1, count):
            pl.semaphore_signal(barrier, inc=1, device_id=peer(k)[1], device_id_type=MESH)

    later = fetch_all(pairs[EARLY:], fetch, EARLY)
    used = [0]

    def put(src, dst, target):
        slot = used[0]
        used[0] += 1
        copy = pltpu.make_async_remote_copy(
            src_ref=src,
            dst_ref=dst,
            send_sem=send.at[slot],
            recv_sem=recv.at[slot],
            device_id=target,
            device_id_type=MESH,
        )
        copy.start()
        return copy

    wait_all(early)
    for f in range(2):
        for o in range(12):
            for part in range(2):
                wide_c[part, pl.ds((f * 16 + o) * 16, 16), :] = cot[
                    f, o, :, part * 128 : part * 128 + 128
                ].astype(jnp.float32)
        for part in range(2):
            wide_c[part, pl.ds((f * 16 + 12) * 16, 64), :] = jnp.zeros((64, 128), jnp.float32)
        for r in range(16):
            for part in range(2):
                cot_rows[f, r, :, part * 128 : part * 128 + 128] = wide_c[
                    part, pl.ds(f * 256 + r, 16, stride=16), :
                ].astype(half)
        for part in range(2):
            block = cot_rows[f, part * 8 : part * 8 + 8].reshape(128, 256)
            cot_cols[f, part] = dot_nt(cols[...], block).astype(half)
    for f in range(2):
        wide_p[pl.ds(f * 512, 512), :] = pre[f].reshape(512, 128).astype(jnp.float32)
    packed = jnp.zeros((64, 128), jnp.float32)
    for f in range(2):
        for i in range(8):
            slab = wide_p[pl.ds(f * 512 + i, 64, stride=8), :].astype(half)
            pre_rows[f, i] = slab
            packed = packed + dot_nn(slab, edge[pl.ds((f * 8 + i) * 128, 128), :])
    pre_cols[...] = packed.astype(half)

    pl.semaphore_wait(barrier, len(SIDES) + GROUP_A + GROUP_Y + Z_COUNT - 3)

    halo = []
    halo.append(put(cot_cols, cols_c.at[1], peer_side((0, -1))))
    halo.append(put(cot_cols, cols_c.at[0], peer_side((0, 1))))
    halo.append(put(pre_cols, cols_p.at[1], peer_side((0, -1))))
    halo.append(put(pre_cols, cols_p.at[0], peer_side((0, 1))))
    halo.append(put(cot_cols, cols_c.at[5], peer_side((-1, -1))))
    halo.append(put(cot_cols, cols_c.at[4], peer_side((-1, 1))))
    halo.append(put(cot_cols, cols_c.at[3], peer_side((1, -1))))
    halo.append(put(cot_cols, cols_c.at[2], peer_side((1, 1))))
    halo.append(put(pre_cols, cols_p.at[5], peer_side((-1, -1))))
    halo.append(put(pre_cols, cols_p.at[4], peer_side((-1, 1))))
    halo.append(put(pre_cols, cols_p.at[3], peer_side((1, -1))))
    halo.append(put(pre_cols, cols_p.at[2], peer_side((1, 1))))
    halo.append(put(cot_rows.at[:, 0:3], rows_c.at[1], peer_side((-1, 0))))
    halo.append(put(cot_rows.at[:, 13:16], rows_c.at[0], peer_side((1, 0))))
    halo.append(put(pre_rows.at[:, 0], rows_p.at[1], peer_side((-1, 0))))
    halo.append(put(pre_rows.at[:, 7], rows_p.at[0], peer_side((1, 0))))

    wait_all(later)

    for f in range(2):
        for i in range(8):
            center = wide_p[pl.ds(f * 512 + i, 64, stride=8), :]
            sigmoid = jax.nn.sigmoid(1.702 * center)
            slopes[f, i] = sigmoid + 1.702 * center * sigmoid * (1.0 - sigmoid)
            hidden[:, (f * 8 + i) * 128 : (f * 8 + i + 1) * 128] = (center * sigmoid).astype(half)

    token_t = dot_nt(proj_t[...], tokens[...]).astype(half)
    mask_row = mask_token[...].astype(jnp.float32).reshape(1, 768)
    mask_t = dot_nt(proj_t[...], jnp.broadcast_to(mask_row, (8, 768)).astype(half)).astype(half)
    mask_column = mask_t[:, 0:1].astype(jnp.float32)
    patch = lax.broadcasted_iota(jnp.int32, (256, 64), 0)
    slot = lax.broadcasted_iota(jnp.int32, (256, 64), 1)
    picks = []
    unseen = []
    first_in = []
    for f in range(2):
        hit = (patch == index[f : f + 1, :]) & (slot < live_counts[f])
        pick = jnp.where(hit, 1.0, 0.0).astype(half)
        picks.append(pick)
        shown = dot_nt(jnp.ones((8, 64), half), pick)
        unseen.append(1.0 - shown)
        placed = dot_nt(token_t[:, f * 64 : f * 64 + 64], pick)
        placed = placed + mask_column * unseen[f][0:1, :]
        first_in.append(placed.astype(half))
    first_grid = jnp.concatenate(first_in, axis=1)
    unseen = jnp.concatenate(unseen, axis=1)
    second_t = dot_tn(
        second[...].astype(jnp.float32).reshape(192, 64).astype(half), order[...]
    ).astype(half)

    row_second = lax.broadcasted_iota(jnp.int32, (128, 128), 0)
    lane_second = lax.broadcasted_iota(jnp.int32, (128, 128), 1)
    owner_row = jnp.concatenate([owners[0], owners[1]], axis=1)
    lane_row = lax.broadcasted_iota(jnp.int32, (1, 128), 1)
    live_row = lane_row < jnp.where(lane_row < 64, live_counts[0], live_counts[1] + 64)
    marked = jnp.where(live_row, owner_row, -1).astype(jnp.float32)
    across = jnp.broadcast_to(marked, (128, 128))
    down = across.T
    earlier = (across == down) & (row_second < lane_second)
    rank = jnp.sum(jnp.where(earlier, 1.0, 0.0), axis=0, keepdims=True)
    target = jnp.where(live_row, marked * 4.0 + rank, -1.0)
    number = lax.broadcasted_iota(jnp.int32, (96, 128), 0).astype(jnp.float32) * 2.0
    even = jnp.where(number == target, 1.0, 0.0).astype(half)
    odd = jnp.where(number + 1.0 == target, 1.0, 0.0).astype(half)

    wait_all(halo)

    north = n > 0
    south = n < n_count - 1
    west = e > 0
    east = e < e_count - 1

    def flag(condition, shape):
        return jnp.full(shape, jnp.where(condition, 1.0, 0.0), jnp.float32)

    row_16 = lax.broadcasted_iota(jnp.int32, (16, 128), 0)

    def side_cols(west_block, east_block):
        east_part = east_block.astype(jnp.float32) * flag(east, (16, 128))
        west_part = west_block.astype(jnp.float32) * flag(west, (16, 128))
        return jnp.where(row_16 < 8, east_part, west_part).astype(half)

    wide_map = wide[...]
    narrow_map = narrow[...]
    for f in range(2):
        for part in range(2):
            value = dot_nn(cot_rows[f, part * 8 : part * 8 + 8].reshape(128, 256), wide_map)
            side = side_cols(cols_c[0, f, part], cols_c[1, f, part])
            value = value + dot_tn(side, narrow_map)
            taps[f, 3 + part * 8 : 11 + part * 8] = value.astype(half).reshape(8, 16, 1024)
        value = dot_nn(rows_c[0, f].reshape(48, 256), wide_map)
        side = side_cols(cols_c[2, f, 1], cols_c[3, f, 1])
        value = (value + dot_tn(side, narrow_map)[80:128]) * flag(north, (48, 1024))
        taps[f, 0:3] = value.astype(half).reshape(3, 16, 1024)
        value = dot_nn(rows_c[1, f].reshape(48, 256), wide_map)
        side = side_cols(cols_c[4, f, 0], cols_c[5, f, 0])
        value = (value + dot_tn(side, narrow_map)[0:48]) * flag(south, (48, 1024))
        taps[f, 19:22] = value.astype(half).reshape(3, 16, 1024)

    lane = lax.broadcasted_iota(jnp.int32, (64, 128), 1)
    spot = lax.rem(lax.rem(lax.div(lane + 1, 2), 64), 10)
    right = lax.rem(lane, 2) == 0
    halo_pre = jnp.where(
        spot == 0,
        jnp.where(right, cols_p[3].astype(jnp.float32), cols_p[2].astype(jnp.float32)),
        jnp.where(
            spot == 9,
            jnp.where(right, cols_p[5].astype(jnp.float32), cols_p[4].astype(jnp.float32)),
            jnp.where(right, cols_p[1].astype(jnp.float32), cols_p[0].astype(jnp.float32)),
        ),
    )
    halo_keep = jnp.where(
        lane == 0, jnp.where(east, 1.0, 0.0), jnp.where(lane == 127, jnp.where(west, 1.0, 0.0), 0.0)
    )
    sigmoid = jax.nn.sigmoid(1.702 * halo_pre)
    halo_slope = sigmoid + 1.702 * halo_pre * sigmoid * (1.0 - sigmoid)

    for f in range(2):
        for i in range(10):
            window = jnp.concatenate(
                [
                    taps[f, 2 * i + a, :, b * 256 : b * 256 + 256]
                    for a in range(4)
                    for b in range(4)
                ],
                axis=0,
            )
            grad = dot_nn(second_t, window)
            if 0 < i < 9:
                windows[:, (f * 8 + i - 1) * 128 : (f * 8 + i) * 128] = window[:, :128]
                slope = slopes[f, i - 1]
            else:
                center = rows_p[i // 9, f].astype(jnp.float32)
                sigmoid = jax.nn.sigmoid(1.702 * center)
                slope = sigmoid + 1.702 * center * sigmoid * (1.0 - sigmoid)
            value = grad[:, :128] * slope
            edge_slope = halo_slope
            if f + i > 0:
                edge_slope = pltpu.roll(halo_slope, 128 - 2 * (f * 10 + i), 1)
            edge_value = grad[:, 128:] * edge_slope * halo_keep
            if i == 0:
                value = value * flag(north, value.shape)
                edge_value = edge_value * flag(north, value.shape)
            if i == 9:
                value = value * flag(south, value.shape)
                edge_value = edge_value * flag(south, value.shape)
            deltas[f, i, :, 0:128] = value.astype(half)
            deltas[f, i, :, 128:256] = edge_value.astype(half)

    fine_map = fine[...]
    for f in range(2):
        for i in range(10):
            taps_fine[f, i] = dot_nn(deltas[f, i], fine_map).astype(half)
    low_lane = lane < 64
    for f in range(2):
        for pair in range(2):
            for a in range(4):
                for b in range(4):
                    low = taps_fine[f, 4 * pair + a, :, b * 128 : b * 128 + 128]
                    high = taps_fine[f, 4 * pair + 2 + a, :, b * 128 : b * 128 + 128]
                    windows_fine[
                        (a * 4 + b) * 64 : (a * 4 + b) * 64 + 64,
                        (f * 2 + pair) * 128 : (f * 2 + pair) * 128 + 128,
                    ] = jnp.where(low_lane, low, high)

    zeros_fine = jnp.zeros((64, 512), half)
    grad_first = dot_nt(windows_fine[0:512], jnp.concatenate([first_grid, zeros_fine], axis=0))
    grad_first = grad_first + dot_nt(
        windows_fine[512:1024], jnp.concatenate([zeros_fine, first_grid], axis=0)
    )
    payload[0] = grad_first.astype(half).reshape(GROUP_A, GROUP_Y, 8, 128)

    def scatter_a(s):
        copies = []
        for k in range(1, GROUP_A):
            other, target_device = peer_a(k)
            copies.append(put(payload.at[s, other], buf_a.at[s, k - 1], target_device))
        return copies

    copies_a = [scatter_a(0)]

    grid = dot_tn(first[...], windows_fine[...]).astype(half)
    chosen = jnp.concatenate(
        [dot_nn(grid[:, f * 256 : f * 256 + 256], picks[f]) for f in range(2)], axis=1
    ).astype(half)
    zeros_slot = jnp.zeros((64, 128), half)
    outgoing = dot_nt(even, jnp.concatenate([chosen, zeros_slot], axis=0))
    outgoing = outgoing + dot_nt(odd, jnp.concatenate([zeros_slot, chosen], axis=0))
    rows_out[...] = outgoing.astype(half).reshape(Z_LOW, 16, 128)
    copies_z = []
    for k in range(1, Z_LOW):
        other, target_device = peer_z(k)
        copies_z.append(put(rows_out.at[other], tok_z.at[zl], target_device))
    tok_z[zl] = rows_out[zl]

    zeros_64 = jnp.zeros((64, 2048), half)
    hidden_value = hidden[...]
    grad_second = dot_nt(windows[0:128, :], jnp.concatenate([hidden_value, zeros_64], axis=0))
    grad_second = grad_second + dot_nt(
        windows[128:256, :], jnp.concatenate([zeros_64, hidden_value], axis=0)
    )
    mask_sum = jnp.sum(grid.astype(jnp.float32) * unseen[0:1, :], axis=1, keepdims=True)
    mask_sum_row = dot_nt(unseen.astype(half), jnp.concatenate([grid, zeros_fine], axis=0))
    grad_proj = dot_nn(chosen, tokens[...]) + mask_sum * mask_row
    mask_sum_row = mask_sum_row[0:1, :]
    mask_rest = mask_sum_row - mask_sum_row.astype(half).astype(jnp.float32)
    grad_second = jnp.where(
        (row_second == 12) & (lane_second < 64),
        mask_sum_row,
        jnp.where((row_second == 13) & (lane_second < 64), mask_rest, grad_second),
    )
    payload[1, 0:2] = grad_second.astype(half).reshape(2, GROUP_Y, 8, 128)
    for part in range(6):
        block = grad_proj[:, part * 128 : part * 128 + 128].astype(half)
        payload[1, 2 + part] = block.reshape(GROUP_Y, 8, 128)
    copies_a.append(scatter_a(1))

    copies_b = []
    for s in range(STREAMS):
        wait_all(copies_a[s])
        summed = payload[s, g].astype(jnp.float32)
        for k in range(1, GROUP_A):
            summed = summed + buf_a[s, k - 1].astype(jnp.float32)
        red_a[s] = summed
        copies = []
        for k in range(1, GROUP_Y):
            other, target_device = peer_b(k)
            copies.append(put(red_a.at[s, other], buf_b.at[s, k - 1], target_device))
        copies_b.append(copies)

    wait_all(copies_z)
    stacked = tok_z[...].reshape(Z_LOW * 16, 128)
    picked = lax.broadcasted_iota(jnp.int32, (GROUP_A * 16, Z_LOW * 16), 0)
    column = lax.broadcasted_iota(jnp.int32, (GROUP_A * 16, Z_LOW * 16), 1)
    wanted = ((picked % 16) // 2) * 16 + (picked // 16) * 2 + picked % 2
    choose = jnp.where(column == wanted, 1.0, 0.0).astype(half)
    tok_s[...] = dot_nn(choose, stacked).astype(half).reshape(GROUP_A, 16, 128)
    copies_t = []
    for k in range(1, GROUP_A):
        other, target_device = peer_a(k)
        copies_t.append(put(tok_s.at[other], buf_s.at[g], target_device))
    buf_s[g] = tok_s[g]

    copies_c = []
    for s in range(STREAMS):
        wait_all(copies_b[s])
        summed = red_a[s, y]
        for k in range(1, GROUP_Y):
            summed = summed + buf_b[s, k - 1]
        buf_c[s, zi] = summed
        copies = []
        for k in range(1, Z_COUNT):
            copies.append(put(buf_c.at[s, zi], buf_c.at[s, zi], peer_c(k)[1]))
        copies_c.append(copies)

    row_8 = lax.broadcasted_iota(jnp.int32, (8, 128), 0)
    copies_d = []
    for s in range(STREAMS):
        wait_all(copies_c[s])
        summed = buf_c[s, 0]
        for k in range(1, Z_COUNT):
            summed = summed + buf_c[s, k]
        if s == 1:
            mask_total = summed[4:5] + summed[5:6]
            rest = mask_total - mask_total.astype(half).astype(jnp.float32)
            here = jnp.where((g == 0) & (y == 1), 4, -2)
            summed = jnp.where(row_8 == here, mask_total, summed)
            summed = jnp.where(row_8 == here + 1, rest, summed)
        buf_d[s, y] = summed.astype(half)
        copies = []
        for k in range(1, GROUP_Y):
            copies.append(put(buf_d.at[s, y], buf_d.at[s, y], peer_b(k)[1]))
        copies_d.append(copies)

    copies_e = []
    own = []
    for s in range(STREAMS):
        wait_all(copies_d[s])
        for k in range(1, GROUP_A):
            copies_e.append(put(buf_d.at[s], total_out.at[s, g], peer_a(k)[1]))
        copy = pltpu.make_async_copy(buf_d.at[s], total_out.at[s, g], local_sem.at[s])
        copy.start()
        own.append(copy)
    wait_all(copies_t)
    rows_in[...] = buf_s[...]
    wait_all(own)
    wait_all(copies_e)


COPIES = 16 + 2 * (2 * (GROUP_A - 1) + 2 * (GROUP_Y - 1) + Z_COUNT - 1) + Z_LOW - 1 + GROUP_A - 1


def main(arrays):
    vmem = pl.BlockSpec(memory_space=pltpu.VMEM)
    hbm = pl.BlockSpec(memory_space=pl.ANY)
    half = jnp.bfloat16
    wide = jnp.float32
    dma = pltpu.SemaphoreType.DMA
    return pl.pallas_call(
        main_kernel,
        out_shape=(
            jax.ShapeDtypeStruct((STREAMS, GROUP_A, GROUP_Y, 8, 128), half),
            jax.ShapeDtypeStruct((GROUP_A, 16, 128), half),
        ),
        in_specs=[pl.BlockSpec(memory_space=pltpu.HBM)] * len(arrays),
        out_specs=(hbm, vmem),
        scratch_shapes=[
            (pltpu.SMEM if x.ndim == 1 and x.dtype == jnp.int32 else pltpu.VMEM)(x.shape, x.dtype)
            for x in arrays
        ]
        + [
            pltpu.VMEM((2, 512, 128), wide),
            pltpu.VMEM((1024, 128), wide),
            pltpu.VMEM((2, 16, 16, 256), half),
            pltpu.VMEM((2, 2, 16, 128), half),
            pltpu.VMEM((2, 8, 64, 128), half),
            pltpu.VMEM((64, 128), half),
            pltpu.VMEM((2, 2, 3, 16, 256), half),
            pltpu.VMEM((2, 2, 64, 128), half),
            pltpu.VMEM((6, 2, 2, 16, 128), half),
            pltpu.VMEM((6, 64, 128), half),
            pltpu.VMEM((2, 8, 64, 128), wide),
            pltpu.VMEM((2, 22, 16, 1024), half),
            pltpu.VMEM((256, 2048), half),
            pltpu.VMEM((64, 2048), half),
            pltpu.VMEM((2, 10, 64, 256), half),
            pltpu.VMEM((2, 10, 64, 512), half),
            pltpu.VMEM((1024, 512), half),
            pltpu.VMEM((STREAMS, GROUP_A, GROUP_Y, 8, 128), half),
            pltpu.VMEM((STREAMS, GROUP_A - 1, GROUP_Y, 8, 128), half),
            pltpu.VMEM((STREAMS, GROUP_Y, 8, 128), wide),
            pltpu.VMEM((STREAMS, GROUP_Y - 1, 8, 128), wide),
            pltpu.VMEM((STREAMS, Z_COUNT, 8, 128), wide),
            pltpu.VMEM((STREAMS, GROUP_Y, 8, 128), half),
            pltpu.VMEM((Z_LOW, 16, 128), half),
            pltpu.VMEM((Z_LOW, 16, 128), half),
            pltpu.VMEM((GROUP_A, 16, 128), half),
            pltpu.VMEM((GROUP_A, 16, 128), half),
            dma((COPIES,)),
            dma((COPIES,)),
            dma((STREAMS,)),
            dma((len(arrays),)),
        ],
        compiler_params=pltpu.CompilerParams(
            collective_id=0, has_side_effects=True, vmem_limit_bytes=MAIN_VMEM
        ),
        name="main",
    )(*[pltpu.with_memory_space_constraint(x, pltpu.HBM) for x in arrays])


def finish_kernel(
    total, rows_in, proj_t, token_grad, grad_proj, grad_first, grad_second, grad_mask
):
    half = jnp.bfloat16
    row = lax.broadcasted_iota(jnp.int32, (192, 128), 0)
    column = lax.broadcasted_iota(jnp.int32, (192, 128), 1)
    tile = lax.div(row, 4)
    source = lax.rem(tile, 8) * 16 + lax.div(tile, 8) * 2 + lax.div(lax.rem(row, 4), 2)
    choose = jnp.where(column == source, 1.0, 0.0).astype(half)
    arrived = dot_nn(choose, rows_in[...].reshape(128, 128))
    arrived = jnp.where(lax.div(column, 64) == lax.rem(row, 2), arrived, 0.0).astype(half)
    double = jnp.concatenate([proj_t[...], proj_t[...]], axis=0)
    token_grad[...] = dot_nn(arrived, double).astype(half)
    packed = total[0].astype(jnp.float32).reshape(512, 128)
    grad_first[0:512] = packed[:, 0:64]
    grad_first[512:1024] = packed[:, 64:128]
    other = total[1].astype(jnp.float32).reshape(512, 128)
    for k in range(16):
        lanes = 64 * (k // 8)
        start = (k % 8) * 16
        grad_second[k // 4, :, k % 4, :] = other[start : start + 12, lanes : lanes + 64]
    for part in range(6):
        grad_proj[:, part * 128 : part * 128 + 128] = other[128 + part * 64 : 192 + part * 64]
    mask_row = other[12:13, 0:64] + other[13:14, 0:64]
    grad_mask[...] = jnp.dot(
        jnp.broadcast_to(mask_row, (8, 64)),
        proj_t[...].astype(jnp.float32),
        precision=lax.Precision.HIGHEST,
        preferred_element_type=jnp.float32,
    )[0:1].reshape(768)


def finish(total, rows_in, proj_t):
    vmem = pl.BlockSpec(memory_space=pltpu.VMEM)
    return pl.pallas_call(
        finish_kernel,
        out_shape=(
            jax.ShapeDtypeStruct((192, 768), jnp.bfloat16),
            jax.ShapeDtypeStruct((64, 768), jnp.float32),
            jax.ShapeDtypeStruct((1024, 64), jnp.float32),
            jax.ShapeDtypeStruct((4, 12, 4, 64), jnp.float32),
            jax.ShapeDtypeStruct((768,), jnp.float32),
        ),
        in_specs=[vmem] * 3,
        out_specs=(vmem,) * 5,
        compiler_params=pltpu.CompilerParams(vmem_limit_bytes=FINISH_VMEM),
        name="finish",
    )(total, rows_in, proj_t)


def per_device(
    tokens,
    vis_index,
    counts,
    owners,
    mask_token,
    proj_weight,
    up_first,
    up_second,
    saved_pre,
    cotangent,
):
    wide, narrow, fine, edge, cols, order = tap_select()
    proj_t = proj_weight.T
    total, rows_in = main(
        [
            cotangent,
            cols,
            saved_pre,
            edge,
            counts.reshape(2),
            vis_index.reshape(2, 64),
            owners.reshape(2, 1, 64),
            tokens.reshape(128, 768),
            mask_token,
            proj_t,
            up_first.reshape(1024, 64),
            up_second.transpose(0, 2, 1, 3),
            wide,
            narrow,
            fine,
            order,
        ],
    )
    token_grad, grad_proj, grad_first, grad_second, grad_mask = finish(total, rows_in, proj_t)
    return (
        token_grad[None, None],
        grad_proj.T,
        grad_first.reshape(4, 4, 64, 64),
        grad_second.transpose(0, 2, 1, 3),
        grad_mask,
    )


def solution(mesh):
    return jax.shard_map(
        per_device,
        mesh=mesh,
        in_specs=(
            P("ns", "ew", None, None, None),
            P("ns", "ew", None, None),
            P("ns", "ew", None),
            P("ns", "ew", None, None, None),
            P(),
            P(),
            P(),
            P(),
            P(None, None, "ns", "ew"),
            P(None, None, "ns", "ew"),
        ),
        out_specs=(P("ns", "ew", None, None), P(), P(), P(), P()),
        check_vma=False,
    )
```

```python
import jax
import jax.numpy as jnp
import numpy as np
from jax import lax
from jax.experimental import pallas as pl
from jax.experimental.pallas import tpu as pltpu
from jax.sharding import PartitionSpec as P

MESH = pl.DeviceIdType.MESH
GROUP_A = 8
GROUP_Y = 8
Z_LOW = 6
Z_HIGH = 2


BANDS_PAD = 16
LANES = 128


def tap_select():
    wide = np.zeros((256, 4, 256), np.float32)
    halo = np.zeros((16, 4, 256), np.float32)
    for tap in range(4):
        for lane, cell in [(j, j) for j in range(128)] + [(128, 128), (255, -1)]:
            col = 2 * cell + tap - 1
            if col < 0:
                halo[8 + col + 3, tap, lane] = 1
            elif col < 256:
                wide[col, tap, lane] = 1
            else:
                halo[col - 256, tap, lane] = 1
    fine = np.zeros((256, 4, 2, 64), np.float32)
    for tap in range(4):
        for cell in range(64):
            col = 2 * cell + tap - 1
            fine[col if col >= 0 else 255, tap, :, cell] = 1
    edge = np.zeros((8, 2, 16, 128), np.float32)
    place = np.zeros((2, 16, 2, 128), np.float32)
    for row in range(8):
        for spot in [row + 1] + ([0] if row == 7 else []) + ([9] if row == 0 else []):
            edge[row, 0, spot, 0] = 1
            edge[row, 1, spot, 127] = 1
    for frame in range(2):
        for spot in range(10):
            pair = 2 * (frame * 10 + spot)
            place[0, spot, frame, pair] = 1
            place[1, spot, frame, (pair - 1) % 128] = 1
    cols = np.zeros((16, 256), np.float32)
    for k in range(3):
        cols[k, k] = 1
        cols[8 + k, 253 + k] = 1
    order = np.zeros((4, 12, 4, 4, 4, 16), np.float32)
    for a in range(4):
        for o in range(12):
            for b in range(4):
                order[a, o, b, a, b, o] = 1
    half = jnp.bfloat16
    return (
        jnp.asarray(wide.reshape(256, 1024), half),
        jnp.asarray(halo.reshape(16, 1024), half),
        jnp.asarray(fine.reshape(256, 512), half),
        jnp.asarray(edge.reshape(8, 32, 128), half),
        jnp.asarray(place.reshape(32, 256), half),
        jnp.asarray(cols, half),
        jnp.asarray(order.reshape(192, 256), half),
    )


def dot_nn(a, b):
    return jnp.dot(a, b, preferred_element_type=jnp.float32)


def dot_nt(a, b):
    return lax.dot_general(a, b, (((1,), (1,)), ((), ())), preferred_element_type=jnp.float32)


def dot_tn(a, b):
    return lax.dot_general(a, b, (((0,), (0,)), ((), ())), preferred_element_type=jnp.float32)


SIDES = ((-1, 0), (1, 0), (0, -1), (0, 1), (-1, -1), (-1, 1), (1, -1), (1, 1))
STREAMS = 2
Z_COUNT = Z_LOW * Z_HIGH


def fetch_all(pairs, sem, first):
    copies = []
    for k, (src, dst) in enumerate(pairs):
        copy = pltpu.make_async_copy(src, dst, sem.at[first + k])
        copy.start()
        copies.append(copy)
    return copies


def wait_all(copies):
    for copy in copies:
        copy.wait()


EARLY = 4
MAIN_VMEM = 24 * 1024 * 1024
FINISH_VMEM = 8 * 1024 * 1024
OPERANDS = tuple(range(17))


def main_kernel(*refs):
    sources = refs[: len(OPERANDS)]
    (total_out, rows_in) = refs[len(OPERANDS) : len(OPERANDS) + 2]
    held = refs[len(OPERANDS) + 2 : 2 * len(OPERANDS) + 2]
    (
        cot,
        cols,
        pre,
        edge,
        live_counts,
        index,
        owners,
        tokens,
        mask_token,
        proj_t,
        first,
        second,
        wide,
        narrow,
        fine,
        order,
        place,
    ) = held
    (
        wide_c,
        wide_p,
        cot_rows,
        cot_cols,
        pre_rows,
        pre_cols,
        rows_c,
        rows_p,
        cols_c,
        corners_c,
        cols_p,
        slopes,
        taps,
        windows,
        hidden,
        deltas,
        taps_fine,
        windows_fine,
        payload,
        buf_a,
        red_a,
        buf_b,
        buf_c,
        buf_d,
        rows_out,
        tok_z,
        tok_s,
        buf_s,
        send,
        recv,
        local_sem,
        fetch,
    ) = refs[2 * len(OPERANDS) + 2 :]
    half = jnp.bfloat16
    n = lax.axis_index("ns")
    e = lax.axis_index("ew")
    n_count = lax.axis_size("ns")
    e_count = lax.axis_size("ew")
    g = lax.rem(n, GROUP_A)
    zl = lax.div(n, GROUP_A)
    zh = lax.div(e, GROUP_Y)
    y = lax.rem(e, GROUP_Y)
    zi = zh * Z_LOW + zl

    def peer_side(side):
        return {
            "ew": lax.rem(e + side[1] + e_count, e_count),
            "ns": lax.rem(n + side[0] + n_count, n_count),
        }

    def peer_a(k):
        other = lax.rem(g + k, GROUP_A)
        return other, {"ew": e, "ns": zl * GROUP_A + other}

    def peer_b(k):
        other = lax.rem(y + k, GROUP_Y)
        return other, {"ew": zh * GROUP_Y + other, "ns": n}

    def peer_c(k):
        other = lax.rem(zi + k, Z_COUNT)
        return other, {
            "ew": lax.div(other, Z_LOW) * GROUP_Y + y,
            "ns": lax.rem(other, Z_LOW) * GROUP_A + g,
        }

    def peer_z(k):
        other = lax.rem(zl + k, Z_LOW)
        return other, {"ew": e, "ns": other * GROUP_A + g}

    pairs = tuple(zip(sources, held))
    early = fetch_all(pairs[:EARLY], fetch, 0)
    barrier = pltpu.get_barrier_semaphore()
    for side in SIDES:
        pl.semaphore_signal(barrier, inc=1, device_id=peer_side(side), device_id_type=MESH)
    for count, peer in ((GROUP_A, peer_a), (GROUP_Y, peer_b), (Z_COUNT, peer_c)):
        for k in range(1, count):
            pl.semaphore_signal(barrier, inc=1, device_id=peer(k)[1], device_id_type=MESH)

    later = fetch_all(pairs[EARLY:], fetch, EARLY)
    used = [0]
    sent = []

    def put(src, dst, target):
        slot = used[0]
        used[0] += 1
        copy = pltpu.make_async_remote_copy(
            src_ref=src,
            dst_ref=dst,
            send_sem=send.at[slot],
            recv_sem=recv.at[slot],
            device_id=target,
            device_id_type=MESH,
        )
        copy.start()
        sent.append(copy)
        return copy

    def wait_here(copies):
        for copy in copies:
            copy.wait_recv()

    wait_all(early)
    for f in range(2):
        for o in range(12):
            for part in range(2):
                wide_c[part, pl.ds((f * 16 + o) * 16, 16), :] = cot[
                    f, o, :, part * 128 : part * 128 + 128
                ].astype(jnp.float32)
        for part in range(2):
            wide_c[part, pl.ds((f * 16 + 12) * 16, 64), :] = jnp.zeros((64, 128), jnp.float32)
        for r in range(16):
            for part in range(2):
                cot_rows[f, r, :, part * 128 : part * 128 + 128] = wide_c[
                    part, pl.ds(f * 256 + r, 16, stride=16), :
                ].astype(half)
        for part in range(2):
            block = cot_rows[f, part * 8 : part * 8 + 8].reshape(128, 256)
            packed = dot_nt(cols[...], block).astype(half)
            cot_cols[0, f, part] = packed[0:8]
            cot_cols[1, f, part] = packed[8:16]
    for f in range(2):
        wide_p[pl.ds(f * 512, 512), :] = pre[f].reshape(512, 128).astype(jnp.float32)
    packed = jnp.zeros((32, 128), jnp.float32)
    for i in range(8):
        slabs = [wide_p[pl.ds(f * 512 + i, 64, stride=8), :].astype(half) for f in range(2)]
        for f in range(2):
            pre_rows[f, i] = slabs[f]
        packed = packed + dot_nt(edge[i], jnp.concatenate(slabs, axis=0))
    pre_cols[...] = packed.astype(half).reshape(2, 16, 128)

    pl.semaphore_wait(barrier, len(SIDES) + GROUP_A + GROUP_Y + Z_COUNT - 3)

    halo = []

    def edge_put(src, dst, side):
        slot = used[0]
        used[0] += 1
        copy = pltpu.make_async_remote_copy(
            src_ref=src,
            dst_ref=dst,
            send_sem=send.at[slot],
            recv_sem=recv.at[slot],
            device_id=peer_side(side),
            device_id_type=MESH,
        )
        halo.append((side, copy))

    edge_put(cot_cols.at[0], cols_c.at[1], (0, -1))
    edge_put(pre_cols.at[0], cols_p.at[1], (0, -1))
    edge_put(cot_cols.at[1], cols_c.at[0], (0, 1))
    edge_put(pre_cols.at[1], cols_p.at[0], (0, 1))
    edge_put(cot_cols.at[0, :, 0], corners_c.at[3], (-1, -1))
    edge_put(pre_cols.at[0], cols_p.at[5], (-1, -1))
    edge_put(cot_cols.at[1, :, 0], corners_c.at[2], (-1, 1))
    edge_put(pre_cols.at[1], cols_p.at[4], (-1, 1))
    edge_put(cot_cols.at[0, :, 1], corners_c.at[1], (1, -1))
    edge_put(pre_cols.at[0], cols_p.at[3], (1, -1))
    edge_put(cot_cols.at[1, :, 1], corners_c.at[0], (1, 1))
    edge_put(pre_cols.at[1], cols_p.at[2], (1, 1))
    edge_put(cot_rows.at[:, 0:3], rows_c.at[1], (-1, 0))
    edge_put(pre_rows.at[:, 0], rows_p.at[1], (-1, 0))
    edge_put(cot_rows.at[:, 13:16], rows_c.at[0], (1, 0))
    edge_put(pre_rows.at[:, 7], rows_p.at[0], (1, 0))

    north = n > 0
    south = n < n_count - 1
    west = e > 0
    east = e < e_count - 1

    def inside(side):
        by_row = {-1: north, 0: None, 1: south}[side[0]]
        by_column = {-1: west, 0: None, 1: east}[side[1]]
        if by_row is None:
            return by_column
        if by_column is None:
            return by_row
        return jnp.logical_and(by_row, by_column)

    for way in ((0, -1), (0, 1), (-1, -1), (-1, 1), (1, -1), (1, 1), (-1, 0), (1, 0)):

        @pl.when(inside(way))
        def _(way=way):
            for side, copy in halo:
                if side == way:
                    copy.start()

    wait_all(later)

    for f in range(2):
        for i in range(8):
            center = wide_p[pl.ds(f * 512 + i, 64, stride=8), :]
            sigmoid = jax.nn.sigmoid(1.702 * center)
            slopes[f, i] = sigmoid + 1.702 * center * sigmoid * (1.0 - sigmoid)
            hidden[:, (f * 8 + i) * 128 : (f * 8 + i + 1) * 128] = (center * sigmoid).astype(half)

    token_t = dot_nt(proj_t[...], tokens[...]).astype(half)
    mask_row = mask_token[...].astype(jnp.float32).reshape(1, 768)
    mask_t = dot_nt(proj_t[...], jnp.broadcast_to(mask_row, (8, 768)).astype(half)).astype(half)
    mask_column = mask_t[:, 0:1].astype(jnp.float32)
    patch = lax.broadcasted_iota(jnp.int32, (256, 64), 0)
    slot = lax.broadcasted_iota(jnp.int32, (256, 64), 1)
    picks = []
    unseen = []
    first_in = []
    for f in range(2):
        hit = (patch == index[f : f + 1, :]) & (slot < live_counts[f])
        pick = jnp.where(hit, 1.0, 0.0).astype(half)
        picks.append(pick)
        shown = dot_nt(jnp.ones((8, 64), half), pick)
        unseen.append(1.0 - shown)
        placed = dot_nt(token_t[:, f * 64 : f * 64 + 64], pick)
        placed = placed + mask_column * unseen[f][0:1, :]
        first_in.append(placed.astype(half))
    first_grid = jnp.concatenate(first_in, axis=1)
    unseen = jnp.concatenate(unseen, axis=1)
    second_t = dot_tn(
        second[...].astype(jnp.float32).reshape(192, 64).astype(half), order[...]
    ).astype(half)

    row_second = lax.broadcasted_iota(jnp.int32, (128, 128), 0)
    lane_second = lax.broadcasted_iota(jnp.int32, (128, 128), 1)
    owner_row = jnp.concatenate([owners[0], owners[1]], axis=1)
    lane_row = lax.broadcasted_iota(jnp.int32, (1, 128), 1)
    live_row = lane_row < jnp.where(lane_row < 64, live_counts[0], live_counts[1] + 64)
    marked = jnp.where(live_row, owner_row, -1).astype(jnp.float32)
    across = jnp.broadcast_to(marked, (128, 128))
    down = across.T
    earlier = (across == down) & (row_second < lane_second)
    rank = jnp.sum(jnp.where(earlier, 1.0, 0.0), axis=0, keepdims=True)
    target = jnp.where(live_row, marked * 4.0 + rank, -1.0)
    number = lax.broadcasted_iota(jnp.int32, (96, 128), 0).astype(jnp.float32) * 2.0
    even = jnp.where(number == target, 1.0, 0.0).astype(half)
    odd = jnp.where(number + 1.0 == target, 1.0, 0.0).astype(half)

    for way in SIDES:

        @pl.when(inside((-way[0], -way[1])))
        def _(way=way):
            for side, copy in halo:
                if side == way:
                    copy.wait_recv()

    def only(condition, value):
        chosen_lanes = jnp.full(value.shape, jnp.where(condition, 1.0, 0.0), jnp.float32) > 0.5
        return jnp.where(chosen_lanes, value.astype(jnp.float32), 0.0)

    def side_cols(west_block, east_block):
        return jnp.concatenate([only(east, east_block), only(west, west_block)], axis=0).astype(half)

    wide_map = wide[...]
    narrow_map = narrow[...]
    for f in range(2):
        for part in range(2):
            value = dot_nn(cot_rows[f, part * 8 : part * 8 + 8].reshape(128, 256), wide_map)
            side = side_cols(cols_c[0, f, part], cols_c[1, f, part])
            value = value + dot_tn(side, narrow_map)
            taps[f, 3 + part * 8 : 11 + part * 8] = value.astype(half).reshape(8, 16, 1024)
        value = dot_nn(rows_c[0, f].reshape(48, 256), wide_map)
        side = side_cols(corners_c[0, f], corners_c[1, f])
        value = only(north, value + dot_tn(side, narrow_map)[80:128])
        taps[f, 0:3] = value.astype(half).reshape(3, 16, 1024)
        value = dot_nn(rows_c[1, f].reshape(48, 256), wide_map)
        side = side_cols(corners_c[2, f], corners_c[3, f])
        value = only(south, value + dot_tn(side, narrow_map)[0:48])
        taps[f, 19:22] = value.astype(half).reshape(3, 16, 1024)

    lane = lax.broadcasted_iota(jnp.int32, (64, 128), 1)
    spot = lax.broadcasted_iota(jnp.int32, (16, 128), 0)

    def side_rows(condition, upper, middle, lower):
        value = jnp.where(spot == 9, only(south, lower), middle.astype(jnp.float32))
        return only(condition, jnp.where(spot == 0, only(north, upper), value))

    side = jnp.concatenate(
        [side_rows(east, cols_p[3], cols_p[1], cols_p[5]), side_rows(west, cols_p[2], cols_p[0], cols_p[4])],
        axis=0,
    ).astype(half)
    placed = dot_tn(side, place[...])
    halo_pre = placed[0:64, 0:128] + placed[64:128, 128:256]
    halo_keep = jnp.where(
        lane == 0, jnp.where(east, 1.0, 0.0), jnp.where(lane == 127, jnp.where(west, 1.0, 0.0), 0.0)
    )
    sigmoid = jax.nn.sigmoid(1.702 * halo_pre)
    halo_slope = sigmoid + 1.702 * halo_pre * sigmoid * (1.0 - sigmoid)

    for f in range(2):
        for i in range(10):
            window = jnp.concatenate(
                [
                    taps[f, 2 * i + a, :, b * 256 : b * 256 + 256]
                    for a in range(4)
                    for b in range(4)
                ],
                axis=0,
            )
            grad = dot_nn(second_t, window)
            if 0 < i < 9:
                windows[:, (f * 8 + i - 1) * 128 : (f * 8 + i) * 128] = window[:, :128]
                slope = slopes[f, i - 1]
            else:
                center = rows_p[i // 9, f].astype(jnp.float32)
                sigmoid = jax.nn.sigmoid(1.702 * center)
                slope = sigmoid + 1.702 * center * sigmoid * (1.0 - sigmoid)
            value = grad[:, :128] * slope
            edge_slope = halo_slope
            if f + i > 0:
                edge_slope = pltpu.roll(halo_slope, 128 - 2 * (f * 10 + i), 1)
            edge_value = grad[:, 128:] * edge_slope * halo_keep
            if i == 0:
                value = only(north, value)
                edge_value = only(north, edge_value)
            if i == 9:
                value = only(south, value)
                edge_value = only(south, edge_value)
            deltas[f, i, :, 0:128] = value.astype(half)
            deltas[f, i, :, 128:256] = edge_value.astype(half)

    fine_map = fine[...]
    for f in range(2):
        for i in range(10):
            taps_fine[f, i] = dot_nn(deltas[f, i], fine_map).astype(half)
    low_lane = lane < 64
    for f in range(2):
        for pair in range(2):
            for a in range(4):
                for b in range(4):
                    low = taps_fine[f, 4 * pair + a, :, b * 128 : b * 128 + 128]
                    high = taps_fine[f, 4 * pair + 2 + a, :, b * 128 : b * 128 + 128]
                    windows_fine[
                        (a * 4 + b) * 64 : (a * 4 + b) * 64 + 64,
                        (f * 2 + pair) * 128 : (f * 2 + pair) * 128 + 128,
                    ] = jnp.where(low_lane, low, high)

    zeros_fine = jnp.zeros((64, 512), half)
    grad_first = dot_nt(windows_fine[0:512], jnp.concatenate([first_grid, zeros_fine], axis=0))
    grad_first = grad_first + dot_nt(
        windows_fine[512:1024], jnp.concatenate([zeros_fine, first_grid], axis=0)
    )
    payload[0] = grad_first.astype(half).reshape(GROUP_A, GROUP_Y, 8, 128)

    def scatter_a(s):
        copies = []
        for k in range(1, GROUP_A):
            other, target_device = peer_a(k)
            copies.append(put(payload.at[s, other], buf_a.at[s, k - 1], target_device))
        return copies

    copies_a = [scatter_a(0)]

    grid = dot_tn(first[...], windows_fine[...]).astype(half)
    chosen = jnp.concatenate(
        [dot_nn(grid[:, f * 256 : f * 256 + 256], picks[f]) for f in range(2)], axis=1
    ).astype(half)
    zeros_slot = jnp.zeros((64, 128), half)
    outgoing = dot_nt(even, jnp.concatenate([chosen, zeros_slot], axis=0))
    outgoing = outgoing + dot_nt(odd, jnp.concatenate([zeros_slot, chosen], axis=0))
    rows_out[...] = outgoing.astype(half).reshape(Z_LOW, 16, 128)
    copies_z = []
    for k in range(1, Z_LOW):
        other, target_device = peer_z(k)
        copies_z.append(put(rows_out.at[other], tok_z.at[zl], target_device))
    tok_z[zl] = rows_out[zl]

    zeros_64 = jnp.zeros((64, 2048), half)
    hidden_value = hidden[...]
    grad_second = dot_nt(windows[0:128, :], jnp.concatenate([hidden_value, zeros_64], axis=0))
    grad_second = grad_second + dot_nt(
        windows[128:256, :], jnp.concatenate([zeros_64, hidden_value], axis=0)
    )
    mask_sum = jnp.sum(grid.astype(jnp.float32) * unseen[0:1, :], axis=1, keepdims=True)
    mask_sum_row = dot_nt(unseen.astype(half), jnp.concatenate([grid, zeros_fine], axis=0))
    grad_proj = dot_nn(chosen, tokens[...]) + mask_sum * mask_row
    mask_sum_row = mask_sum_row[0:1, :]
    mask_rest = mask_sum_row - mask_sum_row.astype(half).astype(jnp.float32)
    grad_second = jnp.where(
        (row_second == 12) & (lane_second < 64),
        mask_sum_row,
        jnp.where((row_second == 13) & (lane_second < 64), mask_rest, grad_second),
    )
    payload[1, 0:2] = grad_second.astype(half).reshape(2, GROUP_Y, 8, 128)
    for part in range(6):
        block = grad_proj[:, part * 128 : part * 128 + 128].astype(half)
        payload[1, 2 + part] = block.reshape(GROUP_Y, 8, 128)
    copies_a.append(scatter_a(1))

    copies_b = []
    for s in range(STREAMS):
        wait_here(copies_a[s])
        summed = payload[s, g].astype(jnp.float32)
        for k in range(1, GROUP_A):
            summed = summed + buf_a[s, k - 1].astype(jnp.float32)
        red_a[s] = summed
        copies = []
        for k in range(1, GROUP_Y):
            other, target_device = peer_b(k)
            copies.append(put(red_a.at[s, other], buf_b.at[s, k - 1], target_device))
        copies_b.append(copies)

    wait_here(copies_z)
    stacked = tok_z[...].reshape(Z_LOW * 16, 128)
    picked = lax.broadcasted_iota(jnp.int32, (GROUP_A * 16, Z_LOW * 16), 0)
    column = lax.broadcasted_iota(jnp.int32, (GROUP_A * 16, Z_LOW * 16), 1)
    wanted = ((picked % 16) // 2) * 16 + (picked // 16) * 2 + picked % 2
    choose = jnp.where(column == wanted, 1.0, 0.0).astype(half)
    tok_s[...] = dot_nn(choose, stacked).astype(half).reshape(GROUP_A, 16, 128)
    copies_t = []
    for k in range(1, GROUP_A):
        other, target_device = peer_a(k)
        copies_t.append(put(tok_s.at[other], buf_s.at[g], target_device))
    buf_s[g] = tok_s[g]

    copies_c = []
    for s in range(STREAMS):
        wait_here(copies_b[s])
        summed = red_a[s, y]
        for k in range(1, GROUP_Y):
            summed = summed + buf_b[s, k - 1]
        buf_c[s, zi] = summed
        copies = []
        for k in range(1, Z_COUNT):
            copies.append(put(buf_c.at[s, zi], buf_c.at[s, zi], peer_c(k)[1]))
        copies_c.append(copies)

    row_8 = lax.broadcasted_iota(jnp.int32, (8, 128), 0)
    copies_d = []
    for s in range(STREAMS):
        wait_here(copies_c[s])
        summed = buf_c[s, 0]
        for k in range(1, Z_COUNT):
            summed = summed + buf_c[s, k]
        if s == 1:
            mask_total = summed[4:5] + summed[5:6]
            rest = mask_total - mask_total.astype(half).astype(jnp.float32)
            here = jnp.where((g == 0) & (y == 1), 4, -2)
            summed = jnp.where(row_8 == here, mask_total, summed)
            summed = jnp.where(row_8 == here + 1, rest, summed)
        buf_d[s, y] = summed.astype(half)
        copies = []
        for k in range(1, GROUP_Y):
            copies.append(put(buf_d.at[s, y], buf_d.at[s, y], peer_b(k)[1]))
        copies_d.append(copies)

    copies_e = []
    own = []
    for s in range(STREAMS):
        wait_here(copies_d[s])
        for k in range(1, GROUP_A):
            copies_e.append(put(buf_d.at[s], total_out.at[s, g], peer_a(k)[1]))
        copy = pltpu.make_async_copy(buf_d.at[s], total_out.at[s, g], local_sem.at[s])
        copy.start()
        own.append(copy)
    wait_here(copies_t)
    rows_in[...] = buf_s[...]
    wait_here(copies_e)
    wait_all(own)
    for copy in sent:
        copy.wait_send()
    for way in SIDES:

        @pl.when(inside(way))
        def _(way=way):
            for side, copy in halo:
                if side == way:
                    copy.wait_send()


COPIES = 16 + 2 * (2 * (GROUP_A - 1) + 2 * (GROUP_Y - 1) + Z_COUNT - 1) + Z_LOW - 1 + GROUP_A - 1


def main(arrays):
    vmem = pl.BlockSpec(memory_space=pltpu.VMEM)
    hbm = pl.BlockSpec(memory_space=pl.ANY)
    half = jnp.bfloat16
    wide = jnp.float32
    dma = pltpu.SemaphoreType.DMA
    return pl.pallas_call(
        main_kernel,
        out_shape=(
            jax.ShapeDtypeStruct((STREAMS, GROUP_A, GROUP_Y, 8, 128), half),
            jax.ShapeDtypeStruct((GROUP_A, 16, 128), half),
        ),
        in_specs=[pl.BlockSpec(memory_space=pltpu.HBM)] * len(arrays),
        out_specs=(hbm, vmem),
        scratch_shapes=[
            (pltpu.SMEM if x.ndim == 1 and x.dtype == jnp.int32 else pltpu.VMEM)(x.shape, x.dtype)
            for x in arrays
        ]
        + [
            pltpu.VMEM((2, 512, 128), wide),
            pltpu.VMEM((1024, 128), wide),
            pltpu.VMEM((2, 16, 16, 256), half),
            pltpu.VMEM((2, 2, 2, 8, 128), half),
            pltpu.VMEM((2, 8, 64, 128), half),
            pltpu.VMEM((2, 16, 128), half),
            pltpu.VMEM((2, 2, 3, 16, 256), half),
            pltpu.VMEM((2, 2, 64, 128), half),
            pltpu.VMEM((2, 2, 2, 8, 128), half),
            pltpu.VMEM((4, 2, 8, 128), half),
            pltpu.VMEM((6, 16, 128), half),
            pltpu.VMEM((2, 8, 64, 128), wide),
            pltpu.VMEM((2, 22, 16, 1024), half),
            pltpu.VMEM((256, 2048), half),
            pltpu.VMEM((64, 2048), half),
            pltpu.VMEM((2, 10, 64, 256), half),
            pltpu.VMEM((2, 10, 64, 512), half),
            pltpu.VMEM((1024, 512), half),
            pltpu.VMEM((STREAMS, GROUP_A, GROUP_Y, 8, 128), half),
            pltpu.VMEM((STREAMS, GROUP_A - 1, GROUP_Y, 8, 128), half),
            pltpu.VMEM((STREAMS, GROUP_Y, 8, 128), wide),
            pltpu.VMEM((STREAMS, GROUP_Y - 1, 8, 128), wide),
            pltpu.VMEM((STREAMS, Z_COUNT, 8, 128), wide),
            pltpu.VMEM((STREAMS, GROUP_Y, 8, 128), half),
            pltpu.VMEM((Z_LOW, 16, 128), half),
            pltpu.VMEM((Z_LOW, 16, 128), half),
            pltpu.VMEM((GROUP_A, 16, 128), half),
            pltpu.VMEM((GROUP_A, 16, 128), half),
            dma((COPIES,)),
            dma((COPIES,)),
            dma((STREAMS,)),
            dma((len(arrays),)),
        ],
        compiler_params=pltpu.CompilerParams(
            collective_id=0, has_side_effects=True, vmem_limit_bytes=MAIN_VMEM
        ),
        name="main",
    )(*[pltpu.with_memory_space_constraint(x, pltpu.HBM) for x in arrays])


def finish_kernel(
    total, rows_in, proj_t, token_grad, grad_proj, grad_first, grad_second, grad_mask
):
    half = jnp.bfloat16
    row = lax.broadcasted_iota(jnp.int32, (192, 128), 0)
    column = lax.broadcasted_iota(jnp.int32, (192, 128), 1)
    tile = lax.div(row, 4)
    source = lax.rem(tile, 8) * 16 + lax.div(tile, 8) * 2 + lax.div(lax.rem(row, 4), 2)
    choose = jnp.where(column == source, 1.0, 0.0).astype(half)
    arrived = dot_nn(choose, rows_in[...].reshape(128, 128))
    arrived = jnp.where(lax.div(column, 64) == lax.rem(row, 2), arrived, 0.0).astype(half)
    double = jnp.concatenate([proj_t[...], proj_t[...]], axis=0)
    token_grad[...] = dot_nn(arrived, double).astype(half)
    packed = total[0].astype(jnp.float32).reshape(512, 128)
    grad_first[0:512] = packed[:, 0:64]
    grad_first[512:1024] = packed[:, 64:128]
    other = total[1].astype(jnp.float32).reshape(512, 128)
    for k in range(16):
        lanes = 64 * (k // 8)
        start = (k % 8) * 16
        grad_second[k // 4, :, k % 4, :] = other[start : start + 12, lanes : lanes + 64]
    for part in range(6):
        grad_proj[:, part * 128 : part * 128 + 128] = other[128 + part * 64 : 192 + part * 64]
    mask_row = other[12:13, 0:64] + other[13:14, 0:64]
    grad_mask[...] = jnp.dot(
        jnp.broadcast_to(mask_row, (8, 64)),
        proj_t[...].astype(jnp.float32),
        precision=lax.Precision.HIGHEST,
        preferred_element_type=jnp.float32,
    )[0:1].reshape(768)


def finish(total, rows_in, proj_t):
    vmem = pl.BlockSpec(memory_space=pltpu.VMEM)
    return pl.pallas_call(
        finish_kernel,
        out_shape=(
            jax.ShapeDtypeStruct((192, 768), jnp.bfloat16),
            jax.ShapeDtypeStruct((64, 768), jnp.float32),
            jax.ShapeDtypeStruct((1024, 64), jnp.float32),
            jax.ShapeDtypeStruct((4, 12, 4, 64), jnp.float32),
            jax.ShapeDtypeStruct((768,), jnp.float32),
        ),
        in_specs=[vmem] * 3,
        out_specs=(vmem,) * 5,
        compiler_params=pltpu.CompilerParams(vmem_limit_bytes=FINISH_VMEM),
        name="finish",
    )(total, rows_in, proj_t)


def per_device(
    tokens,
    vis_index,
    counts,
    owners,
    mask_token,
    proj_weight,
    up_first,
    up_second,
    saved_pre,
    cotangent,
):
    wide, narrow, fine, edge, place, cols, order = tap_select()
    proj_t = proj_weight.T
    total, rows_in = main(
        [
            cotangent,
            cols,
            saved_pre,
            edge,
            counts.reshape(2),
            vis_index.reshape(2, 64),
            owners.reshape(2, 1, 64),
            tokens.reshape(128, 768),
            mask_token,
            proj_t,
            up_first.reshape(1024, 64),
            up_second.transpose(0, 2, 1, 3),
            wide,
            narrow,
            fine,
            order,
            place,
        ],
    )
    token_grad, grad_proj, grad_first, grad_second, grad_mask = finish(total, rows_in, proj_t)
    return (
        token_grad[None, None],
        grad_proj.T,
        grad_first.reshape(4, 4, 64, 64),
        grad_second.transpose(0, 2, 1, 3),
        grad_mask,
    )


def solution(mesh):
    return jax.shard_map(
        per_device,
        mesh=mesh,
        in_specs=(
            P("ns", "ew", None, None, None),
            P("ns", "ew", None, None),
            P("ns", "ew", None),
            P("ns", "ew", None, None, None),
            P(),
            P(),
            P(),
            P(),
            P(None, None, "ns", "ew"),
            P(None, None, "ns", "ew"),
        ),
        out_specs=(P("ns", "ew", None, None), P(), P(), P(), P()),
        check_vma=False,
    )
```

```python
import jax
import jax.numpy as jnp
import numpy as np
from jax import lax
from jax.experimental import pallas as pl
from jax.experimental.pallas import tpu as pltpu
from jax.sharding import PartitionSpec as P

MESH = pl.DeviceIdType.MESH
GROUP_A = 8
GROUP_Y = 8
Z_LOW = 6
Z_HIGH = 2


BANDS_PAD = 16
LANES = 128


def tap_select():
    wide = np.zeros((256, 4, 256), np.float32)
    halo = np.zeros((2, 16, 4, 256), np.float32)
    for tap in range(4):
        for lane, cell in [(j, j) for j in range(128)] + [(128, 128), (255, -1)]:
            col = 2 * cell + tap - 1
            if col < 0:
                for frame in range(2):
                    halo[frame, 8 + frame * 3 + col + 3, tap, lane] = 1
            elif col < 256:
                wide[col, tap, lane] = 1
            else:
                for frame in range(2):
                    halo[frame, frame * 3 + col - 256, tap, lane] = 1
    fine = np.zeros((256, 4, 2, 64), np.float32)
    for tap in range(4):
        for cell in range(64):
            col = 2 * cell + tap - 1
            fine[col if col >= 0 else 255, tap, :, cell] = 1
    edge = np.zeros((8, 2, 16, 128), np.float32)
    place = np.zeros((2, 16, 2, 128), np.float32)
    for row in range(8):
        for line in [row] + ([8] if row == 7 else []) + ([9] if row == 0 else []):
            edge[row, 0, line, 0] = 1
            edge[row, 1, line, 127] = 1
    for frame in range(2):
        for spot in range(10):
            pair = 2 * (frame * 10 + spot)
            line = {0: 8, 9: 9}.get(spot, spot - 1)
            place[0, line, frame, pair] = 1
            place[1, line, frame, (pair - 1) % 128] = 1
    cols = np.zeros((2, 16, 256), np.float32)
    for frame in range(2):
        for k in range(3):
            cols[frame, frame * 3 + k, k] = 1
            cols[frame, 8 + frame * 3 + k, 253 + k] = 1
    order = np.zeros((4, 12, 4, 4, 4, 16), np.float32)
    for a in range(4):
        for o in range(12):
            for b in range(4):
                order[a, o, b, a, b, o] = 1
    half = jnp.bfloat16
    return (
        jnp.asarray(wide.reshape(256, 1024), half),
        jnp.asarray(halo.reshape(2, 16, 1024), half),
        jnp.asarray(fine.reshape(256, 512), half),
        jnp.asarray(edge.reshape(8, 32, 128), half),
        jnp.asarray(place.reshape(32, 256), half),
        jnp.asarray(cols, half),
        jnp.asarray(order.reshape(192, 256), half),
    )


def dot_nn(a, b):
    return jnp.dot(a, b, preferred_element_type=jnp.float32)


def dot_nt(a, b):
    return lax.dot_general(a, b, (((1,), (1,)), ((), ())), preferred_element_type=jnp.float32)


def dot_tn(a, b):
    return lax.dot_general(a, b, (((0,), (0,)), ((), ())), preferred_element_type=jnp.float32)


SIDES = ((-1, 0), (1, 0), (0, -1), (0, 1), (-1, -1), (-1, 1), (1, -1), (1, 1))
STREAMS = 2
Z_COUNT = Z_LOW * Z_HIGH


def fetch_all(pairs, sem, first):
    copies = []
    for k, (src, dst) in enumerate(pairs):
        copy = pltpu.make_async_copy(src, dst, sem.at[first + k])
        copy.start()
        copies.append(copy)
    return copies


def wait_all(copies):
    for copy in copies:
        copy.wait()


EARLY = 4
MAIN_VMEM = 24 * 1024 * 1024
FINISH_VMEM = 8 * 1024 * 1024
OPERANDS = tuple(range(17))


def main_kernel(*refs):
    sources = refs[: len(OPERANDS)]
    (total_out, rows_in) = refs[len(OPERANDS) : len(OPERANDS) + 2]
    held = refs[len(OPERANDS) + 2 : 2 * len(OPERANDS) + 2]
    (
        cot,
        cols,
        pre,
        edge,
        live_counts,
        index,
        owners,
        tokens,
        mask_token,
        proj_t,
        first,
        second,
        wide,
        narrow,
        fine,
        order,
        place,
    ) = held
    (
        wide_c,
        wide_p,
        cot_rows,
        packs,
        pre_rows,
        rows_c,
        rows_p,
        cols_c,
        corners,
        slopes,
        taps,
        windows,
        hidden,
        deltas,
        taps_fine,
        windows_fine,
        payload,
        buf_a,
        red_a,
        buf_b,
        buf_c,
        buf_d,
        rows_out,
        tok_z,
        tok_s,
        buf_s,
        send,
        recv,
        local_sem,
        fetch,
    ) = refs[2 * len(OPERANDS) + 2 :]
    half = jnp.bfloat16
    n = lax.axis_index("ns")
    e = lax.axis_index("ew")
    n_count = lax.axis_size("ns")
    e_count = lax.axis_size("ew")
    g = lax.rem(n, GROUP_A)
    zl = lax.div(n, GROUP_A)
    zh = lax.div(e, GROUP_Y)
    y = lax.rem(e, GROUP_Y)
    zi = zh * Z_LOW + zl

    def peer_side(side):
        return {
            "ew": lax.rem(e + side[1] + e_count, e_count),
            "ns": lax.rem(n + side[0] + n_count, n_count),
        }

    def peer_a(k):
        other = lax.rem(g + k, GROUP_A)
        return other, {"ew": e, "ns": zl * GROUP_A + other}

    def peer_b(k):
        other = lax.rem(y + k, GROUP_Y)
        return other, {"ew": zh * GROUP_Y + other, "ns": n}

    def peer_c(k):
        other = lax.rem(zi + k, Z_COUNT)
        return other, {
            "ew": lax.div(other, Z_LOW) * GROUP_Y + y,
            "ns": lax.rem(other, Z_LOW) * GROUP_A + g,
        }

    def peer_z(k):
        other = lax.rem(zl + k, Z_LOW)
        return other, {"ew": e, "ns": other * GROUP_A + g}

    pairs = tuple(zip(sources, held))
    early = fetch_all(pairs[:EARLY], fetch, 0)
    barrier = pltpu.get_barrier_semaphore()
    for k in (6, 5, 7, 4, 8, 3, 9, 2, 10, 1, 11):
        pl.semaphore_signal(barrier, inc=1, device_id=peer_c(k)[1], device_id_type=MESH)
    for side in reversed(SIDES):
        pl.semaphore_signal(barrier, inc=1, device_id=peer_side(side), device_id_type=MESH)
    for count, peer in ((GROUP_Y, peer_b), (GROUP_A, peer_a)):
        for k in range(1, count):
            pl.semaphore_signal(barrier, inc=1, device_id=peer(k)[1], device_id_type=MESH)

    later = fetch_all(pairs[EARLY:], fetch, EARLY)
    used = [0]
    sent = []

    def put(src, dst, target):
        slot = used[0]
        used[0] += 1
        copy = pltpu.make_async_remote_copy(
            src_ref=src,
            dst_ref=dst,
            send_sem=send.at[slot],
            recv_sem=recv.at[slot],
            device_id=target,
            device_id_type=MESH,
        )
        copy.start()
        sent.append(copy)
        return copy

    def wait_here(copies):
        for copy in copies:
            copy.wait_recv()

    wait_all(early)
    for f in range(2):
        for o in range(12):
            for part in range(2):
                wide_c[part, pl.ds((f * 16 + o) * 16, 16), :] = cot[
                    f, o, :, part * 128 : part * 128 + 128
                ].astype(jnp.float32)
        for part in range(2):
            wide_c[part, pl.ds((f * 16 + 12) * 16, 64), :] = jnp.zeros((64, 128), jnp.float32)
        for r in range(16):
            for part in range(2):
                cot_rows[f, r, :, part * 128 : part * 128 + 128] = wide_c[
                    part, pl.ds(f * 256 + r, 16, stride=16), :
                ].astype(half)
    for part in range(2):
        packed = jnp.zeros((16, 128), jnp.float32)
        for f in range(2):
            block = cot_rows[f, part * 8 : part * 8 + 8].reshape(128, 256)
            packed = packed + dot_nt(cols[f], block)
        for side in range(2):
            packs[side, 1 + 2 * part] = packed[side * 8 : side * 8 + 8].astype(half)
    for f in range(2):
        wide_p[pl.ds(f * 512, 512), :] = pre[f].reshape(512, 128).astype(jnp.float32)
    packed = jnp.zeros((32, 128), jnp.float32)
    for i in range(8):
        slabs = [wide_p[pl.ds(f * 512 + i, 64, stride=8), :].astype(half) for f in range(2)]
        for f in range(2):
            pre_rows[f, i] = slabs[f]
        packed = packed + dot_nt(edge[i], jnp.concatenate(slabs, axis=0))
    for side in range(2):
        packs[side, 2] = packed[side * 16 : side * 16 + 8].astype(half)
        corner = packed[side * 16 + 8 : side * 16 + 16].astype(half)
        packs[side, 0] = corner
        packs[side, 4] = corner

    pl.semaphore_wait(barrier, len(SIDES) + GROUP_A + GROUP_Y + Z_COUNT - 3)

    halo = []

    def edge_put(src, dst, side):
        slot = used[0]
        used[0] += 1
        copy = pltpu.make_async_remote_copy(
            src_ref=src,
            dst_ref=dst,
            send_sem=send.at[slot],
            recv_sem=recv.at[slot],
            device_id=peer_side(side),
            device_id_type=MESH,
        )
        halo.append((side, copy))

    edge_put(packs.at[0, 1:4], cols_c.at[1], (0, -1))
    edge_put(packs.at[1, 1:4], cols_c.at[0], (0, 1))
    edge_put(packs.at[0, 0:2], corners.at[3], (-1, -1))
    edge_put(packs.at[1, 0:2], corners.at[2], (-1, 1))
    edge_put(packs.at[0, 3:5], corners.at[1], (1, -1))
    edge_put(packs.at[1, 3:5], corners.at[0], (1, 1))
    edge_put(cot_rows.at[:, 0:3], rows_c.at[1], (-1, 0))
    edge_put(pre_rows.at[:, 0], rows_p.at[1], (-1, 0))
    edge_put(cot_rows.at[:, 13:16], rows_c.at[0], (1, 0))
    edge_put(pre_rows.at[:, 7], rows_p.at[0], (1, 0))

    north = n > 0
    south = n < n_count - 1
    west = e > 0
    east = e < e_count - 1

    def inside(side):
        by_row = {-1: north, 0: None, 1: south}[side[0]]
        by_column = {-1: west, 0: None, 1: east}[side[1]]
        if by_row is None:
            return by_column
        if by_column is None:
            return by_row
        return jnp.logical_and(by_row, by_column)

    for way in ((0, -1), (0, 1), (-1, -1), (-1, 1), (1, -1), (1, 1), (-1, 0), (1, 0)):

        @pl.when(inside(way))
        def _(way=way):
            for side, copy in halo:
                if side == way:
                    copy.start()

    wait_all(later)

    for f in range(2):
        for i in range(8):
            center = wide_p[pl.ds(f * 512 + i, 64, stride=8), :]
            sigmoid = jax.nn.sigmoid(1.702 * center)
            slopes[f, i] = sigmoid + 1.702 * center * sigmoid * (1.0 - sigmoid)
            hidden[:, (f * 8 + i) * 128 : (f * 8 + i + 1) * 128] = (center * sigmoid).astype(half)

    token_t = dot_nt(proj_t[...], tokens[...]).astype(half)
    mask_row = mask_token[...].astype(jnp.float32).reshape(1, 768)
    mask_t = dot_nt(proj_t[...], jnp.broadcast_to(mask_row, (8, 768)).astype(half)).astype(half)
    mask_column = mask_t[:, 0:1].astype(jnp.float32)
    patch = lax.broadcasted_iota(jnp.int32, (256, 64), 0)
    slot = lax.broadcasted_iota(jnp.int32, (256, 64), 1)
    picks = []
    unseen = []
    first_in = []
    for f in range(2):
        hit = (patch == index[f : f + 1, :]) & (slot < live_counts[f])
        pick = jnp.where(hit, 1.0, 0.0).astype(half)
        picks.append(pick)
        shown = dot_nt(jnp.ones((8, 64), half), pick)
        unseen.append(1.0 - shown)
        placed = dot_nt(token_t[:, f * 64 : f * 64 + 64], pick)
        placed = placed + mask_column * unseen[f][0:1, :]
        first_in.append(placed.astype(half))
    first_grid = jnp.concatenate(first_in, axis=1)
    unseen = jnp.concatenate(unseen, axis=1)
    second_t = dot_tn(
        second[...].astype(jnp.float32).reshape(192, 64).astype(half), order[...]
    ).astype(half)

    row_second = lax.broadcasted_iota(jnp.int32, (128, 128), 0)
    lane_second = lax.broadcasted_iota(jnp.int32, (128, 128), 1)
    owner_row = jnp.concatenate([owners[0], owners[1]], axis=1)
    lane_row = lax.broadcasted_iota(jnp.int32, (1, 128), 1)
    live_row = lane_row < jnp.where(lane_row < 64, live_counts[0], live_counts[1] + 64)
    marked = jnp.where(live_row, owner_row, -1).astype(jnp.float32)
    across = jnp.broadcast_to(marked, (128, 128))
    down = across.T
    earlier = (across == down) & (row_second < lane_second)
    rank = jnp.sum(jnp.where(earlier, 1.0, 0.0), axis=0, keepdims=True)
    target = jnp.where(live_row, marked * 4.0 + rank, -1.0)
    number = lax.broadcasted_iota(jnp.int32, (96, 128), 0).astype(jnp.float32) * 2.0
    even = jnp.where(number == target, 1.0, 0.0).astype(half)
    odd = jnp.where(number + 1.0 == target, 1.0, 0.0).astype(half)

    for way in SIDES:

        @pl.when(inside((-way[0], -way[1])))
        def _(way=way):
            for side, copy in halo:
                if side == way:
                    copy.wait_recv()

    def only(condition, value):
        chosen_lanes = jnp.full(value.shape, jnp.where(condition, 1.0, 0.0), jnp.float32) > 0.5
        return jnp.where(chosen_lanes, value.astype(jnp.float32), 0.0)

    def side_cols(west_block, east_block):
        return jnp.concatenate([only(east, east_block), only(west, west_block)], axis=0).astype(half)

    wide_map = wide[...]
    for f in range(2):
        narrow_map = narrow[f]
        for part in range(2):
            value = dot_nn(cot_rows[f, part * 8 : part * 8 + 8].reshape(128, 256), wide_map)
            side = side_cols(cols_c[0, 2 * part], cols_c[1, 2 * part])
            value = value + dot_tn(side, narrow_map)
            taps[f, 3 + part * 8 : 11 + part * 8] = value.astype(half).reshape(8, 16, 1024)
        value = dot_nn(rows_c[0, f].reshape(48, 256), wide_map)
        side = side_cols(corners[0, 0], corners[1, 0])
        value = only(north, value + dot_tn(side, narrow_map)[80:128])
        taps[f, 0:3] = value.astype(half).reshape(3, 16, 1024)
        value = dot_nn(rows_c[1, f].reshape(48, 256), wide_map)
        side = side_cols(corners[2, 1], corners[3, 1])
        value = only(south, value + dot_tn(side, narrow_map)[0:48])
        taps[f, 19:22] = value.astype(half).reshape(3, 16, 1024)

    lane = lax.broadcasted_iota(jnp.int32, (64, 128), 1)
    line = lax.broadcasted_iota(jnp.int32, (8, 128), 0)

    def side_rows(condition, upper, middle, lower):
        corner = jnp.where(line == 0, only(north, upper), 0.0)
        corner = jnp.where(line == 1, only(south, lower), corner)
        return [only(condition, middle), only(condition, corner)]

    side = jnp.concatenate(
        side_rows(east, corners[1, 1], cols_c[1, 1], corners[3, 0])
        + side_rows(west, corners[0, 1], cols_c[0, 1], corners[2, 0]),
        axis=0,
    ).astype(half)
    placed = dot_tn(side, place[...])
    halo_pre = placed[0:64, 0:128] + placed[64:128, 128:256]
    halo_keep = jnp.where(
        lane == 0, jnp.where(east, 1.0, 0.0), jnp.where(lane == 127, jnp.where(west, 1.0, 0.0), 0.0)
    )
    sigmoid = jax.nn.sigmoid(1.702 * halo_pre)
    halo_slope = sigmoid + 1.702 * halo_pre * sigmoid * (1.0 - sigmoid)

    for f in range(2):
        for i in range(10):
            window = jnp.concatenate(
                [
                    taps[f, 2 * i + a, :, b * 256 : b * 256 + 256]
                    for a in range(4)
                    for b in range(4)
                ],
                axis=0,
            )
            grad = dot_nn(second_t, window)
            if 0 < i < 9:
                windows[:, (f * 8 + i - 1) * 128 : (f * 8 + i) * 128] = window[:, :128]
                slope = slopes[f, i - 1]
            else:
                center = rows_p[i // 9, f].astype(jnp.float32)
                sigmoid = jax.nn.sigmoid(1.702 * center)
                slope = sigmoid + 1.702 * center * sigmoid * (1.0 - sigmoid)
            value = grad[:, :128] * slope
            edge_slope = halo_slope
            if f + i > 0:
                edge_slope = pltpu.roll(halo_slope, 128 - 2 * (f * 10 + i), 1)
            edge_value = grad[:, 128:] * edge_slope * halo_keep
            if i == 0:
                value = only(north, value)
                edge_value = only(north, edge_value)
            if i == 9:
                value = only(south, value)
                edge_value = only(south, edge_value)
            deltas[f, i, :, 0:128] = value.astype(half)
            deltas[f, i, :, 128:256] = edge_value.astype(half)

    fine_map = fine[...]
    for f in range(2):
        for i in range(10):
            taps_fine[f, i] = dot_nn(deltas[f, i], fine_map).astype(half)
    low_lane = lane < 64
    for f in range(2):
        for pair in range(2):
            for a in range(4):
                for b in range(4):
                    low = taps_fine[f, 4 * pair + a, :, b * 128 : b * 128 + 128]
                    high = taps_fine[f, 4 * pair + 2 + a, :, b * 128 : b * 128 + 128]
                    windows_fine[
                        (a * 4 + b) * 64 : (a * 4 + b) * 64 + 64,
                        (f * 2 + pair) * 128 : (f * 2 + pair) * 128 + 128,
                    ] = jnp.where(low_lane, low, high)

    zeros_fine = jnp.zeros((64, 512), half)
    grad_first = dot_nt(windows_fine[0:512], jnp.concatenate([first_grid, zeros_fine], axis=0))
    grad_first = grad_first + dot_nt(
        windows_fine[512:1024], jnp.concatenate([zeros_fine, first_grid], axis=0)
    )
    payload[0] = grad_first.astype(half).reshape(GROUP_A, GROUP_Y, 8, 128)

    def scatter_a(s):
        copies = []
        for k in range(1, GROUP_A):
            other, target_device = peer_a(k)
            copies.append(put(payload.at[s, other], buf_a.at[s, k - 1], target_device))
        return copies

    copies_a = [scatter_a(0)]

    grid = dot_tn(first[...], windows_fine[...]).astype(half)
    chosen = jnp.concatenate(
        [dot_nn(grid[:, f * 256 : f * 256 + 256], picks[f]) for f in range(2)], axis=1
    ).astype(half)
    zeros_slot = jnp.zeros((64, 128), half)
    outgoing = dot_nt(even, jnp.concatenate([chosen, zeros_slot], axis=0))
    outgoing = outgoing + dot_nt(odd, jnp.concatenate([zeros_slot, chosen], axis=0))
    rows_out[...] = outgoing.astype(half).reshape(Z_LOW, 16, 128)
    copies_z = []
    for k in range(1, Z_LOW):
        other, target_device = peer_z(k)
        copies_z.append(put(rows_out.at[other], tok_z.at[zl], target_device))
    tok_z[zl] = rows_out[zl]

    zeros_64 = jnp.zeros((64, 2048), half)
    hidden_value = hidden[...]
    grad_second = dot_nt(windows[0:128, :], jnp.concatenate([hidden_value, zeros_64], axis=0))
    grad_second = grad_second + dot_nt(
        windows[128:256, :], jnp.concatenate([zeros_64, hidden_value], axis=0)
    )
    mask_sum = jnp.sum(grid.astype(jnp.float32) * unseen[0:1, :], axis=1, keepdims=True)
    mask_sum_row = dot_nt(unseen.astype(half), jnp.concatenate([grid, zeros_fine], axis=0))
    grad_proj = dot_nn(chosen, tokens[...]) + mask_sum * mask_row
    mask_sum_row = mask_sum_row[0:1, :]
    mask_rest = mask_sum_row - mask_sum_row.astype(half).astype(jnp.float32)
    grad_second = jnp.where(
        (row_second == 12) & (lane_second < 64),
        mask_sum_row,
        jnp.where((row_second == 13) & (lane_second < 64), mask_rest, grad_second),
    )
    payload[1, 0:2] = grad_second.astype(half).reshape(2, GROUP_Y, 8, 128)
    for part in range(6):
        block = grad_proj[:, part * 128 : part * 128 + 128].astype(half)
        payload[1, 2 + part] = block.reshape(GROUP_Y, 8, 128)
    copies_a.append(scatter_a(1))

    copies_b = []
    for s in range(STREAMS):
        wait_here(copies_a[s])
        summed = payload[s, g].astype(jnp.float32)
        for k in range(1, GROUP_A):
            summed = summed + buf_a[s, k - 1].astype(jnp.float32)
        red_a[s] = summed
        copies = []
        for k in range(1, GROUP_Y):
            other, target_device = peer_b(k)
            copies.append(put(red_a.at[s, other], buf_b.at[s, k - 1], target_device))
        copies_b.append(copies)

    wait_here(copies_z)
    stacked = tok_z[...].reshape(Z_LOW * 16, 128)
    picked = lax.broadcasted_iota(jnp.int32, (GROUP_A * 16, Z_LOW * 16), 0)
    column = lax.broadcasted_iota(jnp.int32, (GROUP_A * 16, Z_LOW * 16), 1)
    wanted = ((picked % 16) // 2) * 16 + (picked // 16) * 2 + picked % 2
    choose = jnp.where(column == wanted, 1.0, 0.0).astype(half)
    tok_s[...] = dot_nn(choose, stacked).astype(half).reshape(GROUP_A, 16, 128)
    copies_t = []
    for k in range(1, GROUP_A):
        other, target_device = peer_a(k)
        copies_t.append(put(tok_s.at[other], buf_s.at[g], target_device))
    buf_s[g] = tok_s[g]

    copies_c = []
    for s in range(STREAMS):
        wait_here(copies_b[s])
        summed = red_a[s, y]
        for k in range(1, GROUP_Y):
            summed = summed + buf_b[s, k - 1]
        buf_c[s, zi] = summed
        copies = []
        for k in range(1, Z_COUNT):
            copies.append(put(buf_c.at[s, zi], buf_c.at[s, zi], peer_c(k)[1]))
        copies_c.append(copies)

    row_8 = lax.broadcasted_iota(jnp.int32, (8, 128), 0)
    copies_d = []
    for s in range(STREAMS):
        wait_here(copies_c[s])
        summed = buf_c[s, 0]
        for k in range(1, Z_COUNT):
            summed = summed + buf_c[s, k]
        if s == 1:
            mask_total = summed[4:5] + summed[5:6]
            rest = mask_total - mask_total.astype(half).astype(jnp.float32)
            here = jnp.where((g == 0) & (y == 1), 4, -2)
            summed = jnp.where(row_8 == here, mask_total, summed)
            summed = jnp.where(row_8 == here + 1, rest, summed)
        buf_d[s, y] = summed.astype(half)
        copies = []
        for k in range(1, GROUP_Y):
            copies.append(put(buf_d.at[s, y], buf_d.at[s, y], peer_b(k)[1]))
        copies_d.append(copies)

    copies_e = []
    own = []
    for s in range(STREAMS):
        wait_here(copies_d[s])
        for k in range(1, GROUP_A):
            copies_e.append(put(buf_d.at[s], total_out.at[s, g], peer_a(k)[1]))
        copy = pltpu.make_async_copy(buf_d.at[s], total_out.at[s, g], local_sem.at[s])
        copy.start()
        own.append(copy)
    wait_here(copies_t)
    rows_in[...] = buf_s[...]
    wait_here(copies_e)
    wait_all(own)
    for copy in sent:
        copy.wait_send()
    for way in SIDES:

        @pl.when(inside(way))
        def _(way=way):
            for side, copy in halo:
                if side == way:
                    copy.wait_send()


COPIES = 10 + 2 * (2 * (GROUP_A - 1) + 2 * (GROUP_Y - 1) + Z_COUNT - 1) + Z_LOW - 1 + GROUP_A - 1


def main(arrays):
    vmem = pl.BlockSpec(memory_space=pltpu.VMEM)
    hbm = pl.BlockSpec(memory_space=pl.ANY)
    half = jnp.bfloat16
    wide = jnp.float32
    dma = pltpu.SemaphoreType.DMA
    return pl.pallas_call(
        main_kernel,
        out_shape=(
            jax.ShapeDtypeStruct((STREAMS, GROUP_A, GROUP_Y, 8, 128), half),
            jax.ShapeDtypeStruct((GROUP_A, 16, 128), half),
        ),
        in_specs=[pl.BlockSpec(memory_space=pltpu.HBM)] * len(arrays),
        out_specs=(hbm, vmem),
        scratch_shapes=[
            (pltpu.SMEM if x.ndim == 1 and x.dtype == jnp.int32 else pltpu.VMEM)(x.shape, x.dtype)
            for x in arrays
        ]
        + [
            pltpu.VMEM((2, 512, 128), wide),
            pltpu.VMEM((1024, 128), wide),
            pltpu.VMEM((2, 16, 16, 256), half),
            pltpu.VMEM((2, 5, 8, 128), half),
            pltpu.VMEM((2, 8, 64, 128), half),
            pltpu.VMEM((2, 2, 3, 16, 256), half),
            pltpu.VMEM((2, 2, 64, 128), half),
            pltpu.VMEM((2, 3, 8, 128), half),
            pltpu.VMEM((4, 2, 8, 128), half),
            pltpu.VMEM((2, 8, 64, 128), wide),
            pltpu.VMEM((2, 22, 16, 1024), half),
            pltpu.VMEM((256, 2048), half),
            pltpu.VMEM((64, 2048), half),
            pltpu.VMEM((2, 10, 64, 256), half),
            pltpu.VMEM((2, 10, 64, 512), half),
            pltpu.VMEM((1024, 512), half),
            pltpu.VMEM((STREAMS, GROUP_A, GROUP_Y, 8, 128), half),
            pltpu.VMEM((STREAMS, GROUP_A - 1, GROUP_Y, 8, 128), half),
            pltpu.VMEM((STREAMS, GROUP_Y, 8, 128), wide),
            pltpu.VMEM((STREAMS, GROUP_Y - 1, 8, 128), wide),
            pltpu.VMEM((STREAMS, Z_COUNT, 8, 128), wide),
            pltpu.VMEM((STREAMS, GROUP_Y, 8, 128), half),
            pltpu.VMEM((Z_LOW, 16, 128), half),
            pltpu.VMEM((Z_LOW, 16, 128), half),
            pltpu.VMEM((GROUP_A, 16, 128), half),
            pltpu.VMEM((GROUP_A, 16, 128), half),
            dma((COPIES,)),
            dma((COPIES,)),
            dma((STREAMS,)),
            dma((len(arrays),)),
        ],
        compiler_params=pltpu.CompilerParams(
            collective_id=0, has_side_effects=True, vmem_limit_bytes=MAIN_VMEM
        ),
        name="main",
    )(*[pltpu.with_memory_space_constraint(x, pltpu.HBM) for x in arrays])


def finish_kernel(
    total, rows_in, proj_t, token_grad, grad_proj, grad_first, grad_second, grad_mask
):
    half = jnp.bfloat16
    row = lax.broadcasted_iota(jnp.int32, (192, 128), 0)
    column = lax.broadcasted_iota(jnp.int32, (192, 128), 1)
    tile = lax.div(row, 4)
    source = lax.rem(tile, 8) * 16 + lax.div(tile, 8) * 2 + lax.div(lax.rem(row, 4), 2)
    choose = jnp.where(column == source, 1.0, 0.0).astype(half)
    arrived = dot_nn(choose, rows_in[...].reshape(128, 128))
    arrived = jnp.where(lax.div(column, 64) == lax.rem(row, 2), arrived, 0.0).astype(half)
    double = jnp.concatenate([proj_t[...], proj_t[...]], axis=0)
    token_grad[...] = dot_nn(arrived, double).astype(half)
    packed = total[0].astype(jnp.float32).reshape(512, 128)
    grad_first[0:512] = packed[:, 0:64]
    grad_first[512:1024] = packed[:, 64:128]
    other = total[1].astype(jnp.float32).reshape(512, 128)
    for k in range(16):
        lanes = 64 * (k // 8)
        start = (k % 8) * 16
        grad_second[k // 4, :, k % 4, :] = other[start : start + 12, lanes : lanes + 64]
    for part in range(6):
        grad_proj[:, part * 128 : part * 128 + 128] = other[128 + part * 64 : 192 + part * 64]
    mask_row = other[12:13, 0:64] + other[13:14, 0:64]
    grad_mask[...] = jnp.dot(
        jnp.broadcast_to(mask_row, (8, 64)),
        proj_t[...].astype(jnp.float32),
        precision=lax.Precision.HIGHEST,
        preferred_element_type=jnp.float32,
    )[0:1].reshape(768)


def finish(total, rows_in, proj_t):
    vmem = pl.BlockSpec(memory_space=pltpu.VMEM)
    return pl.pallas_call(
        finish_kernel,
        out_shape=(
            jax.ShapeDtypeStruct((192, 768), jnp.bfloat16),
            jax.ShapeDtypeStruct((64, 768), jnp.float32),
            jax.ShapeDtypeStruct((1024, 64), jnp.float32),
            jax.ShapeDtypeStruct((4, 12, 4, 64), jnp.float32),
            jax.ShapeDtypeStruct((768,), jnp.float32),
        ),
        in_specs=[vmem] * 3,
        out_specs=(vmem,) * 5,
        compiler_params=pltpu.CompilerParams(vmem_limit_bytes=FINISH_VMEM),
        name="finish",
    )(total, rows_in, proj_t)


def per_device(
    tokens,
    vis_index,
    counts,
    owners,
    mask_token,
    proj_weight,
    up_first,
    up_second,
    saved_pre,
    cotangent,
):
    wide, narrow, fine, edge, place, cols, order = tap_select()
    proj_t = proj_weight.T
    total, rows_in = main(
        [
            cotangent,
            cols,
            saved_pre,
            edge,
            counts.reshape(2),
            vis_index.reshape(2, 64),
            owners.reshape(2, 1, 64),
            tokens.reshape(128, 768),
            mask_token,
            proj_t,
            up_first.reshape(1024, 64),
            up_second.transpose(0, 2, 1, 3),
            wide,
            narrow,
            fine,
            order,
            place,
        ],
    )
    token_grad, grad_proj, grad_first, grad_second, grad_mask = finish(total, rows_in, proj_t)
    return (
        token_grad[None, None],
        grad_proj.T,
        grad_first.reshape(4, 4, 64, 64),
        grad_second.transpose(0, 2, 1, 3),
        grad_mask,
    )


def solution(mesh):
    return jax.shard_map(
        per_device,
        mesh=mesh,
        in_specs=(
            P("ns", "ew", None, None, None),
            P("ns", "ew", None, None),
            P("ns", "ew", None),
            P("ns", "ew", None, None, None),
            P(),
            P(),
            P(),
            P(),
            P(None, None, "ns", "ew"),
            P(None, None, "ns", "ew"),
        ),
        out_specs=(P("ns", "ew", None, None), P(), P(), P(), P()),
        check_vma=False,
    )
```

```python
import jax
import jax.numpy as jnp
import numpy as np
from jax import lax
from jax.experimental import pallas as pl
from jax.experimental.pallas import tpu as pltpu
from jax.sharding import PartitionSpec as P

MESH = pl.DeviceIdType.MESH
GROUP_A = 8
GROUP_Y = 8
Z_LOW = 6
Z_HIGH = 2


BANDS_PAD = 16
LANES = 128


def tap_select():
    wide = np.zeros((256, 4, 256), np.float32)
    halo = np.zeros((2, 16, 4, 256), np.float32)
    for tap in range(4):
        for lane, cell in [(j, j) for j in range(128)] + [(128, 128), (255, -1)]:
            col = 2 * cell + tap - 1
            if col < 0:
                for frame in range(2):
                    halo[frame, 8 + frame * 3 + col + 3, tap, lane] = 1
            elif col < 256:
                wide[col, tap, lane] = 1
            else:
                for frame in range(2):
                    halo[frame, frame * 3 + col - 256, tap, lane] = 1
    fine = np.zeros((256, 4, 2, 64), np.float32)
    for tap in range(4):
        for cell in range(64):
            col = 2 * cell + tap - 1
            fine[col if col >= 0 else 255, tap, :, cell] = 1
    edge = np.zeros((8, 2, 16, 128), np.float32)
    place = np.zeros((2, 16, 2, 128), np.float32)
    for row in range(8):
        for line in [row] + ([8] if row == 7 else []) + ([9] if row == 0 else []):
            edge[row, 0, line, 0] = 1
            edge[row, 1, line, 127] = 1
    for frame in range(2):
        for spot in range(10):
            pair = 2 * (frame * 10 + spot)
            line = {0: 8, 9: 9}.get(spot, spot - 1)
            place[0, line, frame, pair] = 1
            place[1, line, frame, (pair - 1) % 128] = 1
    cols = np.zeros((2, 16, 256), np.float32)
    for frame in range(2):
        for k in range(3):
            cols[frame, frame * 3 + k, k] = 1
            cols[frame, 8 + frame * 3 + k, 253 + k] = 1
    order = np.zeros((4, 12, 4, 4, 4, 16), np.float32)
    for a in range(4):
        for o in range(12):
            for b in range(4):
                order[a, o, b, a, b, o] = 1
    half = jnp.bfloat16
    return (
        jnp.asarray(wide.reshape(256, 1024), half),
        jnp.asarray(halo.reshape(2, 16, 1024), half),
        jnp.asarray(fine.reshape(256, 512), half),
        jnp.asarray(edge.reshape(8, 32, 128), half),
        jnp.asarray(place.reshape(32, 256), half),
        jnp.asarray(cols, half),
        jnp.asarray(order.reshape(192, 256), half),
    )


def dot_nn(a, b):
    return jnp.dot(a, b, preferred_element_type=jnp.float32)


def dot_nt(a, b):
    return lax.dot_general(a, b, (((1,), (1,)), ((), ())), preferred_element_type=jnp.float32)


def dot_tn(a, b):
    return lax.dot_general(a, b, (((0,), (0,)), ((), ())), preferred_element_type=jnp.float32)


SIDES = ((-1, 0), (1, 0), (0, -1), (0, 1), (-1, -1), (-1, 1), (1, -1), (1, 1))
STREAMS = 2
Z_COUNT = Z_LOW * Z_HIGH


def fetch_all(pairs, sem, first):
    copies = []
    for k, (src, dst) in enumerate(pairs):
        copy = pltpu.make_async_copy(src, dst, sem.at[first + k])
        copy.start()
        copies.append(copy)
    return copies


def wait_all(copies):
    for copy in copies:
        copy.wait()


EARLY = 4
MAIN_VMEM = 24 * 1024 * 1024
FINISH_VMEM = 8 * 1024 * 1024
OPERANDS = tuple(range(17))


def main_kernel(*refs):
    sources = refs[: len(OPERANDS)]
    (total_out, rows_in) = refs[len(OPERANDS) : len(OPERANDS) + 2]
    held = refs[len(OPERANDS) + 2 : 2 * len(OPERANDS) + 2]
    (
        cot,
        cols,
        pre,
        edge,
        live_counts,
        index,
        owners,
        tokens,
        mask_token,
        proj_t,
        first,
        second,
        wide,
        narrow,
        fine,
        order,
        place,
    ) = held
    (
        wide_c,
        wide_p,
        cot_rows,
        packs,
        pre_rows,
        rows_c,
        rows_p,
        cols_c,
        corners,
        slopes,
        taps,
        windows,
        hidden,
        deltas,
        taps_fine,
        windows_fine,
        payload,
        buf_a,
        red_a,
        buf_b,
        buf_c,
        buf_d,
        rows_out,
        tok_z,
        tok_s,
        buf_s,
        send,
        recv,
        local_sem,
        fetch,
    ) = refs[2 * len(OPERANDS) + 2 :]
    half = jnp.bfloat16
    n = lax.axis_index("ns")
    e = lax.axis_index("ew")
    n_count = lax.axis_size("ns")
    e_count = lax.axis_size("ew")
    g = lax.rem(n, GROUP_A)
    zl = lax.div(n, GROUP_A)
    zh = lax.div(e, GROUP_Y)
    y = lax.rem(e, GROUP_Y)
    zi = zh * Z_LOW + zl

    def peer_side(side):
        return {
            "ew": lax.rem(e + side[1] + e_count, e_count),
            "ns": lax.rem(n + side[0] + n_count, n_count),
        }

    def peer_a(k):
        other = lax.rem(g + k, GROUP_A)
        return other, {"ew": e, "ns": zl * GROUP_A + other}

    def peer_b(k):
        other = lax.rem(y + k, GROUP_Y)
        return other, {"ew": zh * GROUP_Y + other, "ns": n}

    def peer_c(k):
        other = lax.rem(zi + k, Z_COUNT)
        return other, {
            "ew": lax.div(other, Z_LOW) * GROUP_Y + y,
            "ns": lax.rem(other, Z_LOW) * GROUP_A + g,
        }

    def peer_z(k):
        other = lax.rem(zl + k, Z_LOW)
        return other, {"ew": e, "ns": other * GROUP_A + g}

    pairs = tuple(zip(sources, held))
    early = fetch_all(pairs[:EARLY], fetch, 0)
    barrier = pltpu.get_barrier_semaphore()
    for k in (6, 5, 7, 4, 8, 3, 9, 2, 10, 1, 11):
        pl.semaphore_signal(barrier, inc=1, device_id=peer_c(k)[1], device_id_type=MESH)
    for side in reversed(SIDES):
        pl.semaphore_signal(barrier, inc=1, device_id=peer_side(side), device_id_type=MESH)
    for count, peer in ((GROUP_Y, peer_b), (GROUP_A, peer_a)):
        for k in range(1, count):
            pl.semaphore_signal(barrier, inc=1, device_id=peer(k)[1], device_id_type=MESH)

    later = fetch_all(pairs[EARLY:], fetch, EARLY)
    used = [0]
    sent = []

    def put(src, dst, target):
        slot = used[0]
        used[0] += 1
        copy = pltpu.make_async_remote_copy(
            src_ref=src,
            dst_ref=dst,
            send_sem=send.at[slot],
            recv_sem=recv.at[slot],
            device_id=target,
            device_id_type=MESH,
        )
        copy.start()
        sent.append(copy)
        return copy

    def wait_here(copies):
        for copy in copies:
            copy.wait_recv()

    wait_all(early)
    for f in range(2):
        for o in range(12):
            for part in range(2):
                wide_c[part, pl.ds((f * 16 + o) * 16, 16), :] = cot[
                    f, o, :, part * 128 : part * 128 + 128
                ].astype(jnp.float32)
        for part in range(2):
            wide_c[part, pl.ds((f * 16 + 12) * 16, 64), :] = jnp.zeros((64, 128), jnp.float32)
        for r in range(16):
            for part in range(2):
                cot_rows[f, r, :, part * 128 : part * 128 + 128] = wide_c[
                    part, pl.ds(f * 256 + r, 16, stride=16), :
                ].astype(half)
    for part in range(2):
        packed = jnp.zeros((16, 128), jnp.float32)
        for f in range(2):
            block = cot_rows[f, part * 8 : part * 8 + 8].reshape(128, 256)
            packed = packed + dot_nt(cols[f], block)
        for side in range(2):
            packs[side, 1 + 2 * part] = packed[side * 8 : side * 8 + 8].astype(half)
    for f in range(2):
        wide_p[pl.ds(f * 512, 512), :] = pre[f].reshape(512, 128).astype(jnp.float32)
    packed = jnp.zeros((32, 128), jnp.float32)
    for i in range(8):
        slabs = [wide_p[pl.ds(f * 512 + i, 64, stride=8), :].astype(half) for f in range(2)]
        for f in range(2):
            pre_rows[f, i] = slabs[f]
        packed = packed + dot_nt(edge[i], jnp.concatenate(slabs, axis=0))
    for side in range(2):
        packs[side, 2] = packed[side * 16 : side * 16 + 8].astype(half)
        corner = packed[side * 16 + 8 : side * 16 + 16].astype(half)
        packs[side, 0] = corner
        packs[side, 4] = corner

    pl.semaphore_wait(barrier, len(SIDES) + GROUP_A + GROUP_Y + Z_COUNT - 3)

    halo = []

    def edge_put(src, dst, side):
        slot = used[0]
        used[0] += 1
        copy = pltpu.make_async_remote_copy(
            src_ref=src,
            dst_ref=dst,
            send_sem=send.at[slot],
            recv_sem=recv.at[slot],
            device_id=peer_side(side),
            device_id_type=MESH,
        )
        halo.append((side, copy))

    edge_put(packs.at[0, 1:4], cols_c.at[1], (0, -1))
    edge_put(packs.at[1, 1:4], cols_c.at[0], (0, 1))
    edge_put(packs.at[0, 0:2], corners.at[3], (-1, -1))
    edge_put(packs.at[1, 0:2], corners.at[2], (-1, 1))
    edge_put(packs.at[0, 3:5], corners.at[1], (1, -1))
    edge_put(packs.at[1, 3:5], corners.at[0], (1, 1))
    edge_put(cot_rows.at[:, 0:3], rows_c.at[1], (-1, 0))
    edge_put(pre_rows.at[:, 0], rows_p.at[1], (-1, 0))
    edge_put(cot_rows.at[:, 13:16], rows_c.at[0], (1, 0))
    edge_put(pre_rows.at[:, 7], rows_p.at[0], (1, 0))

    north = n > 0
    south = n < n_count - 1
    west = e > 0
    east = e < e_count - 1

    def inside(side):
        by_row = {-1: north, 0: None, 1: south}[side[0]]
        by_column = {-1: west, 0: None, 1: east}[side[1]]
        if by_row is None:
            return by_column
        if by_column is None:
            return by_row
        return jnp.logical_and(by_row, by_column)

    for way in ((0, -1), (0, 1), (-1, -1), (-1, 1), (1, -1), (1, 1), (-1, 0), (1, 0)):

        @pl.when(inside(way))
        def _(way=way):
            for side, copy in halo:
                if side == way:
                    copy.start()

    wait_all(later)

    for f in range(2):
        for i in range(8):
            center = wide_p[pl.ds(f * 512 + i, 64, stride=8), :]
            sigmoid = jax.nn.sigmoid(1.702 * center)
            slopes[f, i] = sigmoid + 1.702 * center * sigmoid * (1.0 - sigmoid)
            hidden[:, (f * 8 + i) * 128 : (f * 8 + i + 1) * 128] = (center * sigmoid).astype(half)

    token_t = dot_nt(proj_t[...], tokens[...]).astype(half)
    mask_row = mask_token[...].astype(jnp.float32).reshape(1, 768)
    mask_t = dot_nt(proj_t[...], jnp.broadcast_to(mask_row, (8, 768)).astype(half)).astype(half)
    mask_column = mask_t[:, 0:1].astype(jnp.float32)
    patch = lax.broadcasted_iota(jnp.int32, (256, 64), 0)
    slot = lax.broadcasted_iota(jnp.int32, (256, 64), 1)
    picks = []
    unseen = []
    first_in = []
    for f in range(2):
        hit = (patch == index[f : f + 1, :]) & (slot < live_counts[f])
        pick = jnp.where(hit, 1.0, 0.0).astype(half)
        picks.append(pick)
        shown = dot_nt(jnp.ones((8, 64), half), pick)
        unseen.append(1.0 - shown)
        placed = dot_nt(token_t[:, f * 64 : f * 64 + 64], pick)
        placed = placed + mask_column * unseen[f][0:1, :]
        first_in.append(placed.astype(half))
    first_grid = jnp.concatenate(first_in, axis=1)
    unseen = jnp.concatenate(unseen, axis=1)
    second_t = dot_tn(
        second[...].astype(jnp.float32).reshape(192, 64).astype(half), order[...]
    ).astype(half)

    row_second = lax.broadcasted_iota(jnp.int32, (128, 128), 0)
    lane_second = lax.broadcasted_iota(jnp.int32, (128, 128), 1)
    owner_row = jnp.concatenate([owners[0], owners[1]], axis=1)
    lane_row = lax.broadcasted_iota(jnp.int32, (1, 128), 1)
    live_row = lane_row < jnp.where(lane_row < 64, live_counts[0], live_counts[1] + 64)
    marked = jnp.where(live_row, owner_row, -1).astype(jnp.float32)
    across = jnp.broadcast_to(marked, (128, 128))
    down = across.T
    earlier = (across == down) & (row_second < lane_second)
    rank = jnp.sum(jnp.where(earlier, 1.0, 0.0), axis=0, keepdims=True)
    target = jnp.where(live_row, marked * 4.0 + rank, -1.0)
    number = lax.broadcasted_iota(jnp.int32, (96, 128), 0).astype(jnp.float32) * 2.0
    even = jnp.where(number == target, 1.0, 0.0).astype(half)
    odd = jnp.where(number + 1.0 == target, 1.0, 0.0).astype(half)

    def wait_sides(ways):
        for way in ways:

            @pl.when(inside((-way[0], -way[1])))
            def _(way=way):
                for side, copy in halo:
                    if side == way:
                        copy.wait_recv()

    wait_sides(SIDES[:2])

    def only(condition, value):
        chosen_lanes = jnp.full(value.shape, jnp.where(condition, 1.0, 0.0), jnp.float32) > 0.5
        return jnp.where(chosen_lanes, value.astype(jnp.float32), 0.0)

    def side_cols(west_block, east_block):
        return jnp.concatenate([only(east, east_block), only(west, west_block)], axis=0).astype(half)

    wide_map = wide[...]
    for f in range(2):
        for part in range(2):
            value = dot_nn(cot_rows[f, part * 8 : part * 8 + 8].reshape(128, 256), wide_map)
            taps[f, 3 + part * 8 : 11 + part * 8] = value.astype(half).reshape(8, 16, 1024)
        value = only(north, dot_nn(rows_c[0, f].reshape(48, 256), wide_map))
        taps[f, 0:3] = value.astype(half).reshape(3, 16, 1024)
        value = only(south, dot_nn(rows_c[1, f].reshape(48, 256), wide_map))
        taps[f, 19:22] = value.astype(half).reshape(3, 16, 1024)

    wait_sides(SIDES[2:])

    blocks = [(3, 11, 0, None, side_cols(cols_c[0, 0], cols_c[1, 0]))]
    blocks.append((11, 19, 0, None, side_cols(cols_c[0, 2], cols_c[1, 2])))
    blocks.append((0, 3, 80, north, side_cols(corners[0, 0], corners[1, 0])))
    blocks.append((19, 22, 0, south, side_cols(corners[2, 1], corners[3, 1])))
    for f in range(2):
        for low, high, start, condition, side in blocks:
            count = high - low
            for first_lane, last_lane in ((0, 256), (384, 512), (640, 1024)):
                width = last_lane - first_lane
                value = dot_tn(side, narrow[f, :, first_lane:last_lane])
                value = value[start : start + count * 16]
                if condition is not None:
                    value = only(condition, value)
                held_taps = taps[f, low:high, :, first_lane:last_lane].astype(jnp.float32)
                value = held_taps + value.reshape(count, 16, width)
                taps[f, low:high, :, first_lane:last_lane] = value.astype(half)

    lane = lax.broadcasted_iota(jnp.int32, (64, 128), 1)
    line = lax.broadcasted_iota(jnp.int32, (8, 128), 0)

    def side_rows(condition, upper, middle, lower):
        corner = jnp.where(line == 0, only(north, upper), 0.0)
        corner = jnp.where(line == 1, only(south, lower), corner)
        return [only(condition, middle), only(condition, corner)]

    side = jnp.concatenate(
        side_rows(east, corners[1, 1], cols_c[1, 1], corners[3, 0])
        + side_rows(west, corners[0, 1], cols_c[0, 1], corners[2, 0]),
        axis=0,
    ).astype(half)
    placed = dot_tn(side, place[...])
    halo_pre = placed[0:64, 0:128] + placed[64:128, 128:256]
    halo_keep = jnp.where(
        lane == 0, jnp.where(east, 1.0, 0.0), jnp.where(lane == 127, jnp.where(west, 1.0, 0.0), 0.0)
    )
    sigmoid = jax.nn.sigmoid(1.702 * halo_pre)
    halo_slope = sigmoid + 1.702 * halo_pre * sigmoid * (1.0 - sigmoid)

    for f in range(2):
        for i in range(10):
            window = jnp.concatenate(
                [
                    taps[f, 2 * i + a, :, b * 256 : b * 256 + 256]
                    for a in range(4)
                    for b in range(4)
                ],
                axis=0,
            )
            grad = dot_nn(second_t, window)
            if 0 < i < 9:
                windows[:, (f * 8 + i - 1) * 128 : (f * 8 + i) * 128] = window[:, :128]
                slope = slopes[f, i - 1]
            else:
                center = rows_p[i // 9, f].astype(jnp.float32)
                sigmoid = jax.nn.sigmoid(1.702 * center)
                slope = sigmoid + 1.702 * center * sigmoid * (1.0 - sigmoid)
            value = grad[:, :128] * slope
            edge_slope = halo_slope
            if f + i > 0:
                edge_slope = pltpu.roll(halo_slope, 128 - 2 * (f * 10 + i), 1)
            edge_value = grad[:, 128:] * edge_slope * halo_keep
            if i == 0:
                value = only(north, value)
                edge_value = only(north, edge_value)
            if i == 9:
                value = only(south, value)
                edge_value = only(south, edge_value)
            deltas[f, i, :, 0:128] = value.astype(half)
            deltas[f, i, :, 128:256] = edge_value.astype(half)

    fine_map = fine[...]
    for f in range(2):
        for i in range(10):
            taps_fine[f, i] = dot_nn(deltas[f, i], fine_map).astype(half)
    low_lane = lane < 64
    for f in range(2):
        for pair in range(2):
            for a in range(4):
                for b in range(4):
                    low = taps_fine[f, 4 * pair + a, :, b * 128 : b * 128 + 128]
                    high = taps_fine[f, 4 * pair + 2 + a, :, b * 128 : b * 128 + 128]
                    windows_fine[
                        (a * 4 + b) * 64 : (a * 4 + b) * 64 + 64,
                        (f * 2 + pair) * 128 : (f * 2 + pair) * 128 + 128,
                    ] = jnp.where(low_lane, low, high)

    zeros_fine = jnp.zeros((64, 512), half)
    grad_first = dot_nt(windows_fine[0:512], jnp.concatenate([first_grid, zeros_fine], axis=0))
    grad_first = grad_first + dot_nt(
        windows_fine[512:1024], jnp.concatenate([zeros_fine, first_grid], axis=0)
    )
    payload[0] = grad_first.astype(half).reshape(GROUP_A, GROUP_Y, 8, 128)

    def scatter_a(s):
        copies = []
        for k in range(1, GROUP_A):
            other, target_device = peer_a(k)
            copies.append(put(payload.at[s, other], buf_a.at[s, k - 1], target_device))
        return copies

    copies_a = [scatter_a(0)]

    grid = dot_tn(first[...], windows_fine[...]).astype(half)
    chosen = jnp.concatenate(
        [dot_nn(grid[:, f * 256 : f * 256 + 256], picks[f]) for f in range(2)], axis=1
    ).astype(half)
    zeros_slot = jnp.zeros((64, 128), half)
    outgoing = dot_nt(even, jnp.concatenate([chosen, zeros_slot], axis=0))
    outgoing = outgoing + dot_nt(odd, jnp.concatenate([zeros_slot, chosen], axis=0))
    rows_out[...] = outgoing.astype(half).reshape(Z_LOW, 16, 128)
    copies_z = []
    for k in range(1, Z_LOW):
        other, target_device = peer_z(k)
        copies_z.append(put(rows_out.at[other], tok_z.at[zl], target_device))
    tok_z[zl] = rows_out[zl]

    zeros_64 = jnp.zeros((64, 2048), half)
    hidden_value = hidden[...]
    grad_second = dot_nt(windows[0:128, :], jnp.concatenate([hidden_value, zeros_64], axis=0))
    grad_second = grad_second + dot_nt(
        windows[128:256, :], jnp.concatenate([zeros_64, hidden_value], axis=0)
    )
    mask_sum = jnp.sum(grid.astype(jnp.float32) * unseen[0:1, :], axis=1, keepdims=True)
    mask_sum_row = dot_nt(unseen.astype(half), jnp.concatenate([grid, zeros_fine], axis=0))
    grad_proj = dot_nn(chosen, tokens[...]) + mask_sum * mask_row
    mask_sum_row = mask_sum_row[0:1, :]
    mask_rest = mask_sum_row - mask_sum_row.astype(half).astype(jnp.float32)
    grad_second = jnp.where(
        (row_second == 12) & (lane_second < 64),
        mask_sum_row,
        jnp.where((row_second == 13) & (lane_second < 64), mask_rest, grad_second),
    )
    payload[1, 0:2] = grad_second.astype(half).reshape(2, GROUP_Y, 8, 128)
    for part in range(6):
        block = grad_proj[:, part * 128 : part * 128 + 128].astype(half)
        payload[1, 2 + part] = block.reshape(GROUP_Y, 8, 128)
    copies_a.append(scatter_a(1))

    copies_b = []
    for s in range(STREAMS):
        wait_here(copies_a[s])
        summed = payload[s, g].astype(jnp.float32)
        for k in range(1, GROUP_A):
            summed = summed + buf_a[s, k - 1].astype(jnp.float32)
        red_a[s] = summed
        copies = []
        for k in range(1, GROUP_Y):
            other, target_device = peer_b(k)
            copies.append(put(red_a.at[s, other], buf_b.at[s, k - 1], target_device))
        copies_b.append(copies)

    wait_here(copies_z)
    stacked = tok_z[...].reshape(Z_LOW * 16, 128)
    picked = lax.broadcasted_iota(jnp.int32, (GROUP_A * 16, Z_LOW * 16), 0)
    column = lax.broadcasted_iota(jnp.int32, (GROUP_A * 16, Z_LOW * 16), 1)
    wanted = ((picked % 16) // 2) * 16 + (picked // 16) * 2 + picked % 2
    choose = jnp.where(column == wanted, 1.0, 0.0).astype(half)
    tok_s[...] = dot_nn(choose, stacked).astype(half).reshape(GROUP_A, 16, 128)
    copies_t = []
    for k in range(1, GROUP_A):
        other, target_device = peer_a(k)
        copies_t.append(put(tok_s.at[other], buf_s.at[g], target_device))
    buf_s[g] = tok_s[g]

    copies_c = []
    for s in range(STREAMS):
        wait_here(copies_b[s])
        summed = red_a[s, y]
        for k in range(1, GROUP_Y):
            summed = summed + buf_b[s, k - 1]
        buf_c[s, zi] = summed
        copies = []
        for k in range(1, Z_COUNT):
            copies.append(put(buf_c.at[s, zi], buf_c.at[s, zi], peer_c(k)[1]))
        copies_c.append(copies)

    row_8 = lax.broadcasted_iota(jnp.int32, (8, 128), 0)
    copies_d = []
    for s in range(STREAMS):
        wait_here(copies_c[s])
        summed = buf_c[s, 0]
        for k in range(1, Z_COUNT):
            summed = summed + buf_c[s, k]
        if s == 1:
            mask_total = summed[4:5] + summed[5:6]
            rest = mask_total - mask_total.astype(half).astype(jnp.float32)
            here = jnp.where((g == 0) & (y == 1), 4, -2)
            summed = jnp.where(row_8 == here, mask_total, summed)
            summed = jnp.where(row_8 == here + 1, rest, summed)
        buf_d[s, y] = summed.astype(half)
        copies = []
        for k in range(1, GROUP_Y):
            copies.append(put(buf_d.at[s, y], buf_d.at[s, y], peer_b(k)[1]))
        copies_d.append(copies)

    copies_e = []
    own = []
    for s in range(STREAMS):
        wait_here(copies_d[s])
        for k in range(1, GROUP_A):
            copies_e.append(put(buf_d.at[s], total_out.at[s, g], peer_a(k)[1]))
        copy = pltpu.make_async_copy(buf_d.at[s], total_out.at[s, g], local_sem.at[s])
        copy.start()
        own.append(copy)
    wait_here(copies_t)
    rows_in[...] = buf_s[...]
    wait_here(copies_e)
    wait_all(own)
    for copy in sent:
        copy.wait_send()
    for way in SIDES:

        @pl.when(inside(way))
        def _(way=way):
            for side, copy in halo:
                if side == way:
                    copy.wait_send()


COPIES = 10 + 2 * (2 * (GROUP_A - 1) + 2 * (GROUP_Y - 1) + Z_COUNT - 1) + Z_LOW - 1 + GROUP_A - 1


def main(arrays):
    vmem = pl.BlockSpec(memory_space=pltpu.VMEM)
    hbm = pl.BlockSpec(memory_space=pl.ANY)
    half = jnp.bfloat16
    wide = jnp.float32
    dma = pltpu.SemaphoreType.DMA
    return pl.pallas_call(
        main_kernel,
        out_shape=(
            jax.ShapeDtypeStruct((STREAMS, GROUP_A, GROUP_Y, 8, 128), half),
            jax.ShapeDtypeStruct((GROUP_A, 16, 128), half),
        ),
        in_specs=[pl.BlockSpec(memory_space=pltpu.HBM)] * len(arrays),
        out_specs=(hbm, vmem),
        scratch_shapes=[
            (pltpu.SMEM if x.ndim == 1 and x.dtype == jnp.int32 else pltpu.VMEM)(x.shape, x.dtype)
            for x in arrays
        ]
        + [
            pltpu.VMEM((2, 512, 128), wide),
            pltpu.VMEM((1024, 128), wide),
            pltpu.VMEM((2, 16, 16, 256), half),
            pltpu.VMEM((2, 5, 8, 128), half),
            pltpu.VMEM((2, 8, 64, 128), half),
            pltpu.VMEM((2, 2, 3, 16, 256), half),
            pltpu.VMEM((2, 2, 64, 128), half),
            pltpu.VMEM((2, 3, 8, 128), half),
            pltpu.VMEM((4, 2, 8, 128), half),
            pltpu.VMEM((2, 8, 64, 128), wide),
            pltpu.VMEM((2, 22, 16, 1024), half),
            pltpu.VMEM((256, 2048), half),
            pltpu.VMEM((64, 2048), half),
            pltpu.VMEM((2, 10, 64, 256), half),
            pltpu.VMEM((2, 10, 64, 512), half),
            pltpu.VMEM((1024, 512), half),
            pltpu.VMEM((STREAMS, GROUP_A, GROUP_Y, 8, 128), half),
            pltpu.VMEM((STREAMS, GROUP_A - 1, GROUP_Y, 8, 128), half),
            pltpu.VMEM((STREAMS, GROUP_Y, 8, 128), wide),
            pltpu.VMEM((STREAMS, GROUP_Y - 1, 8, 128), wide),
            pltpu.VMEM((STREAMS, Z_COUNT, 8, 128), wide),
            pltpu.VMEM((STREAMS, GROUP_Y, 8, 128), half),
            pltpu.VMEM((Z_LOW, 16, 128), half),
            pltpu.VMEM((Z_LOW, 16, 128), half),
            pltpu.VMEM((GROUP_A, 16, 128), half),
            pltpu.VMEM((GROUP_A, 16, 128), half),
            dma((COPIES,)),
            dma((COPIES,)),
            dma((STREAMS,)),
            dma((len(arrays),)),
        ],
        compiler_params=pltpu.CompilerParams(
            collective_id=0, has_side_effects=True, vmem_limit_bytes=MAIN_VMEM
        ),
        name="main",
    )(*[pltpu.with_memory_space_constraint(x, pltpu.HBM) for x in arrays])


def finish_kernel(
    total, rows_in, proj_t, token_grad, grad_proj, grad_first, grad_second, grad_mask
):
    half = jnp.bfloat16
    row = lax.broadcasted_iota(jnp.int32, (192, 128), 0)
    column = lax.broadcasted_iota(jnp.int32, (192, 128), 1)
    tile = lax.div(row, 4)
    source = lax.rem(tile, 8) * 16 + lax.div(tile, 8) * 2 + lax.div(lax.rem(row, 4), 2)
    choose = jnp.where(column == source, 1.0, 0.0).astype(half)
    arrived = dot_nn(choose, rows_in[...].reshape(128, 128))
    arrived = jnp.where(lax.div(column, 64) == lax.rem(row, 2), arrived, 0.0).astype(half)
    double = jnp.concatenate([proj_t[...], proj_t[...]], axis=0)
    token_grad[...] = dot_nn(arrived, double).astype(half)
    packed = total[0].astype(jnp.float32).reshape(512, 128)
    grad_first[0:512] = packed[:, 0:64]
    grad_first[512:1024] = packed[:, 64:128]
    other = total[1].astype(jnp.float32).reshape(512, 128)
    for k in range(16):
        lanes = 64 * (k // 8)
        start = (k % 8) * 16
        grad_second[k // 4, :, k % 4, :] = other[start : start + 12, lanes : lanes + 64]
    for part in range(6):
        grad_proj[:, part * 128 : part * 128 + 128] = other[128 + part * 64 : 192 + part * 64]
    mask_row = other[12:13, 0:64] + other[13:14, 0:64]
    grad_mask[...] = jnp.dot(
        jnp.broadcast_to(mask_row, (8, 64)),
        proj_t[...].astype(jnp.float32),
        precision=lax.Precision.HIGHEST,
        preferred_element_type=jnp.float32,
    )[0:1].reshape(768)


def finish(total, rows_in, proj_t):
    vmem = pl.BlockSpec(memory_space=pltpu.VMEM)
    return pl.pallas_call(
        finish_kernel,
        out_shape=(
            jax.ShapeDtypeStruct((192, 768), jnp.bfloat16),
            jax.ShapeDtypeStruct((64, 768), jnp.float32),
            jax.ShapeDtypeStruct((1024, 64), jnp.float32),
            jax.ShapeDtypeStruct((4, 12, 4, 64), jnp.float32),
            jax.ShapeDtypeStruct((768,), jnp.float32),
        ),
        in_specs=[vmem] * 3,
        out_specs=(vmem,) * 5,
        compiler_params=pltpu.CompilerParams(vmem_limit_bytes=FINISH_VMEM),
        name="finish",
    )(total, rows_in, proj_t)


def per_device(
    tokens,
    vis_index,
    counts,
    owners,
    mask_token,
    proj_weight,
    up_first,
    up_second,
    saved_pre,
    cotangent,
):
    wide, narrow, fine, edge, place, cols, order = tap_select()
    proj_t = proj_weight.T
    total, rows_in = main(
        [
            cotangent,
            cols,
            saved_pre,
            edge,
            counts.reshape(2),
            vis_index.reshape(2, 64),
            owners.reshape(2, 1, 64),
            tokens.reshape(128, 768),
            mask_token,
            proj_t,
            up_first.reshape(1024, 64),
            up_second.transpose(0, 2, 1, 3),
            wide,
            narrow,
            fine,
            order,
            place,
        ],
    )
    token_grad, grad_proj, grad_first, grad_second, grad_mask = finish(total, rows_in, proj_t)
    return (
        token_grad[None, None],
        grad_proj.T,
        grad_first.reshape(4, 4, 64, 64),
        grad_second.transpose(0, 2, 1, 3),
        grad_mask,
    )


def solution(mesh):
    return jax.shard_map(
        per_device,
        mesh=mesh,
        in_specs=(
            P("ns", "ew", None, None, None),
            P("ns", "ew", None, None),
            P("ns", "ew", None),
            P("ns", "ew", None, None, None),
            P(),
            P(),
            P(),
            P(),
            P(None, None, "ns", "ew"),
            P(None, None, "ns", "ew"),
        ),
        out_specs=(P("ns", "ew", None, None), P(), P(), P(), P()),
        check_vma=False,
    )
```
